32 devices in a mesh: ta: 4 (over y, x), gx: 2 (over core), gy: 4 (over z).
Axes of the slice: x: 2, y: 2, z: 4, core: 2. Of those that a mesh axis runs over, the one named last changes fastest.
Arguments:
- velocity: float32 [3, 4, 32, 64, 256], P(None, 'ta', 'gx', 'gy'), may hold values from -6 to 6
- pressure: float32 [4, 32, 64, 256], P('ta', 'gx', 'gy'), may hold values from -6 to 6
- forcing: float32 [3, 4, 32, 64, 256], P(None, 'ta', 'gx', 'gy'), may hold values from -6 to 6
- source: float32 [4, 32, 64, 256], P('ta', 'gx', 'gy'), may hold values from -6 to 6
- viscosity: float32 [3, 32, 64, 256], P(None, 'gx', 'gy'), may hold values from 0.05 to 0.5
Outputs:
- new_velocity: float32 [3, 4, 32, 64, 256], P(None, 'ta', 'gx', 'gy')
- new_pressure: float32 [4, 32, 64, 256], P('ta', 'gx', 'gy')
The draws below stay inside these ranges and needn't reach their ends.
All inputs are finite; a program needn't handle non-finite values.
Results may differ from the reference program's by a relative error of at most 0.00002.
Values sent between devices are 32-bit elements; how exact they have to be, the bound alone decides.
A program may use at most 64 MiB of HBM per device.

```python
import math
import jax
import jax.numpy as jnp

CZ = 256
SWEEPS = 2
NT = 4
NX = 32
NY = 64


def levels(stream_key, dims, shards, least, largest):
    gain, own = 1.0, jax.random.fold_in(stream_key, 6)
    for position, parts in shards:
        draws = jnp.exp(jax.random.uniform(jax.random.fold_in(own, position), (parts,), jnp.float32, least / len(shards), largest / len(shards)))
        gain = gain * jnp.repeat(draws, dims[position] // parts).reshape([-1 if axis == position else 1 for axis in range(len(dims))])
    return gain


def bell_draw(own_key, dims, spread, most, split=(), held_as=jnp.bfloat16):
    result = spread * jax.random.normal(own_key, dims, jnp.float32)
    if split:
        result = result * levels(own_key, dims, split, -0.22, 0.18)
    return jnp.clip(result, -most, most).astype(held_as)


def setup_inputs(seed: int = 0) -> dict:
    seeds = jax.random.split(jax.random.key(seed), 6)
    velocity = bell_draw(seeds[0], (3, NT, NX, NY, CZ), 1.0, 6.0, ((1, 4), (2, 2), (3, 4)), jnp.float32)
    pressure = bell_draw(seeds[1], (NT, NX, NY, CZ), 1.0, 6.0, ((0, 4), (1, 2), (2, 4)), jnp.float32)
    forcing = bell_draw(seeds[2], (3, NT, NX, NY, CZ), 1.0, 6.0, ((1, 4), (2, 2), (3, 4)), jnp.float32)
    source = bell_draw(seeds[3], (NT, NX, NY, CZ), 1.0, 6.0, ((0, 4), (1, 2), (2, 4)), jnp.float32)
    viscosity = jnp.clip(jnp.exp(math.log(0.5) - 2.3025851 * jax.random.uniform(seeds[4], (3, NX, NY, CZ), jnp.float32) ** levels(seeds[4], (3, NX, NY, CZ), ((1, 2), (2, 4)), -0.2, 0.2)), 0.05, 0.5)
    return {"velocity": velocity, "pressure": pressure, "forcing": forcing, "source": source, "viscosity": viscosity}


inverse_step = 1.0
relax_factor = 1.5
damping = 0.8


def gradient(field):
    return jnp.stack([jnp.roll(field, -1, -3) - field, jnp.roll(field, -1, -2) - field, jnp.roll(field, -1, -1) - field])


def divergence(flux):
    return (flux[0] - jnp.roll(flux[0], 1, -3)) + (flux[1] - jnp.roll(flux[1], 1, -2)) + (flux[2] - jnp.roll(flux[2], 1, -1))


def neighbours(field):
    total = jnp.roll(field, 1, -3) + jnp.roll(field, -1, -3)
    total = total + jnp.roll(field, 1, -2) + jnp.roll(field, -1, -2)
    return total + jnp.roll(field, 1, -1) + jnp.roll(field, -1, -1)


def diagonal_sum(coeff):
    return coeff[0] + jnp.roll(coeff[0], 1, -3) + coeff[1] + jnp.roll(coeff[1], 1, -2) + coeff[2] + jnp.roll(coeff[2], 1, -1)


def reference(velocity, pressure, forcing, source, viscosity):
    previous = jnp.concatenate([jnp.zeros_like(velocity[:, :1]), velocity[:, :-1]], axis=1)
    driven = forcing + inverse_step * previous
    visc = viscosity[:, None]
    momentum = driven - (inverse_step * velocity + visc * (6.0 * velocity - neighbours(velocity))) - gradient(pressure)
    coeff = 1.0 / (relax_factor * (inverse_step + 6.0 * visc))
    total = diagonal_sum(coeff)
    right = divergence(coeff * momentum) - (source - divergence(velocity))
    change = -damping * right / total
    for sweep in range(SWEEPS - 1):
        change = change - damping * (right - divergence(coeff * gradient(change))) / total
    new_velocity = velocity + coeff * (momentum - gradient(change))
    return new_velocity, pressure + change
```

```python
import functools

import jax
import jax.numpy as jnp
from jax import lax
from jax.experimental import pallas as pl
from jax.experimental.pallas import tpu as pltpu
from jax.sharding import PartitionSpec as P

relax_factor = 1.5
damping = 0.8
MESH = pl.DeviceIdType.MESH


def loop(lo, hi, body):
    def step(i, carry):
        body(i)
        return carry

    if hi > lo:
        lax.fori_loop(lo, hi, step, 0, unroll=hi - lo)


def row_index(f):
    return lax.broadcasted_iota(jnp.int32, f.shape, 0)


def y_next(f, row):
    n = f.shape[0]
    return jnp.where(row_index(f) == n - 1, row, pltpu.roll(f, n - 1, 0))


def y_last(f, row):
    return jnp.where(row_index(f) == 0, row, pltpu.roll(f, 1, 0))


def z_next(f):
    return pltpu.roll(f, f.shape[1] - 1, 1)


def z_last(f):
    return pltpu.roll(f, 1, 1)


def groups_of(lo, hi, size):
    return [(a, min(a + size, hi)) for a in range(lo, hi, size)]


def kernel(
    slabs, nx_parts, ny_parts, groups,
    vel, prs, frc, src, vis, out_v, out_p,
    V, Pr, F, S, Nu, C, W, SC, c1, c2, OV, OP,
    sE, rE, sI, rI, yu_s, yd_s, yu_r, yd_r, Ch, f_s, Fh,
    c1d_s, c1u_s, c1d_r, c1u_r, c2x_s, c2y_s, c2y_r,
    load_sem, out_sem, send_sem, recv_sem,
):
    _, nx, ny, nz = vel.shape
    parts = (ny - 4) // 4
    ta, gx, gy = lax.axis_index("ta"), lax.axis_index("gx"), lax.axis_index("gy")
    t_next, t_prev = lax.rem(ta + 1, slabs), lax.rem(ta + slabs - 1, slabs)
    has_next, has_prev = ta < slabs - 1, ta > 0
    xu, xd = lax.rem(gx + 1, nx_parts), lax.rem(gx + nx_parts - 1, nx_parts)
    yu, yd = lax.rem(gy + 1, ny_parts), lax.rem(gy + ny_parts - 1, ny_parts)

    loads = [
        pltpu.make_async_copy(vel, V.at[:, pl.ds(1, nx)], load_sem.at[0]),
        pltpu.make_async_copy(vis, Nu.at[:, pl.ds(1, nx)], load_sem.at[1]),
        pltpu.make_async_copy(prs, Pr.at[pl.ds(0, nx)], load_sem.at[2]),
        pltpu.make_async_copy(frc, F, load_sem.at[3]),
        pltpu.make_async_copy(src, S, load_sem.at[4]),
    ]
    for copy in loads:
        copy.start()

    barrier = pltpu.get_barrier_semaphore()

    def greet(axis, index):
        pl.semaphore_signal(barrier, inc=1, device_id={axis: index}, device_id_type=MESH)

    first_row = gy == 0
    greet("gx", xu)
    greet("gx", xd)

    @pl.when(has_prev)
    def _():
        greet("ta", t_prev)

    for beside in (yu, yd):

        @pl.when(jnp.logical_not(first_row) & (beside != 0))
        def _():
            greet("gy", beside)

    def remote(k, source, target, axis, index):
        return pltpu.make_async_remote_copy(
            src_ref=source, dst_ref=target, send_sem=send_sem.at[k], recv_sem=recv_sem.at[k],
            device_id={axis: index}, device_id_type=MESH,
        )

    vx_up = remote(0, V.at[:, nx], V.at[:, 0], "gx", xu)
    vx_dn = remote(1, V.at[:, 1], V.at[:, nx + 1], "gx", xd)
    px_dn = remote(2, Pr.at[0], Pr.at[nx], "gx", xd)
    nx_up = remote(3, Nu.at[0, nx], Nu.at[0, 0], "gx", xu)
    ry_up = remote(4, yu_s, yu_r, "gy", yu)
    ry_dn = remote(5, yd_s, yd_r, "gy", yd)
    fx_up = remote(6, W.at[0, nx], W.at[0, 0], "gx", xu)
    fy_up = remote(7, f_s, Fh, "gy", yu)
    cx_dn = remote(8, c1.at[1], c1.at[nx + 1], "gx", xd)
    cx_up = remote(9, c1.at[nx], c1.at[0], "gx", xu)
    cy_dn = remote(10, c1d_s, c1d_r, "gy", yd)
    cy_up = remote(11, c1u_s, c1u_r, "gy", yu)
    ex_dn = remote(12, c2x_s, c2.at[nx], "gx", xd)
    ey_dn = remote(13, c2y_s, c2y_r, "gy", yd)
    edge = remote(14, sE, rE, "ta", t_next)
    pieces = [
        remote(15 + k, sI.at[pl.ds(a, b - a)], rI.at[pl.ds(a, b - a)], "ta", t_next)
        for k, (a, b) in enumerate(groups)
    ]

    def pack_edges(x):
        for c in range(3):
            sE[c, x, 0:2] = V[c, x + 1, 0:2]
            sE[c, x, 2:4] = V[c, x + 1, ny - 2 : ny]

    def pack_rows(x):
        for c in range(3):
            yu_s[c, x] = V[c, x + 1, ny - 1 : ny]
            yd_s[c, x] = V[c, x + 1, 0:1]
        yu_s[3, x] = Nu[1, x + 1, ny - 1 : ny]
        yd_s[3, x] = Pr[x, 0:1]

    def pack_inner(x):
        for c in range(3):
            for p in range(parts):
                sI[x, p, c] = V[c, x + 1, 2 + 4 * p : 6 + 4 * p]

    loads[0].wait()
    loop(0, nx, pack_edges)
    pl.semaphore_wait(barrier, 2 + has_next.astype(jnp.int32) + jnp.where(first_row, 0, 2))
    for beside in (yu, yd):

        @pl.when(first_row | (beside == 0))
        def _():
            greet("gy", beside)

    @pl.when(has_next)
    def _():
        edge.start()

    loads[1].wait()
    loads[2].wait()
    loop(0, nx, pack_rows)
    for copy in (vx_up, vx_dn, px_dn, nx_up):
        copy.start()

    @pl.when(jnp.logical_not(first_row))
    def _():
        ry_up.start()
        ry_dn.start()

    loop(0, nx, pack_inner)

    @pl.when(has_next)
    def _():
        for copy in pieces:
            copy.start()

    @pl.when(first_row)
    def _():
        pl.semaphore_wait(barrier, 2)
        ry_up.start()
        ry_dn.start()

    def coeff_of(nu):
        return 1.0 / (relax_factor * (1.0 + 6.0 * nu))

    loads[3].wait()
    loads[4].wait()
    for copy in (vx_up, vx_dn, px_dn, nx_up, ry_up, ry_dn):
        copy.wait_recv()
    C[0, 0] = coeff_of(Nu[0, 0])

    def prepare(x):
        e = x + 1
        below = coeff_of(yu_r[3, x])
        Ch[x] = below
        coeff = [coeff_of(Nu[c, e]) for c in range(3)]
        for c in range(3):
            C[c, e] = coeff[c]
        total = coeff[0] + C[0, x] + coeff[1] + y_last(coeff[1], below) + coeff[2] + z_last(coeff[2])
        SC[x] = damping / total
        press = Pr[x]
        grads = (Pr[x + 1] - press, y_next(press, yd_r[3, x]) - press, z_next(press) - press)
        for c in range(3):
            v = V[c, e]
            near = V[c, e - 1] + V[c, e + 1] + y_last(v, yu_r[c, x]) + y_next(v, yd_r[c, x])
            near = near + z_last(v) + z_next(v)
            momentum = F[c, x] - (v + Nu[c, e] * (6.0 * v - near)) - grads[c]
            W[c, e] = v + coeff[c] * momentum

    loop(0, nx, prepare)

    def add_edges(x):
        for c in range(3):
            for s, t in ((0, 0), (2, ny - 2)):
                W[c, x + 1, t : t + 2] = (
                    W[c, x + 1, t : t + 2] + C[c, x + 1, t : t + 2] * rE[c, x, s : s + 2]
                )

    def add_inner(x):
        for c in range(3):
            for p in range(parts):
                t = 2 + 4 * p
                W[c, x + 1, t : t + 4] = W[c, x + 1, t : t + 4] + C[c, x + 1, t : t + 4] * rI[x, p, c]

    def arrive(k):
        @pl.when(has_prev)
        def _():
            pieces[k].wait_recv()
            loop(*groups[k], add_inner)

    @pl.when(has_prev)
    def _():
        edge.wait_recv()
        loop(0, nx, add_edges)

    def pack_flux(x):
        f_s[x] = W[1, x + 1, ny - 1 : ny]

    loop(0, nx, pack_flux)
    fy_up.start()
    arrive(0)
    arrive(1)
    fx_up.start()
    fy_up.wait_recv()

    fx_up.wait_recv()

    def sweep_one(x):
        e = x + 1
        w1, w2 = W[1, e], W[2, e]
        div = (W[0, e] - W[0, x]) + (w1 - y_last(w1, Fh[x])) + (w2 - z_last(w2))
        return SC[x] * (S[x] - div)

    def first_edges(x):
        change = sweep_one(x)
        c1[x + 1] = change
        c1d_s[x] = change[0:1]
        c1u_s[x] = change[ny - 1 : ny]

    loop(0, nx, first_edges)
    for copy in (cy_dn, cy_up, cx_dn, cx_up):
        copy.start()
    for copy in (cx_dn, cx_up, cy_dn, cy_up):
        copy.wait_recv()

    def sweep_two(x):
        e = x + 1
        here = c1[e]
        w0 = W[0, e] - C[0, e] * (c1[e + 1] - here)
        w0_last = W[0, x] - C[0, x] * (here - c1[x])
        w1 = W[1, e] - C[1, e] * (y_next(here, c1d_r[x]) - here)
        row = Fh[x] - Ch[x] * (here[0:1] - c1u_r[x])
        w2 = W[2, e] - C[2, e] * (z_next(here) - here)
        div = (w0 - w0_last) + (w1 - y_last(w1, row)) + (w2 - z_last(w2))
        return here + SC[x] * (S[x] - div)

    c2x_s[...] = sweep_two(0)

    def second_edges(x):
        c2y_s[x] = sweep_two(x)[0:1]

    loop(0, nx, second_edges)
    ey_dn.start()
    ex_dn.start()

    for copy in (cx_dn, cx_up):
        copy.wait_send()

    def first(x):
        c1[x + 1] = sweep_one(x)

    def second(x):
        c2[x] = sweep_two(x)

    def finish(x):
        e = x + 1
        here = c2[x]
        OP[x] = Pr[x] + here
        OV[0, x] = W[0, e] - C[0, e] * (c2[x + 1] - here)
        OV[1, x] = W[1, e] - C[1, e] * (y_next(here, c2y_r[x]) - here)
        OV[2, x] = W[2, e] - C[2, e] * (z_next(here) - here)

    stores = []

    def emit(a, b):
        k = len(stores)
        loop(a, b, finish)
        part = pl.ds(a, b - a)
        stores.append(pltpu.make_async_copy(OV.at[:, part], out_v.at[:, part], out_sem.at[k]))
        stores.append(pltpu.make_async_copy(OP.at[part], out_p.at[part], out_sem.at[k + 1]))
        for copy in stores[-2:]:
            copy.start()

    done = 0
    for k in range(2, len(groups)):
        last = k == len(groups) - 1
        if last:
            ex_dn.wait_recv()
            ey_dn.wait_recv()
            ready = done - 2
            emit(0, ready)
        arrive(k)
        stop = nx if last else groups[k][1]
        loop(done, stop, first)
        loop(max(done - 1, 0), nx if last else stop - 1, second)
        done = stop
    emit(ready, nx)

    @pl.when(has_next)
    def _():
        edge.wait_send()
        for copy in pieces:
            copy.wait_send()

    for copy in (vx_up, vx_dn, px_dn, nx_up, ry_up, ry_dn, fx_up, fy_up, cy_dn, cy_up, ex_dn, ey_dn):
        copy.wait_send()
    for copy in stores:
        copy.wait()


def place(from_v, from_p, out_v, out_p, sem):
    copies = [
        pltpu.make_async_copy(from_v.at[c], out_v.at[c], sem.at[c]) for c in range(3)
    ] + [pltpu.make_async_copy(from_p, out_p, sem.at[3])]
    for copy in copies:
        copy.start()
    for copy in copies:
        copy.wait()


def body(counts, velocity, pressure, forcing, source, viscosity):
    _, steps, nx, ny, nz = velocity.shape
    assert steps == 1 and nx >= 8 and ny >= 8 and ny % 4 == 0
    groups = [(0, 2), (nx - 2, nx)] + groups_of(2, nx - 4, 5) + [(nx - 4, nx - 2)]
    parts = (ny - 4) // 4
    vmem = lambda *shape: pltpu.VMEM(shape, jnp.float32)
    rows = lambda *lead: vmem(*lead, nx, 1, nz)
    any_space = pl.BlockSpec(memory_space=pl.ANY)
    out_v, out_p = pl.pallas_call(
        functools.partial(kernel, *counts, groups),
        out_shape=(
            jax.ShapeDtypeStruct((3, nx, ny, nz), jnp.float32),
            jax.ShapeDtypeStruct((nx, ny, nz), jnp.float32),
        ),
        in_specs=[any_space] * 5,
        out_specs=(any_space, any_space),
        scratch_shapes=[
            vmem(3, nx + 2, ny, nz), vmem(nx + 1, ny, nz), vmem(3, nx, ny, nz), vmem(nx, ny, nz),
            vmem(3, nx + 1, ny, nz), vmem(3, nx + 1, ny, nz), vmem(3, nx + 1, ny, nz),
            vmem(nx, ny, nz), vmem(nx + 2, ny, nz), vmem(nx + 1, ny, nz),
            vmem(3, nx, ny, nz), vmem(nx, ny, nz),
            vmem(3, nx, 4, nz), vmem(3, nx, 4, nz),
            vmem(nx, parts, 3, 4, nz), vmem(nx, parts, 3, 4, nz),
            rows(4), rows(4), rows(4), rows(4), rows(), rows(), rows(),
            rows(), rows(), rows(), rows(), vmem(ny, nz), rows(), rows(),
            pltpu.SemaphoreType.DMA((5,)),
            pltpu.SemaphoreType.DMA((4,)),
            pltpu.SemaphoreType.DMA((15 + len(groups),)),
            pltpu.SemaphoreType.DMA((15 + len(groups),)),
        ],
        compiler_params=pltpu.CompilerParams(
            collective_id=0, has_side_effects=True, vmem_limit_bytes=48 << 20
        ),
        name="smoother",
    )(*(pltpu.with_memory_space_constraint(a, pltpu.HBM) for a in (velocity[:, 0], pressure[0], forcing[:, 0], source[0], viscosity)))
    out_v, out_p = pl.pallas_call(
        place,
        out_shape=(
            jax.ShapeDtypeStruct(out_v.shape, jnp.float32),
            jax.ShapeDtypeStruct(out_p.shape, jnp.float32),
        ),
        in_specs=[any_space] * 2,
        out_specs=(any_space, any_space),
        scratch_shapes=[pltpu.SemaphoreType.DMA((4,))],
        compiler_params=pltpu.CompilerParams(vmem_limit_bytes=1 << 20),
        name="place",
    )(out_v, out_p)
    return out_v[:, None], out_p[None]


def solution(mesh):
    placed = (
        P(None, "ta", "gx", "gy", None),
        P("ta", "gx", "gy", None),
        P(None, "ta", "gx", "gy", None),
        P("ta", "gx", "gy", None),
        P(None, "gx", "gy", None),
    )
    counts = tuple(mesh.shape[axis] for axis in ("ta", "gx", "gy"))
    return jax.shard_map(
        functools.partial(body, counts),
        mesh=mesh,
        in_specs=placed,
        out_specs=(P(None, "ta", "gx", "gy", None), P("ta", "gx", "gy", None)),
        check_vma=False,
    )
```

```python
import functools

import jax
import jax.numpy as jnp
from jax import lax
from jax.experimental import pallas as pl
from jax.experimental.pallas import tpu as pltpu
from jax.sharding import PartitionSpec as P

relax_factor = 1.5
damping = 0.8
MESH = pl.DeviceIdType.MESH


def loop(lo, hi, body):
    def step(i, carry):
        body(i)
        return carry

    if hi > lo:
        lax.fori_loop(lo, hi, step, 0, unroll=hi - lo)


def row_index(f):
    return lax.broadcasted_iota(jnp.int32, f.shape, 0)


def y_next(f, row):
    n = f.shape[0]
    return jnp.where(row_index(f) == n - 1, row, pltpu.roll(f, n - 1, 0))


def y_last(f, row):
    return jnp.where(row_index(f) == 0, row, pltpu.roll(f, 1, 0))


def z_next(f):
    return pltpu.roll(f, f.shape[1] - 1, 1)


def z_last(f):
    return pltpu.roll(f, 1, 1)


def coeff_of(nu):
    return 1.0 / (relax_factor * (1.0 + 6.0 * nu))


def groups_of(lo, hi, size):
    return [(a, min(a + size, hi)) for a in range(lo, hi, size)]


def first_change(scale, source, w0, w0_last, w1, row, w2):
    div = (w0 - w0_last) + (w1 - y_last(w1, row)) + (w2 - z_last(w2))
    return scale * (source - div)


def second_change(scale, here, x_above, x_below, above, row, c0, c0_last, c1, c1_row, c2):
    g0, g0_last = c0 * (x_above - here), c0_last * (here - x_below)
    g1 = c1 * (y_next(here, above) - here)
    g2 = c2 * (z_next(here) - here)
    div = (g0 - g0_last) + (g1 - y_last(g1, c1_row * (here[0:1] - row))) + (g2 - z_last(g2))
    return 2.0 * here + scale * div


def final_velocity(w, c, here, x_above, above):
    return (
        w[0] - c[0] * (x_above - here),
        w[1] - c[1] * (y_next(here, above) - here),
        w[2] - c[2] * (z_next(here) - here),
    )


def kernel(
    slabs, nx_parts, ny_parts, groups, detour,
    vel, prs, frc, src, vis,
    OV, OP, rL, W, C, c1, c2, c2e, SC, S, Pr, up_r, Ch,
    V, F, Nu, sE, rE, sI, rI, rR, yu_s, yd_s, yu_r, yd_r, Ce, m_s, fe_s, fe_r, up_s, dn_s, dn_r,
    load_sem, send_sem, recv_sem,
):
    _, nx, ny, nz = vel.shape
    parts = (ny - 4) // 4
    final = len(groups) - 1
    ta, gx, gy = lax.axis_index("ta"), lax.axis_index("gx"), lax.axis_index("gy")
    t_next, t_prev = lax.rem(ta + 1, slabs), lax.rem(ta + slabs - 1, slabs)
    has_next, has_prev = ta < slabs - 1, ta > 0
    xu, xd = lax.rem(gx + 1, nx_parts), lax.rem(gx + nx_parts - 1, nx_parts)
    yu, yd = lax.rem(gy + 1, ny_parts), lax.rem(gy + ny_parts - 1, ny_parts)
    first_row = gy == 0

    loads = [
        pltpu.make_async_copy(vel, V.at[:, pl.ds(1, nx)], load_sem.at[0]),
        pltpu.make_async_copy(vis, Nu.at[:, pl.ds(1, nx)], load_sem.at[1]),
        pltpu.make_async_copy(prs, Pr.at[pl.ds(0, nx)], load_sem.at[2]),
        pltpu.make_async_copy(frc, F, load_sem.at[3]),
        pltpu.make_async_copy(src, S, load_sem.at[4]),
    ]
    for copy in loads:
        copy.start()

    barrier = pltpu.get_barrier_semaphore()

    def greet(axis, index):
        pl.semaphore_signal(barrier, inc=1, device_id={axis: index}, device_id_type=MESH)

    greet("gx", xu)
    greet("gx", xd)

    @pl.when(has_prev)
    def _():
        greet("ta", t_prev)

    expected = 2 + has_next.astype(jnp.int32) + jnp.where(first_row, 0, 2)
    if detour:
        giver, via, taker, lane = detour

        @pl.when(ta == via)
        def _():
            greet("ta", giver)

        @pl.when(ta == taker)
        def _():
            greet("ta", via)

        expected = expected + ((ta == giver) | (ta == via)).astype(jnp.int32)

    for beside in (yu, yd):

        @pl.when(jnp.logical_not(first_row) & (beside != 0))
        def _():
            greet("gy", beside)

    def remote(k, source, target, axis, index):
        return pltpu.make_async_remote_copy(
            src_ref=source, dst_ref=target, send_sem=send_sem.at[k], recv_sem=recv_sem.at[k],
            device_id={axis: index}, device_id_type=MESH,
        )

    vx_up = remote(0, V.at[:, nx], V.at[:, 0], "gx", xu)
    vx_dn = remote(1, V.at[:, 1], V.at[:, nx + 1], "gx", xd)
    px_dn = remote(2, Pr.at[0], Pr.at[nx], "gx", xd)
    nx_up = remote(3, Nu.at[0, nx], Nu.at[0, 0], "gx", xu)
    ry_up = remote(4, yu_s, yu_r, "gy", yu)
    ry_dn = remote(5, yd_s, yd_r, "gy", yd)
    fe_up = remote(6, fe_s, fe_r, "gx", xu)
    fx_up = remote(7, W.at[0, nx], W.at[0, 0], "gx", xu)
    cx_dn = remote(8, c1.at[1], c1.at[nx + 1], "gx", xd)
    cx_up = remote(9, c1.at[nx], c1.at[0], "gx", xu)
    m_dn = remote(10, m_s, Ce.at[:, pl.ds(1, nx)], "gy", yd)
    ce_up = remote(11, Ce.at[0, nx], Ce.at[0, 0], "gx", xu)
    y_up = remote(12, up_s, up_r, "gy", yu)
    y_dn = remote(13, dn_s, dn_r, "gy", yd)
    ex_dn = remote(14, c2.at[0], c2.at[nx], "gx", xd)
    edge = remote(15, sE, rE, "ta", t_next)
    landing = [rI.at[pl.ds(a, b - a)] for a, b in groups[:final]] + [rL]
    leaving = [sI.at[pl.ds(a, b - a)] for a, b in groups]
    pieces = [remote(16 + k, leaving[k], landing[k], "ta", t_next) for k in range(final + 1)]
    if detour:
        to_via = remote(17 + final, leaving[lane], rR, "ta", via)
        from_via = remote(16 + lane, rR, landing[lane], "ta", taker)

    def pack_edges(x):
        for c in range(3):
            sE[c, x, 0:2] = V[c, x + 1, 0:2]
            sE[c, x, 2:4] = V[c, x + 1, ny - 2 : ny]

    def pack_rows(x):
        for c in range(3):
            yu_s[c, x] = V[c, x + 1, ny - 1 : ny]
            yd_s[c, x] = V[c, x + 1, 0:1]
        yu_s[3, x] = Nu[1, x + 1, ny - 1 : ny]
        yd_s[3, x] = Pr[x, 0:1]

    def pack_inner(x):
        for c in range(3):
            for p in range(parts):
                sI[x, p, c] = V[c, x + 1, 2 + 4 * p : 6 + 4 * p]

    loads[0].wait()
    loop(0, nx, pack_edges)
    pl.semaphore_wait(barrier, expected)
    for beside in (yu, yd):

        @pl.when(first_row | (beside == 0))
        def _():
            greet("gy", beside)

    @pl.when(has_next)
    def _():
        edge.start()

    loads[1].wait()
    loads[2].wait()
    loop(0, nx, pack_rows)
    for copy in (vx_up, vx_dn, px_dn, nx_up):
        copy.start()

    @pl.when(jnp.logical_not(first_row))
    def _():
        ry_up.start()
        ry_dn.start()

    loop(0, nx, pack_inner)

    @pl.when(has_next)
    def _():
        for k, copy in enumerate(pieces):
            if detour and k == lane:

                @pl.when(ta == giver)
                def _():
                    to_via.start()

                @pl.when(ta != giver)
                def _():
                    copy.start()

            else:
                copy.start()

    @pl.when(first_row)
    def _():
        pl.semaphore_wait(barrier, 2)
        ry_up.start()
        ry_dn.start()

    loads[3].wait()
    loads[4].wait()
    for copy in (vx_up, vx_dn, px_dn, nx_up, ry_up, ry_dn):
        copy.wait_recv()
    C[0, 0] = coeff_of(Nu[0, 0])

    def prepare(x):
        e = x + 1
        below = coeff_of(yu_r[3, x])
        Ch[x] = below
        coeff = [coeff_of(Nu[c, e]) for c in range(3)]
        for c in range(3):
            C[c, e] = coeff[c]
            m_s[c, x] = coeff[c][0:1]
        total = coeff[0] + C[0, x] + coeff[1] + y_last(coeff[1], below) + coeff[2] + z_last(coeff[2])
        scale = damping / total
        SC[x] = scale
        m_s[3, x] = scale[0:1]
        press = Pr[x]
        grads = (Pr[x + 1] - press, y_next(press, yd_r[3, x]) - press, z_next(press) - press)
        for c in range(3):
            v = V[c, e]
            near = V[c, e - 1] + V[c, e + 1] + y_last(v, yu_r[c, x]) + y_next(v, yd_r[c, x])
            near = near + z_last(v) + z_next(v)
            momentum = F[c, x] - (v + Nu[c, e] * (6.0 * v - near)) - grads[c]
            W[c, e] = v + coeff[c] * momentum

    loop(0, nx, prepare)
    m_dn.start()
    if detour:

        @pl.when(ta == via)
        def _():
            to_via.wait_recv()
            from_via.start()

    def add_edges(x):
        for c in range(3):
            for s, t in ((0, 0), (2, ny - 2)):
                W[c, x + 1, t : t + 2] = (
                    W[c, x + 1, t : t + 2] + C[c, x + 1, t : t + 2] * rE[c, x, s : s + 2]
                )

    def add_inner(x):
        for c in range(3):
            for p in range(parts):
                t = 2 + 4 * p
                W[c, x + 1, t : t + 4] = W[c, x + 1, t : t + 4] + C[c, x + 1, t : t + 4] * rI[x, p, c]

    def arrive(k):
        @pl.when(has_prev)
        def _():
            pieces[k].wait_recv()
            loop(*groups[k], add_inner)

    @pl.when(has_prev)
    def _():
        edge.wait_recv()
        loop(0, nx, add_edges)

    fe_s[...] = W[0, nx]
    fe_up.start()
    fe_up.wait_recv()

    def edge_rows(x, w0_last):
        e = x + 1
        zero = jnp.zeros((1, nz), jnp.float32)
        change = first_change(SC[x], S[x], W[0, e], w0_last, W[1, e], zero, W[2, e])
        up_s[0, x] = W[1, e, ny - 1 : ny]
        up_s[1, x] = change[ny - 1 : ny]
        dn_s[0, x] = change[0:1]
        dn_s[1, x] = change[1:2]

    edge_rows(0, fe_r[...])
    loop(1, nx, lambda x: edge_rows(x, W[0, x]))
    y_up.start()
    y_dn.start()

    arrive(0)
    arrive(1)
    fx_up.start()
    m_dn.wait_recv()
    ce_up.start()
    for copy in (fx_up, y_up, y_dn):
        copy.wait_recv()

    def first(x):
        e = x + 1
        c1[e, 0:ny] = first_change(SC[x], S[x], W[0, e], W[0, x], W[1, e], up_r[0, x], W[2, e])

    def first_above(x):
        e = x + 1
        c1[e, ny : ny + 1] = dn_r[0, x] + Ce[3, e] * W[1, e, ny - 1 : ny]

    loop(0, nx, first)
    loop(0, nx, first_above)
    for copy in (cx_dn, cx_up):
        copy.start()
    for copy in (cx_dn, cx_up, ce_up):
        copy.wait_recv()

    def second(x):
        e = x + 1
        c2[x] = second_change(
            SC[x], c1[e, 0:ny], c1[e + 1, 0:ny], c1[e - 1, 0:ny], c1[e, ny : ny + 1], up_r[1, x],
            C[0, e], C[0, x], C[1, e], Ch[x], C[2, e],
        )

    def second_above(x):
        e = x + 1
        wide = lambda row: jnp.broadcast_to(row, (8, nz))
        here = wide(c1[e, ny : ny + 1])
        g0 = wide(Ce[0, e]) * (wide(c1[e + 1, ny : ny + 1]) - here)
        g0_last = wide(Ce[0, x]) * (here - wide(c1[e - 1, ny : ny + 1]))
        g1 = wide(Ce[1, e]) * (wide(dn_r[1, x]) - here)
        g1_last = wide(C[1, e, ny - 1 : ny]) * (here - wide(c1[e, ny - 1 : ny]))
        g2 = wide(Ce[2, e]) * (z_next(here) - here)
        div = (g0 - g0_last) + (g1 - g1_last) + (g2 - z_last(g2))
        c2e[x] = (2.0 * here + wide(Ce[3, e]) * div)[0:1]

    second(0)
    ex_dn.start()
    loop(0, nx, second_above)

    def finish(x):
        e = x + 1
        here = c2[x]
        OP[x] = Pr[x] + here
        moved = final_velocity(
            [W[c, e] for c in range(3)], [C[c, e] for c in range(3)], here, c2[x + 1], c2e[x]
        )
        for c in range(3):
            OV[c, x] = moved[c]

    for k in range(2, final):
        a, b = groups[k]
        arrive(k)
        loop(a, b, first)
        loop(a - 1, b - 1, second)
        loop(a - 2, b - 2, finish)

    ex_dn.wait_recv()

    @pl.when(has_prev)
    def _():
        pieces[final].wait_recv()

    @pl.when(jnp.logical_not(has_prev))
    def _():
        rL[...] = jnp.zeros_like(rL)

    @pl.when(has_next)
    def _():
        edge.wait_send()
        for k, copy in enumerate(pieces):
            if detour and k == lane:

                @pl.when(ta == giver)
                def _():
                    to_via.wait_send()

                @pl.when(ta != giver)
                def _():
                    copy.wait_send()

            else:
                copy.wait_send()

    if detour:

        @pl.when(ta == via)
        def _():
            from_via.wait_send()

    for copy in (
        vx_up, vx_dn, px_dn, nx_up, ry_up, ry_dn, fe_up, fx_up, cx_dn, cx_up, m_dn, ce_up, y_up, y_dn, ex_dn
    ):
        copy.wait_send()


def settle(
    last, moved, pressed, rL, W, C, c1, c2, c2e, SC, S, Pr, up_r, Ch, out_v, out_p, nV, nP, nW, n1, n2, sem
):
    _, nx, ny, nz = out_v.shape
    parts = (ny - 4) // 4
    a, b = last
    ready = a - 2

    early = [
        pltpu.make_async_copy(moved.at[c, pl.ds(0, ready)], out_v.at[c, pl.ds(0, ready)], sem.at[c])
        for c in range(3)
    ] + [pltpu.make_async_copy(pressed.at[pl.ds(0, ready)], out_p.at[pl.ds(0, ready)], sem.at[3])]
    for copy in early:
        copy.start()

    def w(c, x):
        return nW[c, x - a] if a <= x < b else W[c, x + 1]

    def change(x):
        return n1[x - a] if a <= x < nx - 1 else c1[x + 1, 0:ny]

    def second(x):
        return n2[x - (a - 1)] if a - 1 <= x < nx else c2[x]

    for x in range(a, b):
        for c in range(3):
            nW[c, x - a, 0:2] = W[c, x + 1, 0:2]
            nW[c, x - a, ny - 2 : ny] = W[c, x + 1, ny - 2 : ny]
            for p in range(parts):
                t = 2 + 4 * p
                nW[c, x - a, t : t + 4] = W[c, x + 1, t : t + 4] + C[c, x + 1, t : t + 4] * rL[x - a, p, c]
    for x in range(a, nx - 1):
        n1[x - a] = first_change(SC[x], S[x], w(0, x), w(0, x - 1), w(1, x), up_r[0, x], w(2, x))
    for x in range(a - 1, nx):
        e = x + 1
        n2[x - (a - 1)] = second_change(
            SC[x], change(x), change(x + 1), change(x - 1), c1[e, ny : ny + 1], up_r[1, x],
            C[0, e], C[0, x], C[1, e], Ch[x], C[2, e],
        )
    for x in range(ready, nx):
        e = x + 1
        here = second(x)
        nP[x - ready] = Pr[x] + here
        fresh = final_velocity(
            [w(c, x) for c in range(3)], [C[c, e] for c in range(3)], here, second(x + 1), c2e[x]
        )
        for c in range(3):
            nV[c, x - ready] = fresh[c]
    late = [
        pltpu.make_async_copy(nV.at[c], out_v.at[c, pl.ds(ready, nx - ready)], sem.at[4 + c]) for c in range(3)
    ] + [pltpu.make_async_copy(nP, out_p.at[pl.ds(ready, nx - ready)], sem.at[7])]
    for copy in late:
        copy.start()
    for copy in early + late:
        copy.wait()


def body(counts, velocity, pressure, forcing, source, viscosity):
    _, steps, nx, ny, nz = velocity.shape
    assert steps == 1 and nx >= 8 and ny >= 8 and ny % 4 == 0
    groups = [(0, 2), (nx - 2, nx), (2, 4)] + groups_of(4, nx - 4, 4) + [(nx - 4, nx - 2)]
    detour = (1, 3, 2, 2) if counts[0] == 4 else None
    last = groups[-1]
    parts = (ny - 4) // 4
    vmem = lambda *shape: pltpu.VMEM(shape, jnp.float32)
    rows = lambda *lead: vmem(*lead, nx, 1, nz)
    any_space = pl.BlockSpec(memory_space=pl.ANY)
    on_chip = pl.BlockSpec(memory_space=pltpu.VMEM)
    kept = (
        vmem(3, nx, ny, nz), vmem(nx, ny, nz), vmem(last[1] - last[0], parts, 3, 4, nz),
        vmem(3, nx + 1, ny, nz), vmem(3, nx + 1, ny, nz), vmem(nx + 2, ny + 8, nz), vmem(nx + 1, ny, nz), rows(),
        vmem(nx, ny, nz), vmem(nx, ny, nz), vmem(nx + 1, ny, nz), rows(2), rows(),
    )
    inputs = (velocity[:, 0], pressure[0], forcing[:, 0], source[0], viscosity)
    held = pl.pallas_call(
        functools.partial(kernel, *counts, groups, detour),
        out_shape=kept,
        in_specs=[any_space] * 5,
        out_specs=(on_chip,) * len(kept),
        scratch_shapes=[
            vmem(3, nx + 2, ny, nz), vmem(3, nx, ny, nz), vmem(3, nx + 1, ny, nz),
            vmem(3, nx, 4, nz), vmem(3, nx, 4, nz),
            vmem(nx, parts, 3, 4, nz), vmem(nx, parts, 3, 4, nz), vmem(2, parts, 3, 4, nz),
            rows(4), rows(4), rows(4), rows(4), vmem(4, nx + 1, 1, nz), rows(4),
            vmem(ny, nz), vmem(ny, nz), rows(2), rows(2), rows(2),
            pltpu.SemaphoreType.DMA((5,)),
            pltpu.SemaphoreType.DMA((17 + len(groups),)),
            pltpu.SemaphoreType.DMA((17 + len(groups),)),
        ],
        compiler_params=pltpu.CompilerParams(
            collective_id=0, has_side_effects=True, vmem_limit_bytes=40 << 20
        ),
        name="smoother",
    )(*(pltpu.with_memory_space_constraint(a, pltpu.HBM) for a in inputs))
    out_v, out_p = pl.pallas_call(
        functools.partial(settle, last),
        out_shape=(
            jax.ShapeDtypeStruct((3, nx, ny, nz), jnp.float32),
            jax.ShapeDtypeStruct((nx, ny, nz), jnp.float32),
        ),
        in_specs=[on_chip] * len(kept),
        out_specs=(any_space, any_space),
        scratch_shapes=[
            vmem(3, 6, ny, nz), vmem(6, ny, nz), vmem(3, 2, ny, nz), vmem(3, ny, nz), vmem(5, ny, nz),
            pltpu.SemaphoreType.DMA((8,)),
        ],
        compiler_params=pltpu.CompilerParams(vmem_limit_bytes=2 << 20),
        name="settle",
    )(*held)
    return out_v[:, None], out_p[None]


def solution(mesh):
    placed = (
        P(None, "ta", "gx", "gy", None),
        P("ta", "gx", "gy", None),
        P(None, "ta", "gx", "gy", None),
        P("ta", "gx", "gy", None),
        P(None, "gx", "gy", None),
    )
    counts = tuple(mesh.shape[axis] for axis in ("ta", "gx", "gy"))
    return jax.shard_map(
        functools.partial(body, counts),
        mesh=mesh,
        in_specs=placed,
        out_specs=(P(None, "ta", "gx", "gy", None), P("ta", "gx", "gy", None)),
        check_vma=False,
    )
```

```python
import functools

import jax
import jax.numpy as jnp
from jax import lax
from jax.experimental import pallas as pl
from jax.experimental.pallas import tpu as pltpu
from jax.sharding import PartitionSpec as P

relax_factor = 1.5
damping = 0.8
MESH = pl.DeviceIdType.MESH


def loop(lo, hi, body):
    def step(i, carry):
        body(i)
        return carry

    if hi > lo:
        lax.fori_loop(lo, hi, step, 0, unroll=hi - lo)


def row_index(f):
    return lax.broadcasted_iota(jnp.int32, f.shape, 0)


def y_next(f, row):
    n = f.shape[0]
    return jnp.where(row_index(f) == n - 1, row, pltpu.roll(f, n - 1, 0))


def y_last(f, row):
    return jnp.where(row_index(f) == 0, row, pltpu.roll(f, 1, 0))


def z_next(f):
    return pltpu.roll(f, f.shape[1] - 1, 1)


def z_last(f):
    return pltpu.roll(f, 1, 1)


def coeff_of(nu):
    return 1.0 / (relax_factor * (1.0 + 6.0 * nu))


def groups_of(lo, hi, size):
    return [(a, min(a + size, hi)) for a in range(lo, hi, size)]


def first_change(scale, source, w0, w0_last, w1, row, w2):
    div = (w0 - w0_last) + (w1 - y_last(w1, row)) + (w2 - z_last(w2))
    return scale * (source - div)


def second_change(scale, here, x_above, x_below, above, row, c0, c0_last, c1, c1_row, c2):
    g0, g0_last = c0 * (x_above - here), c0_last * (here - x_below)
    g1 = c1 * (y_next(here, above) - here)
    g2 = c2 * (z_next(here) - here)
    div = (g0 - g0_last) + (g1 - y_last(g1, c1_row * (here[0:1] - row))) + (g2 - z_last(g2))
    return 2.0 * here + scale * div


def final_velocity(w, c, here, x_above, above):
    return (
        w[0] - c[0] * (x_above - here),
        w[1] - c[1] * (y_next(here, above) - here),
        w[2] - c[2] * (z_next(here) - here),
    )


def kernel(
    slabs, nx_parts, ny_parts, groups, detour,
    vel, prs, frc, src, vis,
    OV, OP, rL, W, C, c1, c2, c2e, SC, S, Pr, up_r, Ch,
    V, F, Nu, sE, rE, sI, rI, rR, yu_s, yd_s, yu_r, yd_r, Ce, m_s, fe_s, fe_r, up_s, dn_s, dn_r, tally,
    load_sem, send_sem, recv_sem,
):
    _, nx, ny, nz = vel.shape
    parts = (ny - 4) // 4
    final = len(groups) - 1
    ta, gx, gy = lax.axis_index("ta"), lax.axis_index("gx"), lax.axis_index("gy")
    t_next, t_prev = lax.rem(ta + 1, slabs), lax.rem(ta + slabs - 1, slabs)
    has_next, has_prev = ta < slabs - 1, ta > 0
    xu, xd = lax.rem(gx + 1, nx_parts), lax.rem(gx + nx_parts - 1, nx_parts)
    yu, yd = lax.rem(gy + 1, ny_parts), lax.rem(gy + ny_parts - 1, ny_parts)
    first_row = gy == 0

    barrier = pltpu.get_barrier_semaphore()

    def greet(axis, index):
        pl.semaphore_signal(barrier, inc=1, device_id={axis: index}, device_id_type=MESH)

    greet("gx", xu)
    greet("gx", xd)

    @pl.when(has_prev)
    def _():
        greet("ta", t_prev)

    expected = 2 + has_next.astype(jnp.int32) + jnp.where(first_row, 0, 2)
    if detour:
        giver, via, taker, lane = detour

        @pl.when(ta == via)
        def _():
            greet("ta", giver)

        @pl.when(ta == taker)
        def _():
            greet("ta", via)

        expected = expected + ((ta == giver) | (ta == via)).astype(jnp.int32)

    for beside in (yu, yd):

        @pl.when(jnp.logical_not(first_row) & (beside != 0))
        def _():
            greet("gy", beside)

    def fetch(source, target, k):
        pltpu.make_async_copy(source, target, load_sem.at[k]).start()

    def wait_rows(sem, count):
        size = pl.ds(0, count)
        pltpu.make_async_copy(tally.at[size], tally.at[size], sem).wait()

    half = nx // 2
    for a, n in ((0, half), (half, nx - half)):
        for c in range(3):
            fetch(vel.at[c, pl.ds(a, n)], V.at[c, pl.ds(1 + a, n)], 0)
    fetch(vis, Nu.at[:, pl.ds(1, nx)], 1)
    fetch(prs, Pr.at[pl.ds(0, nx)], 1)
    fetch(frc, F, 2)
    fetch(src, S, 2)

    def remote(send, recv, source, target, axis, index):
        return pltpu.make_async_remote_copy(
            src_ref=source, dst_ref=target, send_sem=send_sem.at[send], recv_sem=recv_sem.at[recv],
            device_id={axis: index}, device_id_type=MESH,
        )

    vx_up = remote(0, 0, V.at[:, nx], V.at[:, 0], "gx", xu)
    vx_dn = remote(0, 0, V.at[:, 1], V.at[:, nx + 1], "gx", xd)
    px_dn = remote(0, 0, Pr.at[0], Pr.at[nx], "gx", xd)
    nx_up = remote(0, 0, Nu.at[0, nx], Nu.at[0, 0], "gx", xu)
    ry_up = remote(0, 0, yu_s, yu_r, "gy", yu)
    ry_dn = remote(0, 0, yd_s, yd_r, "gy", yd)
    fe_up = remote(0, 1, fe_s, fe_r, "gx", xu)
    fx_up = remote(0, 3, W.at[0, nx], W.at[0, 0], "gx", xu)
    cx_dn = remote(0, 4, c1.at[1], c1.at[nx + 1], "gx", xd)
    cx_up = remote(0, 4, c1.at[nx], c1.at[0], "gx", xu)
    m_dn = remote(0, 2, m_s, Ce.at[:, pl.ds(1, nx)], "gy", yd)
    ce_up = remote(3, 5, Ce.at[0, nx], Ce.at[0, 0], "gx", xu)
    y_up = remote(0, 3, up_s, up_r, "gy", yu)
    y_dn = remote(0, 3, dn_s, dn_r, "gy", yd)
    ex_dn = remote(0, 6, c2.at[0], c2.at[nx], "gx", xd)
    edge = remote(1, 7, sE, rE, "ta", t_next)
    landing = [rI.at[pl.ds(a, b - a)] for a, b in groups[:final]] + [rL]
    leaving = [sI.at[pl.ds(a, b - a)] for a, b in groups]
    pieces = [remote(1, 8 + k, leaving[k], landing[k], "ta", t_next) for k in range(final + 1)]
    if detour:
        to_via = remote(1, 9 + final, leaving[lane], rR, "ta", via)
        from_via = remote(2, 8 + lane, rR, landing[lane], "ta", taker)

    def pack_edges(x):
        for c in range(3):
            sE[c, x, 0:2] = V[c, x + 1, 0:2]
            sE[c, x, 2:4] = V[c, x + 1, ny - 2 : ny]

    def pack_rows(x):
        for c in range(3):
            yu_s[c, x] = V[c, x + 1, ny - 1 : ny]
            yd_s[c, x] = V[c, x + 1, 0:1]
        yu_s[3, x] = Nu[1, x + 1, ny - 1 : ny]
        yd_s[3, x] = Pr[x, 0:1]

    def pack_inner(x):
        for c in range(3):
            for p in range(parts):
                sI[x, p, c] = V[c, x + 1, 2 + 4 * p : 6 + 4 * p]

    wait_rows(load_sem.at[0], 3 * nx * ny)
    loop(0, nx, pack_edges)
    pl.semaphore_wait(barrier, expected)
    for beside in (yu, yd):

        @pl.when(first_row | (beside == 0))
        def _():
            greet("gy", beside)

    @pl.when(has_next)
    def _():
        edge.start()

    wait_rows(load_sem.at[1], 4 * nx * ny)
    loop(0, nx, pack_rows)
    for copy in (vx_up, vx_dn, px_dn, nx_up):
        copy.start()

    @pl.when(jnp.logical_not(first_row))
    def _():
        ry_up.start()
        ry_dn.start()

    loop(0, nx, pack_inner)

    @pl.when(has_next)
    def _():
        for k, copy in enumerate(pieces):
            if detour and k == lane:

                @pl.when(ta == giver)
                def _():
                    to_via.start()

                @pl.when(ta != giver)
                def _():
                    copy.start()

            else:
                copy.start()

    @pl.when(first_row)
    def _():
        pl.semaphore_wait(barrier, 2)
        ry_up.start()
        ry_dn.start()

    wait_rows(load_sem.at[2], 4 * nx * ny)
    wait_rows(recv_sem.at[0], 8 * (ny + nx))
    C[0, 0] = coeff_of(Nu[0, 0])

    def prepare(x):
        e = x + 1
        below = coeff_of(yu_r[3, x])
        Ch[x] = below
        coeff = [coeff_of(Nu[c, e]) for c in range(3)]
        for c in range(3):
            C[c, e] = coeff[c]
            m_s[c, x] = coeff[c][0:1]
        total = coeff[0] + C[0, x] + coeff[1] + y_last(coeff[1], below) + coeff[2] + z_last(coeff[2])
        scale = damping / total
        SC[x] = scale
        m_s[3, x] = scale[0:1]
        press = Pr[x]
        grads = (Pr[x + 1] - press, y_next(press, yd_r[3, x]) - press, z_next(press) - press)
        for c in range(3):
            v = V[c, e]
            near = V[c, e - 1] + V[c, e + 1] + y_last(v, yu_r[c, x]) + y_next(v, yd_r[c, x])
            near = near + z_last(v) + z_next(v)
            momentum = F[c, x] - (v + Nu[c, e] * (6.0 * v - near)) - grads[c]
            W[c, e] = v + coeff[c] * momentum

    loop(0, nx, prepare)
    m_dn.start()
    if detour:

        @pl.when(ta == via)
        def _():
            to_via.wait_recv()
            from_via.start()

    def add_edges(x):
        for c in range(3):
            for s, t in ((0, 0), (2, ny - 2)):
                W[c, x + 1, t : t + 2] = (
                    W[c, x + 1, t : t + 2] + C[c, x + 1, t : t + 2] * rE[c, x, s : s + 2]
                )

    def add_inner(x):
        for c in range(3):
            for p in range(parts):
                t = 2 + 4 * p
                W[c, x + 1, t : t + 4] = W[c, x + 1, t : t + 4] + C[c, x + 1, t : t + 4] * rI[x, p, c]

    def arrive(k):
        @pl.when(has_prev)
        def _():
            pieces[k].wait_recv()
            loop(*groups[k], add_inner)

    @pl.when(has_prev)
    def _():
        edge.wait_recv()
        loop(0, nx, add_edges)

    fe_s[...] = W[0, nx]
    fe_up.start()
    fe_up.wait_recv()

    def edge_rows(x, w0_last):
        e = x + 1
        zero = jnp.zeros((1, nz), jnp.float32)
        change = first_change(SC[x], S[x], W[0, e], w0_last, W[1, e], zero, W[2, e])
        up_s[0, x] = W[1, e, ny - 1 : ny]
        up_s[1, x] = change[ny - 1 : ny]
        dn_s[0, x] = change[0:1]
        dn_s[1, x] = change[1:2]

    edge_rows(0, fe_r[...])
    loop(1, nx, lambda x: edge_rows(x, W[0, x]))
    y_up.start()
    y_dn.start()

    arrive(0)
    arrive(1)
    fx_up.start()
    m_dn.wait_recv()
    ce_up.start()
    wait_rows(recv_sem.at[3], ny + 4 * nx)

    def first(x):
        e = x + 1
        c1[e, 0:ny] = first_change(SC[x], S[x], W[0, e], W[0, x], W[1, e], up_r[0, x], W[2, e])

    def first_above(x):
        e = x + 1
        c1[e, ny : ny + 1] = dn_r[0, x] + Ce[3, e] * W[1, e, ny - 1 : ny]

    loop(0, nx, first)
    loop(0, nx, first_above)
    for copy in (cx_dn, cx_up):
        copy.start()
    wait_rows(recv_sem.at[4], 2 * (ny + 8))
    ce_up.wait_recv()

    def second(x):
        e = x + 1
        c2[x] = second_change(
            SC[x], c1[e, 0:ny], c1[e + 1, 0:ny], c1[e - 1, 0:ny], c1[e, ny : ny + 1], up_r[1, x],
            C[0, e], C[0, x], C[1, e], Ch[x], C[2, e],
        )

    def second_above(x):
        e = x + 1
        wide = lambda row: jnp.broadcast_to(row, (8, nz))
        here = wide(c1[e, ny : ny + 1])
        g0 = wide(Ce[0, e]) * (wide(c1[e + 1, ny : ny + 1]) - here)
        g0_last = wide(Ce[0, x]) * (here - wide(c1[e - 1, ny : ny + 1]))
        g1 = wide(Ce[1, e]) * (wide(dn_r[1, x]) - here)
        g1_last = wide(C[1, e, ny - 1 : ny]) * (here - wide(c1[e, ny - 1 : ny]))
        g2 = wide(Ce[2, e]) * (z_next(here) - here)
        div = (g0 - g0_last) + (g1 - g1_last) + (g2 - z_last(g2))
        c2e[x] = (2.0 * here + wide(Ce[3, e]) * div)[0:1]

    second(0)
    ex_dn.start()
    loop(0, nx, second_above)

    def finish(x):
        e = x + 1
        here = c2[x]
        OP[x] = Pr[x] + here
        moved = final_velocity(
            [W[c, e] for c in range(3)], [C[c, e] for c in range(3)], here, c2[x + 1], c2e[x]
        )
        for c in range(3):
            OV[c, x] = moved[c]

    for k in range(2, final):
        a, b = groups[k]
        arrive(k)
        loop(a, b, first)
        loop(a - 1, b - 1, second)
        loop(a - 2, b - 2, finish)

    ex_dn.wait_recv()

    @pl.when(has_prev)
    def _():
        pieces[final].wait_recv()

    @pl.when(jnp.logical_not(has_prev))
    def _():
        rL[...] = jnp.zeros_like(rL)

    @pl.when(has_next)
    def _():
        wait_rows(send_sem.at[1], 3 * nx * ny)

    if detour:

        @pl.when(ta == via)
        def _():
            from_via.wait_send()

    ce_up.wait_send()
    wait_rows(send_sem.at[0], 13 * ny + 16 + 16 * nx)


def settle(
    last, moved, pressed, rL, W, C, c1, c2, c2e, SC, S, Pr, up_r, Ch, out_v, out_p, nV, nP, nW, n1, n2, sem
):
    _, nx, ny, nz = out_v.shape
    parts = (ny - 4) // 4
    a, b = last
    ready = a - 2

    early = [
        pltpu.make_async_copy(moved.at[c, pl.ds(0, ready)], out_v.at[c, pl.ds(0, ready)], sem.at[c])
        for c in range(3)
    ] + [pltpu.make_async_copy(pressed.at[pl.ds(0, ready)], out_p.at[pl.ds(0, ready)], sem.at[3])]
    for copy in early:
        copy.start()

    def w(c, x):
        return nW[c, x - a] if a <= x < b else W[c, x + 1]

    def change(x):
        return n1[x - a] if a <= x < nx - 1 else c1[x + 1, 0:ny]

    def second(x):
        return n2[x - (a - 1)] if a - 1 <= x < nx else c2[x]

    late = [
        pltpu.make_async_copy(nV.at[c], out_v.at[c, pl.ds(ready, nx - ready)], sem.at[4 + c]) for c in range(3)
    ] + [pltpu.make_async_copy(nP, out_p.at[pl.ds(ready, nx - ready)], sem.at[7])]

    @pl.when(lax.axis_index("ta") >= 0)
    def _():
        for x in range(a, b):
            for c in range(3):
                nW[c, x - a, 0:2] = W[c, x + 1, 0:2]
                nW[c, x - a, ny - 2 : ny] = W[c, x + 1, ny - 2 : ny]
                for p in range(parts):
                    t = 2 + 4 * p
                    nW[c, x - a, t : t + 4] = W[c, x + 1, t : t + 4] + C[c, x + 1, t : t + 4] * rL[x - a, p, c]
        for x in range(a, nx - 1):
            n1[x - a] = first_change(SC[x], S[x], w(0, x), w(0, x - 1), w(1, x), up_r[0, x], w(2, x))
        for x in range(a - 1, nx):
            e = x + 1
            n2[x - (a - 1)] = second_change(
                SC[x], change(x), change(x + 1), change(x - 1), c1[e, ny : ny + 1], up_r[1, x],
                C[0, e], C[0, x], C[1, e], Ch[x], C[2, e],
            )
        for x in range(ready, nx):
            e = x + 1
            here = second(x)
            nP[x - ready] = Pr[x] + here
            fresh = final_velocity(
                [w(c, x) for c in range(3)], [C[c, e] for c in range(3)], here, second(x + 1), c2e[x]
            )
            for c in range(3):
                nV[c, x - ready] = fresh[c]
        for copy in late:
            copy.start()

    for copy in early + late:
        copy.wait()


def body(counts, velocity, pressure, forcing, source, viscosity):
    _, steps, nx, ny, nz = velocity.shape
    assert steps == 1 and nx >= 8 and ny >= 8 and ny % 4 == 0
    groups = [(0, 2), (nx - 2, nx), (2, 4)] + groups_of(4, nx - 4, 4) + [(nx - 4, nx - 2)]
    detour = (1, 3, 2, 2) if counts[0] == 4 else None
    last = groups[-1]
    parts = (ny - 4) // 4
    vmem = lambda *shape: pltpu.VMEM(shape, jnp.float32)
    rows = lambda *lead: vmem(*lead, nx, 1, nz)
    any_space = pl.BlockSpec(memory_space=pl.ANY)
    on_chip = pl.BlockSpec(memory_space=pltpu.VMEM)
    kept = (
        vmem(3, nx, ny, nz), vmem(nx, ny, nz), vmem(last[1] - last[0], parts, 3, 4, nz),
        vmem(3, nx + 1, ny, nz), vmem(3, nx + 1, ny, nz), vmem(nx + 2, ny + 8, nz), vmem(nx + 1, ny, nz), rows(),
        vmem(nx, ny, nz), vmem(nx, ny, nz), vmem(nx + 1, ny, nz), rows(2), rows(),
    )
    inputs = (velocity[:, 0], pressure[0], forcing[:, 0], source[0], viscosity)
    held = pl.pallas_call(
        functools.partial(kernel, *counts, groups, detour),
        out_shape=kept,
        in_specs=[any_space] * 5,
        out_specs=(on_chip,) * len(kept),
        scratch_shapes=[
            vmem(3, nx + 2, ny, nz), vmem(3, nx, ny, nz), vmem(3, nx + 1, ny, nz),
            vmem(3, nx, 4, nz), vmem(3, nx, 4, nz),
            vmem(nx, parts, 3, 4, nz), vmem(nx, parts, 3, 4, nz), vmem(2, parts, 3, 4, nz),
            rows(4), rows(4), rows(4), rows(4), vmem(4, nx + 1, 1, nz), rows(4),
            vmem(ny, nz), vmem(ny, nz), rows(2), rows(2), rows(2), vmem(4 * nx * ny, nz),
            pltpu.SemaphoreType.DMA((3,)),
            pltpu.SemaphoreType.DMA((4,)),
            pltpu.SemaphoreType.DMA((9 + len(groups),)),
        ],
        compiler_params=pltpu.CompilerParams(
            collective_id=0, has_side_effects=True, vmem_limit_bytes=40 << 20
        ),
        name="smoother",
    )(*(pltpu.with_memory_space_constraint(a, pltpu.HBM) for a in inputs))
    out_v, out_p = pl.pallas_call(
        functools.partial(settle, last),
        out_shape=(
            jax.ShapeDtypeStruct((3, nx, ny, nz), jnp.float32),
            jax.ShapeDtypeStruct((nx, ny, nz), jnp.float32),
        ),
        in_specs=[on_chip] * len(kept),
        out_specs=(any_space, any_space),
        scratch_shapes=[
            vmem(3, 6, ny, nz), vmem(6, ny, nz), vmem(3, 2, ny, nz), vmem(3, ny, nz), vmem(5, ny, nz),
            pltpu.SemaphoreType.DMA((8,)),
        ],
        compiler_params=pltpu.CompilerParams(vmem_limit_bytes=2 << 20),
        name="settle",
    )(*held)
    return out_v[:, None], out_p[None]


def solution(mesh):
    placed = (
        P(None, "ta", "gx", "gy", None),
        P("ta", "gx", "gy", None),
        P(None, "ta", "gx", "gy", None),
        P("ta", "gx", "gy", None),
        P(None, "gx", "gy", None),
    )
    counts = tuple(mesh.shape[axis] for axis in ("ta", "gx", "gy"))
    return jax.shard_map(
        functools.partial(body, counts),
        mesh=mesh,
        in_specs=placed,
        out_specs=(P(None, "ta", "gx", "gy", None), P("ta", "gx", "gy", None)),
        check_vma=False,
    )
```

```python
import functools

import jax
import jax.numpy as jnp
from jax import lax
from jax.experimental import pallas as pl
from jax.experimental.pallas import tpu as pltpu
from jax.sharding import PartitionSpec as P

relax_factor = 1.5
damping = 0.8
MESH = pl.DeviceIdType.MESH


def loop(lo, hi, body):
    def step(i, carry):
        body(i)
        return carry

    if hi > lo:
        lax.fori_loop(lo, hi, step, 0, unroll=hi - lo)


def row_index(f):
    return lax.broadcasted_iota(jnp.int32, f.shape, 0)


def y_next(f, row):
    n = f.shape[0]
    return jnp.where(row_index(f) == n - 1, row, pltpu.roll(f, n - 1, 0))


def y_last(f, row):
    return jnp.where(row_index(f) == 0, row, pltpu.roll(f, 1, 0))


def z_next(f):
    return pltpu.roll(f, f.shape[1] - 1, 1)


def z_last(f):
    return pltpu.roll(f, 1, 1)


def coeff_of(nu):
    return 1.0 / (relax_factor * (1.0 + 6.0 * nu))


def groups_of(lo, hi, size):
    return [(a, min(a + size, hi)) for a in range(lo, hi, size)]


def first_change(scale, source, w0, w0_last, w1, row, w2):
    div = (w0 - w0_last) + (w1 - y_last(w1, row)) + (w2 - z_last(w2))
    return scale * (source - div)


def second_change(scale, here, x_above, x_below, above, row, c0, c0_last, c1, c1_row, c2):
    g0, g0_last = c0 * (x_above - here), c0_last * (here - x_below)
    g1 = c1 * (y_next(here, above) - here)
    g2 = c2 * (z_next(here) - here)
    div = (g0 - g0_last) + (g1 - y_last(g1, c1_row * (here[0:1] - row))) + (g2 - z_last(g2))
    return 2.0 * here + scale * div


def final_velocity(w, c, here, x_above, above):
    return (
        w[0] - c[0] * (x_above - here),
        w[1] - c[1] * (y_next(here, above) - here),
        w[2] - c[2] * (z_next(here) - here),
    )


def kernel(
    slabs, nx_parts, ny_parts, groups, detour,
    vel, prs, frc, src, vis,
    OV, OP, rL, W, C, c1, c2, c2e, SC, S, Pr, up_r, Ch,
    V, F, Nu, sE, rE, sI, rI, rR, yu_s, yd_s, yu_r, yd_r, Ce, m_s, fe_s, fe_r, up_s, dn_s, dn_r, Se, tally,
    load_sem, send_sem, recv_sem,
):
    _, nx, ny, nz = vel.shape
    parts = (ny - 4) // 4
    final = len(groups) - 1
    ta, gx, gy = lax.axis_index("ta"), lax.axis_index("gx"), lax.axis_index("gy")
    t_next, t_prev = lax.rem(ta + 1, slabs), lax.rem(ta + slabs - 1, slabs)
    has_next, has_prev = ta < slabs - 1, ta > 0
    xu, xd = lax.rem(gx + 1, nx_parts), lax.rem(gx + nx_parts - 1, nx_parts)
    yu, yd = lax.rem(gy + 1, ny_parts), lax.rem(gy + ny_parts - 1, ny_parts)
    first_row = gy == 0

    barrier = pltpu.get_barrier_semaphore()

    def greet(axis, index):
        pl.semaphore_signal(barrier, inc=1, device_id={axis: index}, device_id_type=MESH)

    @pl.when(has_prev)
    def _():
        greet("ta", t_prev)

    expected = 2 + has_next.astype(jnp.int32) + jnp.where(first_row, 0, 2)
    if detour:
        giver, via, taker, lane = detour

        @pl.when(ta == via)
        def _():
            greet("ta", giver)

        @pl.when(ta == taker)
        def _():
            greet("ta", via)

        expected = expected + ((ta == giver) | (ta == via)).astype(jnp.int32)

    def fetch(source, target, k):
        pltpu.make_async_copy(source, target, load_sem.at[k]).start()

    def wait_rows(sem, count):
        size = pl.ds(0, count)
        pltpu.make_async_copy(tally.at[size], tally.at[size], sem).wait()

    half = nx // 2
    for a, n in ((0, half), (half, nx - half)):
        for c in range(3):
            fetch(vel.at[c, pl.ds(a, n)], V.at[c, pl.ds(1 + a, n)], 0)
    for c in range(3):
        fetch(vis.at[c], Nu.at[c, pl.ds(1, nx)], 1)
    fetch(prs, Pr.at[pl.ds(0, nx)], 1)
    for c in range(3):
        fetch(frc.at[c], F.at[c], 2)
    fetch(src, S, 2)

    greet("gx", xu)
    greet("gx", xd)
    for beside in (yu, yd):

        @pl.when(jnp.logical_not(first_row) & (beside != 0))
        def _():
            greet("gy", beside)

    def remote(send, recv, source, target, axis, index):
        return pltpu.make_async_remote_copy(
            src_ref=source, dst_ref=target, send_sem=send_sem.at[send], recv_sem=recv_sem.at[recv],
            device_id={axis: index}, device_id_type=MESH,
        )

    vx_up = remote(0, 0, V.at[:, nx], V.at[:, 0], "gx", xu)
    vx_dn = remote(0, 0, V.at[:, 1], V.at[:, nx + 1], "gx", xd)
    px_dn = remote(0, 0, Pr.at[0], Pr.at[nx], "gx", xd)
    nx_up = remote(0, 0, Nu.at[0, nx], Nu.at[0, 0], "gx", xu)
    three, fourth = pl.ds(0, 3), pl.ds(3, 1)
    ry_up = remote(0, final + 9, yu_s.at[three], yu_r.at[three], "gy", yu)
    ry_dn = remote(0, final + 9, yd_s.at[three], yd_r.at[three], "gy", yd)
    rz_up = remote(0, final + 9, yu_s.at[fourth], yu_r.at[fourth], "gy", yu)
    rz_dn = remote(0, final + 9, yd_s.at[fourth], yd_r.at[fourth], "gy", yd)
    fe_up = remote(0, 1, fe_s, fe_r, "gx", xu)
    fx_up = remote(0, 3, W.at[0, nx], W.at[0, 0], "gx", xu)
    cx_dn = remote(0, 4, c1.at[1], c1.at[nx + 1], "gx", xd)
    cx_up = remote(0, 4, c1.at[nx], c1.at[0], "gx", xu)
    m_dn = remote(0, 2, m_s, Ce.at[:, pl.ds(1, nx)], "gy", yd)
    ce_up = remote(3, 5, Ce.at[0, nx], Ce.at[0, 0], "gx", xu)
    y_up = remote(0, 3, up_s, up_r, "gy", yu)
    y_dn = remote(0, 3, dn_s, dn_r, "gy", yd)
    ex_dn = remote(0, 6, c2.at[0], c2.at[nx], "gx", xd)
    edge = remote(1, 7, sE, rE, "ta", t_next)
    landing = [rI.at[pl.ds(a, b - a), pl.ds(p, q - p)] for a, b, p, q in groups[:final]] + [rL]
    leaving = [sI.at[pl.ds(a, b - a), pl.ds(p, q - p)] for a, b, p, q in groups]
    pieces = [remote(1, 8 + k, leaving[k], landing[k], "ta", t_next) for k in range(final + 1)]
    if detour:
        to_via = remote(1, 10 + final, leaving[lane], rR, "ta", via)
        from_via = remote(2, 8 + lane, rR, landing[lane], "ta", taker)

    def pack_edges(x):
        for c in range(3):
            sE[c, x, 0:2] = V[c, x + 1, 0:2]
            sE[c, x, 2:4] = V[c, x + 1, ny - 2 : ny]

    def pack_rows(x):
        for c in range(3):
            yu_s[c, x] = V[c, x + 1, ny - 1 : ny]
            yd_s[c, x] = V[c, x + 1, 0:1]

    def pack_more(x):
        yu_s[3, x] = Nu[1, x + 1, ny - 1 : ny]
        yd_s[3, x] = Pr[x, 0:1]

    def pack_inner(x):
        for c in range(3):
            for p in range(parts):
                sI[x, p, c] = V[c, x + 1, 2 + 4 * p : 6 + 4 * p]

    wait_rows(load_sem.at[0], 3 * nx * ny)
    loop(0, nx, pack_edges)
    pl.semaphore_wait(barrier, expected)

    @pl.when(has_next)
    def _():
        edge.start()

    for beside in (yu, yd):

        @pl.when(first_row | (beside == 0))
        def _():
            greet("gy", beside)

    loop(0, nx, pack_rows)
    for copy in (vx_up, vx_dn):
        copy.start()

    @pl.when(jnp.logical_not(first_row))
    def _():
        ry_up.start()
        ry_dn.start()

    wait_rows(load_sem.at[1], 4 * nx * ny)
    loop(0, nx, pack_more)
    for copy in (px_dn, nx_up):
        copy.start()

    @pl.when(jnp.logical_not(first_row))
    def _():
        rz_up.start()
        rz_dn.start()

    loop(0, nx, pack_inner)

    @pl.when(has_next)
    def _():
        for k, copy in enumerate(pieces):
            if detour and k == lane:

                @pl.when(ta == giver)
                def _():
                    to_via.start()

                @pl.when(ta != giver)
                def _():
                    copy.start()

            else:
                copy.start()

    @pl.when(first_row)
    def _():
        pl.semaphore_wait(barrier, 2)
        for copy in (ry_up, ry_dn, rz_up, rz_dn):
            copy.start()

    wait_rows(load_sem.at[2], 4 * nx * ny)
    wait_rows(recv_sem.at[0], 8 * ny)
    C[0, 0] = coeff_of(Nu[0, 0])

    def prepare(x):
        e = x + 1
        none = jnp.zeros((1, nz), jnp.float32)
        coeff = [coeff_of(Nu[c, e]) for c in range(3)]
        for c in range(3):
            C[c, e] = coeff[c]
            m_s[c, x] = coeff[c][0:1]
        total = coeff[0] + C[0, x] + coeff[1] + y_last(coeff[1], none) + coeff[2] + z_last(coeff[2])
        SC[x] = damping / total
        m_s[3, x] = total[0:1]
        press = Pr[x]
        grads = (Pr[x + 1] - press, y_next(press, none) - press, z_next(press) - press)
        for c in range(3):
            v = V[c, e]
            near = V[c, e - 1] + V[c, e + 1] + y_last(v, none) + y_next(v, none)
            near = near + z_last(v) + z_next(v)
            momentum = F[c, x] - (v + Nu[c, e] * (6.0 * v - near)) - grads[c]
            W[c, e] = v + coeff[c] * momentum

    def complete(x):
        e, t = x + 1, ny - 1
        below = coeff_of(yu_r[3, x])
        Ch[x] = below
        SC[x, 0:1] = damping / (m_s[3, x] + below)
        for c in range(3):
            W[c, e, 0:1] = W[c, e, 0:1] + C[c, e, 0:1] * (Nu[c, e, 0:1] * yu_r[c, x])
            more = Nu[c, e, t:ny] * yd_r[c, x]
            if c == 1:
                more = more - yd_r[3, x]
            W[c, e, t:ny] = W[c, e, t:ny] + C[c, e, t:ny] * more

    loop(0, nx, prepare)
    m_dn.start()
    wait_rows(recv_sem.at[final + 9], 8 * nx)
    loop(0, nx, complete)
    if detour:

        @pl.when(ta == via)
        def _():
            to_via.wait_recv()
            from_via.start()

    def add_edges(x):
        for c in range(3):
            for s, t in ((0, 0), (2, ny - 2)):
                W[c, x + 1, t : t + 2] = (
                    W[c, x + 1, t : t + 2] + C[c, x + 1, t : t + 2] * rE[c, x, s : s + 2]
                )

    def add_inner(x, first_part, parts_end):
        for c in range(3):
            for p in range(first_part, parts_end):
                t = 2 + 4 * p
                W[c, x + 1, t : t + 4] = W[c, x + 1, t : t + 4] + C[c, x + 1, t : t + 4] * rI[x, p, c]

    def arrive(k):
        @pl.when(has_prev)
        def _():
            pieces[k].wait_recv()
            a, b, p, q = groups[k]
            loop(a, b, lambda x: add_inner(x, p, q))

    @pl.when(has_prev)
    def _():
        edge.wait_recv()
        loop(0, nx, add_edges)

    fe_s[...] = W[0, nx]
    fe_up.start()
    fe_up.wait_recv()

    def edge_rows(x, w0_last):
        e = x + 1
        zero = jnp.zeros((1, nz), jnp.float32)
        change = first_change(SC[x], S[x], W[0, e], w0_last, W[1, e], zero, W[2, e])
        up_s[0, x] = W[1, e, ny - 1 : ny]
        up_s[1, x] = change[ny - 1 : ny]
        dn_s[0, x] = change[0:1]
        dn_s[1, x] = change[1:2]

    edge_rows(0, fe_r[...])
    loop(1, nx, lambda x: edge_rows(x, W[0, x]))
    y_up.start()
    y_dn.start()

    arrive(0)
    arrive(1)
    fx_up.start()
    m_dn.wait_recv()
    ce_up.start()
    wait_rows(recv_sem.at[3], ny + 4 * nx)

    def first(x):
        e = x + 1
        c1[e, 0:ny] = first_change(SC[x], S[x], W[0, e], W[0, x], W[1, e], up_r[0, x], W[2, e])

    def first_above(x):
        e = x + 1
        scale = damping / (Ce[3, e] + C[1, e, ny - 1 : ny])
        Se[x] = scale
        c1[e, ny : ny + 1] = dn_r[0, x] + scale * W[1, e, ny - 1 : ny]

    for x in (0, nx - 1):
        first(x)
        first_above(x)
    for copy in (cx_dn, cx_up):
        copy.start()
    loop(1, nx - 1, first)
    loop(1, nx - 1, first_above)
    wait_rows(recv_sem.at[4], 2 * (ny + 8))
    ce_up.wait_recv()

    def second(x):
        e = x + 1
        c2[x] = second_change(
            SC[x], c1[e, 0:ny], c1[e + 1, 0:ny], c1[e - 1, 0:ny], c1[e, ny : ny + 1], up_r[1, x],
            C[0, e], C[0, x], C[1, e], Ch[x], C[2, e],
        )

    def second_above(x):
        e = x + 1
        wide = lambda row: jnp.broadcast_to(row, (8, nz))
        here = wide(c1[e, ny : ny + 1])
        g0 = wide(Ce[0, e]) * (wide(c1[e + 1, ny : ny + 1]) - here)
        g0_last = wide(Ce[0, x]) * (here - wide(c1[e - 1, ny : ny + 1]))
        g1 = wide(Ce[1, e]) * (wide(dn_r[1, x]) - here)
        g1_last = wide(C[1, e, ny - 1 : ny]) * (here - wide(c1[e, ny - 1 : ny]))
        g2 = wide(Ce[2, e]) * (z_next(here) - here)
        div = (g0 - g0_last) + (g1 - g1_last) + (g2 - z_last(g2))
        c2e[x] = (2.0 * here + wide(Se[x]) * div)[0:1]

    second(0)
    ex_dn.start()
    loop(0, nx, second_above)

    def finish(x):
        e = x + 1
        here = c2[x]
        OP[x] = Pr[x] + here
        moved = final_velocity(
            [W[c, e] for c in range(3)], [C[c, e] for c in range(3)], here, c2[x + 1], c2e[x]
        )
        for c in range(3):
            OV[c, x] = moved[c]

    def finish_low(x):
        e, low = x + 1, slice(0, ny - 8)
        here = c2[x, low]
        OP[x, low] = Pr[x, low] + here
        moved = final_velocity(
            [W[c, e, low] for c in range(3)], [C[c, e, low] for c in range(3)], here, c2[x + 1, low],
            c2[x, ny - 8 : ny - 7],
        )
        for c in range(3):
            OV[c, x, low] = moved[c]

    for k in range(2, final - 1):
        a, b, _, _ = groups[k]
        arrive(k)
        loop(a, b, first)
        loop(a - 1, b - 1, second)
        loop(a - 2, b - 2, finish)

    @pl.when(jnp.logical_not(has_prev))
    def _():
        rL[...] = jnp.zeros_like(rL)

    ex_dn.wait_recv()
    a = groups[final][0]
    arrive(final - 1)
    loop(a, nx - 1, first)
    loop(a - 1, nx, second)
    loop(a - 2, nx, finish_low)

    @pl.when(has_prev)
    def _():
        pieces[final].wait_recv()

    @pl.when(has_next)
    def _():
        wait_rows(send_sem.at[1], 3 * nx * ny)

    if detour:

        @pl.when(ta == via)
        def _():
            from_via.wait_send()

    ce_up.wait_send()
    wait_rows(send_sem.at[0], 13 * ny + 16 + 16 * nx)


def settle(
    last, moved, pressed, rL, W, C, c1, c2, c2e, SC, S, Pr, up_r, Ch, out_v, out_p, nV, nP, nW, n1, n2, sem
):
    _, nx, ny, nz = out_v.shape
    a, b = last
    ready, u = a - 2, ny - 8
    done, rest = pl.ds(0, ready), pl.ds(ready, nx - ready)
    low, top = pl.ds(0, u), pl.ds(u, 8)

    for c in range(3):
        pltpu.make_async_copy(moved.at[c, done], out_v.at[c, done], sem.at[0]).start()
        pltpu.make_async_copy(moved.at[c, rest, low], out_v.at[c, rest, low], sem.at[0]).start()
    pltpu.make_async_copy(pressed.at[done], out_p.at[done], sem.at[1]).start()
    pltpu.make_async_copy(pressed.at[rest, low], out_p.at[rest, low], sem.at[1]).start()

    def w(c, x):
        return nW[c, x - a] if a <= x < b else W[c, x + 1, u:ny]

    def change(x):
        return n1[x - a] if a <= x < nx - 1 else c1[x + 1, u:ny]

    def second(x):
        return n2[x - (a - 1)] if a - 1 <= x < nx else c2[x, u:ny]

    @pl.when(lax.axis_index("ta") >= 0)
    def _():
        for x in range(a, b):
            for c in range(3):
                nW[c, x - a] = W[c, x + 1, u:ny]
                nW[c, x - a, 2:6] = W[c, x + 1, u + 2 : u + 6] + C[c, x + 1, u + 2 : u + 6] * rL[x - a, 0, c]
        for x in range(a, nx - 1):
            n1[x - a] = first_change(
                SC[x, u:ny], S[x, u:ny], w(0, x), w(0, x - 1), w(1, x), W[1, x + 1, u - 1 : u], w(2, x)
            )
        for x in range(a - 1, nx):
            e = x + 1
            n2[x - (a - 1)] = second_change(
                SC[x, u:ny], change(x), change(x + 1), change(x - 1), c1[e, ny : ny + 1], c1[e, u - 1 : u],
                C[0, e, u:ny], C[0, x, u:ny], C[1, e, u:ny], C[1, e, u - 1 : u], C[2, e, u:ny],
            )
        for x in range(ready, nx):
            here = second(x)
            nP[x - ready] = Pr[x, u:ny] + here
            fresh = final_velocity(
                [w(c, x) for c in range(3)], [C[c, x + 1, u:ny] for c in range(3)], here, second(x + 1), c2e[x]
            )
            for c in range(3):
                nV[c, x - ready] = fresh[c]
        for c in range(3):
            pltpu.make_async_copy(nV.at[c], out_v.at[c, rest, top], sem.at[0]).start()
        pltpu.make_async_copy(nP, out_p.at[rest, top], sem.at[1]).start()

    pltpu.make_async_copy(moved, out_v, sem.at[0]).wait()
    pltpu.make_async_copy(pressed, out_p, sem.at[1]).wait()


def body(counts, velocity, pressure, forcing, source, viscosity):
    _, steps, nx, ny, nz = velocity.shape
    assert steps == 1 and nx >= 12 and ny >= 16 and ny % 8 == 0
    parts = (ny - 4) // 4
    last = (nx - 4, nx - 2)
    whole = [(0, 2), (nx - 2, nx), (2, 4)] + groups_of(4, nx - 4, 4)
    groups = [(a, b, 0, parts) for a, b in whole] + [(*last, 0, parts - 1), (*last, parts - 1, parts)]
    detour = (1, 3, 2, 2) if counts[0] == 4 else None
    vmem = lambda *shape: pltpu.VMEM(shape, jnp.float32)
    rows = lambda *lead: vmem(*lead, nx, 1, nz)
    any_space = pl.BlockSpec(memory_space=pl.ANY)
    on_chip = pl.BlockSpec(memory_space=pltpu.VMEM)
    kept = (
        vmem(3, nx, ny, nz), vmem(nx, ny, nz), vmem(2, 1, 3, 4, nz),
        vmem(3, nx + 1, ny, nz), vmem(3, nx + 1, ny, nz), vmem(nx + 2, ny + 8, nz), vmem(nx + 1, ny, nz), rows(),
        vmem(nx, ny, nz), vmem(nx, ny, nz), vmem(nx + 1, ny, nz), rows(2), rows(),
    )
    inputs = (velocity[:, 0], pressure[0], forcing[:, 0], source[0], viscosity)
    held = pl.pallas_call(
        functools.partial(kernel, *counts, groups, detour),
        out_shape=kept,
        in_specs=[any_space] * 5,
        out_specs=(on_chip,) * len(kept),
        scratch_shapes=[
            vmem(3, nx + 2, ny, nz), vmem(3, nx, ny, nz), vmem(3, nx + 1, ny, nz),
            vmem(3, nx, 4, nz), vmem(3, nx, 4, nz),
            vmem(nx, parts, 3, 4, nz), vmem(nx, parts, 3, 4, nz), vmem(2, parts, 3, 4, nz),
            rows(4), rows(4), rows(4), rows(4), vmem(4, nx + 1, 1, nz), rows(4),
            vmem(ny, nz), vmem(ny, nz), rows(2), rows(2), rows(2), rows(), vmem(4 * nx * ny, nz),
            pltpu.SemaphoreType.DMA((3,)),
            pltpu.SemaphoreType.DMA((4,)),
            pltpu.SemaphoreType.DMA((10 + len(groups),)),
        ],
        compiler_params=pltpu.CompilerParams(
            collective_id=0, has_side_effects=True, vmem_limit_bytes=40 << 20
        ),
        name="smoother",
    )(*(pltpu.with_memory_space_constraint(a, pltpu.HBM) for a in inputs))
    out_v, out_p = pl.pallas_call(
        functools.partial(settle, last),
        out_shape=(
            jax.ShapeDtypeStruct((3, nx, ny, nz), jnp.float32),
            jax.ShapeDtypeStruct((nx, ny, nz), jnp.float32),
        ),
        in_specs=[on_chip] * len(kept),
        out_specs=(any_space, any_space),
        scratch_shapes=[
            vmem(3, 6, 8, nz), vmem(6, 8, nz), vmem(3, 2, 8, nz), vmem(3, 8, nz), vmem(5, 8, nz),
            pltpu.SemaphoreType.DMA((2,)),
        ],
        compiler_params=pltpu.CompilerParams(vmem_limit_bytes=2 << 20),
        name="settle",
    )(*held)
    return out_v[:, None], out_p[None]


def solution(mesh):
    placed = (
        P(None, "ta", "gx", "gy", None),
        P("ta", "gx", "gy", None),
        P(None, "ta", "gx", "gy", None),
        P("ta", "gx", "gy", None),
        P(None, "gx", "gy", None),
    )
    counts = tuple(mesh.shape[axis] for axis in ("ta", "gx", "gy"))
    return jax.shard_map(
        functools.partial(body, counts),
        mesh=mesh,
        in_specs=placed,
        out_specs=(P(None, "ta", "gx", "gy", None), P("ta", "gx", "gy", None)),
        check_vma=False,
    )
```

```python
import functools

import jax
import jax.numpy as jnp
from jax import lax
from jax.experimental import pallas as pl
from jax.experimental.pallas import tpu as pltpu
from jax.sharding import PartitionSpec as P

relax_factor = 1.5
damping = 0.8
MESH = pl.DeviceIdType.MESH


def loop(lo, hi, body):
    def step(i, carry):
        body(i)
        return carry

    if hi > lo:
        lax.fori_loop(lo, hi, step, 0, unroll=hi - lo)


def row_index(f):
    return lax.broadcasted_iota(jnp.int32, f.shape, 0)


def y_next(f, row):
    n = f.shape[0]
    return jnp.where(row_index(f) == n - 1, row, pltpu.roll(f, n - 1, 0))


def y_last(f, row):
    return jnp.where(row_index(f) == 0, row, pltpu.roll(f, 1, 0))


def z_next(f):
    return pltpu.roll(f, f.shape[1] - 1, 1)


def z_last(f):
    return pltpu.roll(f, 1, 1)


def coeff_of(nu):
    return 1.0 / (relax_factor * (1.0 + 6.0 * nu))


def groups_of(lo, hi, size):
    return [(a, min(a + size, hi)) for a in range(lo, hi, size)]


def first_change(scale, source, w0, w0_last, w1, row, w2):
    div = (w0 - w0_last) + (w1 - y_last(w1, row)) + (w2 - z_last(w2))
    return scale * (source - div)


def second_change(scale, here, x_above, x_below, above, row, c0, c0_last, c1, c1_row, c2):
    g0, g0_last = c0 * (x_above - here), c0_last * (here - x_below)
    g1 = c1 * (y_next(here, above) - here)
    g2 = c2 * (z_next(here) - here)
    div = (g0 - g0_last) + (g1 - y_last(g1, c1_row * (here[0:1] - row))) + (g2 - z_last(g2))
    return 2.0 * here + scale * div


def final_velocity(w, c, here, x_above, above):
    return (
        w[0] - c[0] * (x_above - here),
        w[1] - c[1] * (y_next(here, above) - here),
        w[2] - c[2] * (z_next(here) - here),
    )


def kernel(
    slabs, nx_parts, ny_parts, groups, detour,
    vel, prs, frc, src, vis,
    OV, OP, rL, W, C, c1, c2, c2e, SC, S, Pr, up_r, Ch,
    V, F, Nu, sE, rE, sI, rI, rR, yu_s, yd_s, yu_r, yd_r, Ce, m_s, fe_s, fe_r, up_s, dn_s, dn_r, Se, tally,
    load_sem, send_sem, recv_sem,
):
    _, nx, ny, nz = vel.shape
    parts = (ny - 4) // 4
    final = len(groups) - 1
    ta, gx, gy = lax.axis_index("ta"), lax.axis_index("gx"), lax.axis_index("gy")
    t_next, t_prev = lax.rem(ta + 1, slabs), lax.rem(ta + slabs - 1, slabs)
    has_next, has_prev = ta < slabs - 1, ta > 0
    xu, xd = lax.rem(gx + 1, nx_parts), lax.rem(gx + nx_parts - 1, nx_parts)
    yu, yd = lax.rem(gy + 1, ny_parts), lax.rem(gy + ny_parts - 1, ny_parts)
    first_row = gy == 0

    barrier = pltpu.get_barrier_semaphore()

    def greet(axis, index):
        pl.semaphore_signal(barrier, inc=1, device_id={axis: index}, device_id_type=MESH)

    @pl.when(has_prev)
    def _():
        greet("ta", t_prev)

    expected = 2 + has_next.astype(jnp.int32) + jnp.where(first_row, 0, 2)
    if detour:
        giver, via, taker, lane = detour

        @pl.when(ta == via)
        def _():
            greet("ta", giver)

        @pl.when(ta == taker)
        def _():
            greet("ta", via)

        expected = expected + ((ta == giver) | (ta == via)).astype(jnp.int32)

    def fetch(source, target, k):
        pltpu.make_async_copy(source, target, load_sem.at[k]).start()

    def wait_rows(sem, count):
        size = pl.ds(0, count)
        pltpu.make_async_copy(tally.at[size], tally.at[size], sem).wait()

    half = nx // 2
    for a, n in ((0, half), (half, nx - half)):
        for c in range(3):
            fetch(vel.at[c, pl.ds(a, n)], V.at[c, pl.ds(1 + a, n)], 0)
    greet("gx", xu)
    greet("gx", xd)
    for beside in (yu, yd):

        @pl.when(jnp.logical_not(first_row) & (beside != 0))
        def _():
            greet("gy", beside)

    def remote(send, recv, source, target, axis, index):
        return pltpu.make_async_remote_copy(
            src_ref=source, dst_ref=target, send_sem=send_sem.at[send], recv_sem=recv_sem.at[recv],
            device_id={axis: index}, device_id_type=MESH,
        )

    vx_up = remote(0, 0, V.at[:, nx], V.at[:, 0], "gx", xu)
    vx_dn = remote(0, 0, V.at[:, 1], V.at[:, nx + 1], "gx", xd)
    px_dn = remote(0, 0, Pr.at[0], Pr.at[nx], "gx", xd)
    nx_up = remote(0, 0, Nu.at[0, nx], Nu.at[0, 0], "gx", xu)
    three, fourth = pl.ds(0, 3), pl.ds(3, 1)
    ry_up = remote(0, 6, yu_s.at[three], yu_r.at[three], "gy", yu)
    ry_dn = remote(0, 6, yd_s.at[three], yd_r.at[three], "gy", yd)
    rz_up = remote(0, 6, yu_s.at[fourth], yu_r.at[fourth], "gy", yu)
    rz_dn = remote(0, 6, yd_s.at[fourth], yd_r.at[fourth], "gy", yd)
    fe_up = remote(0, 1, fe_s, fe_r, "gx", xu)
    fx_up = remote(0, 2, W.at[0, nx], W.at[0, 0], "gx", xu)
    cx_dn = remote(0, 3, c1.at[1], c1.at[nx + 1], "gx", xd)
    cx_up = remote(0, 3, c1.at[nx], c1.at[0], "gx", xu)
    m_dn = remote(0, 2, m_s, Ce, "gy", yd)
    y_up = remote(0, 2, up_s, up_r, "gy", yu)
    y_dn = remote(0, 2, dn_s, dn_r, "gy", yd)
    ex_dn = remote(0, 4, c2.at[0], c2.at[nx], "gx", xd)
    edge = remote(1, 5, sE, rE, "ta", t_next)
    landing = [rI.at[pl.ds(a, b - a), pl.ds(p, q - p)] for a, b, p, q in groups[:final]] + [rL]
    leaving = [sI.at[pl.ds(a, b - a), pl.ds(p, q - p)] for a, b, p, q in groups]
    pieces = [remote(1, 7 + max(k, 1), leaving[k], landing[k], "ta", t_next) for k in range(final + 1)]
    if detour:
        to_via = remote(1, 7, leaving[lane], rR, "ta", via)
        from_via = remote(1, 7 + lane, rR, landing[lane], "ta", taker)

    def pack_edges(x):
        for c in range(3):
            sE[c, x, 0:2] = V[c, x + 1, 0:2]
            sE[c, x, 2:4] = V[c, x + 1, ny - 2 : ny]

    def pack_rows(x):
        for c in range(3):
            yu_s[c, x] = V[c, x + 1, ny - 1 : ny]
            yd_s[c, x] = V[c, x + 1, 0:1]

    def pack_more(x):
        yu_s[3, x] = Nu[1, x + 1, ny - 1 : ny]
        yd_s[3, x] = Pr[x, 0:1]

    def pack_inner(x):
        for c in range(3):
            for p in range(parts):
                sI[x, p, c] = V[c, x + 1, 2 + 4 * p : 6 + 4 * p]

    wait_rows(load_sem.at[0], 3 * nx * ny)
    for c in range(3):
        fetch(vis.at[c], Nu.at[c, pl.ds(1, nx)], 1)
    fetch(prs, Pr.at[pl.ds(0, nx)], 1)
    for c in range(3):
        fetch(frc.at[c], F.at[c], 2)
    fetch(src, S, 2)
    loop(0, nx, pack_edges)
    pl.semaphore_wait(barrier, expected)

    @pl.when(has_next)
    def _():
        edge.start()

    for beside in (yu, yd):

        @pl.when(first_row | (beside == 0))
        def _():
            greet("gy", beside)

    loop(0, nx, pack_rows)
    for copy in (vx_up, vx_dn):
        copy.start()

    @pl.when(jnp.logical_not(first_row))
    def _():
        ry_up.start()
        ry_dn.start()

    wait_rows(load_sem.at[1], 4 * nx * ny)
    loop(0, nx, pack_more)
    for copy in (px_dn, nx_up):
        copy.start()

    @pl.when(jnp.logical_not(first_row))
    def _():
        rz_up.start()
        rz_dn.start()

    loop(0, nx, pack_inner)

    pauses = first_row & (ta == 0) & (lax.rem(gx, 2) == 1)
    outer_rows = 12 * nx + 48 * parts

    def send_inner():
        for k in range(2, final + 1):
            if detour and k == lane:

                @pl.when(ta == giver)
                def _():
                    to_via.start()

                @pl.when(ta != giver)
                def _():
                    pieces[k].start()

            else:
                pieces[k].start()

    @pl.when(has_next)
    def _():
        pieces[0].start()
        pieces[1].start()

    @pl.when(has_next & jnp.logical_not(pauses))
    def _():
        send_inner()

    @pl.when(first_row)
    def _():
        pl.semaphore_wait(barrier, 2)
        for copy in (ry_up, ry_dn, rz_up, rz_dn):
            copy.start()

    wait_rows(load_sem.at[2], 4 * nx * ny)
    wait_rows(recv_sem.at[0], 8 * ny)
    C[0, 0] = coeff_of(Nu[0, 0])

    def prepare(x):
        e = x + 1
        none = jnp.zeros((1, nz), jnp.float32)
        coeff = [coeff_of(Nu[c, e]) for c in range(3)]
        for c in range(3):
            C[c, e] = coeff[c]
            m_s[c, x] = coeff[c][0:1]
        total = coeff[0] + C[0, x] + coeff[1] + y_last(coeff[1], none) + coeff[2] + z_last(coeff[2])
        SC[x] = damping / total
        m_s[3, x] = total[0:1]
        press = Pr[x]
        grads = (Pr[x + 1] - press, y_next(press, none) - press, z_next(press) - press)
        for c in range(3):
            v = V[c, e]
            near = V[c, e - 1] + V[c, e + 1] + y_last(v, none) + y_next(v, none)
            near = near + z_last(v) + z_next(v)
            momentum = F[c, x] - (v + Nu[c, e] * (6.0 * v - near)) - grads[c]
            W[c, e] = v + coeff[c] * momentum

    def complete(x):
        e, t = x + 1, ny - 1
        below = coeff_of(yu_r[3, x])
        Ch[x] = below
        SC[x, 0:1] = damping / (m_s[3, x] + below)
        for c in range(3):
            W[c, e, 0:1] = W[c, e, 0:1] + C[c, e, 0:1] * (Nu[c, e, 0:1] * yu_r[c, x])
            more = Nu[c, e, t:ny] * yd_r[c, x]
            if c == 1:
                more = more - yd_r[3, x]
            W[c, e, t:ny] = W[c, e, t:ny] + C[c, e, t:ny] * more

    loop(0, nx, prepare)
    m_dn.start()
    wait_rows(recv_sem.at[6], 8 * nx)
    loop(0, nx, complete)
    if detour:

        @pl.when(ta == via)
        def _():
            to_via.wait_recv()
            from_via.start()

    def add_edges(x):
        for c in range(3):
            for s, t in ((0, 0), (2, ny - 2)):
                W[c, x + 1, t : t + 2] = (
                    W[c, x + 1, t : t + 2] + C[c, x + 1, t : t + 2] * rE[c, x, s : s + 2]
                )

    def add_inner(x, first_part, parts_end):
        for c in range(3):
            for p in range(first_part, parts_end):
                t = 2 + 4 * p
                W[c, x + 1, t : t + 4] = W[c, x + 1, t : t + 4] + C[c, x + 1, t : t + 4] * rI[x, p, c]

    @pl.when(has_prev)
    def _():
        edge.wait_recv()
        loop(0, nx, add_edges)

    def arrive(k):
        @pl.when(has_prev)
        def _():
            pieces[k].wait_recv()
            a, b, p, q = groups[k]
            loop(a, b, lambda x: add_inner(x, p, q))

    fe_s[...] = W[0, nx]
    fe_up.start()
    fe_up.wait_recv()

    def edge_rows(x, w0_last):
        e = x + 1
        zero = jnp.zeros((1, nz), jnp.float32)
        change = first_change(SC[x], S[x], W[0, e], w0_last, W[1, e], zero, W[2, e])
        up_s[0, x] = W[1, e, ny - 1 : ny]
        up_s[1, x] = change[ny - 1 : ny]
        dn_s[0, x] = change[0:1]
        dn_s[1, x] = change[1:2]

    edge_rows(0, fe_r[...])
    loop(1, nx, lambda x: edge_rows(x, W[0, x]))
    y_up.start()
    y_dn.start()

    @pl.when(has_next & pauses)
    def _():
        wait_rows(send_sem.at[1], outer_rows)
        send_inner()

    @pl.when(has_prev)
    def _():
        wait_rows(recv_sem.at[8], 48 * parts)
        for a in (0, nx - 2):
            loop(a, a + 2, lambda x: add_inner(x, 0, parts))

    fx_up.start()
    wait_rows(recv_sem.at[2], ny + 8 * nx)

    def first(x):
        e = x + 1
        c1[e, 0:ny] = first_change(SC[x], S[x], W[0, e], W[0, x], W[1, e], up_r[0, x], W[2, e])

    def first_above(x):
        e = x + 1
        scale = damping / (Ce[3, x] + C[1, e, ny - 1 : ny])
        Se[x] = scale
        c1[e, ny : ny + 1] = dn_r[0, x] + scale * W[1, e, ny - 1 : ny]

    for x in (0, nx - 1):
        first(x)
        first_above(x)
    c1[nx, ny + 1 : ny + 2] = Ce[0, nx - 1]
    for copy in (cx_dn, cx_up):
        copy.start()
    loop(1, nx - 1, first)
    loop(1, nx - 1, first_above)
    wait_rows(recv_sem.at[3], 2 * (ny + 8))

    def second(x):
        e = x + 1
        c2[x] = second_change(
            SC[x], c1[e, 0:ny], c1[e + 1, 0:ny], c1[e - 1, 0:ny], c1[e, ny : ny + 1], up_r[1, x],
            C[0, e], C[0, x], C[1, e], Ch[x], C[2, e],
        )

    def second_above(x, c0_last):
        e = x + 1
        wide = lambda row: jnp.broadcast_to(row, (8, nz))
        here = wide(c1[e, ny : ny + 1])
        g0 = wide(Ce[0, x]) * (wide(c1[e + 1, ny : ny + 1]) - here)
        g0_last = wide(c0_last) * (here - wide(c1[e - 1, ny : ny + 1]))
        g1 = wide(Ce[1, x]) * (wide(dn_r[1, x]) - here)
        g1_last = wide(C[1, e, ny - 1 : ny]) * (here - wide(c1[e, ny - 1 : ny]))
        g2 = wide(Ce[2, x]) * (z_next(here) - here)
        div = (g0 - g0_last) + (g1 - g1_last) + (g2 - z_last(g2))
        c2e[x] = (2.0 * here + wide(Se[x]) * div)[0:1]

    second(0)
    ex_dn.start()
    second_above(0, c1[0, ny + 1 : ny + 2])
    loop(1, nx, lambda x: second_above(x, Ce[0, x - 1]))

    def finish(x):
        e = x + 1
        here = c2[x]
        OP[x] = Pr[x] + here
        moved = final_velocity(
            [W[c, e] for c in range(3)], [C[c, e] for c in range(3)], here, c2[x + 1], c2e[x]
        )
        for c in range(3):
            OV[c, x] = moved[c]

    def finish_low(x):
        e, low = x + 1, slice(0, ny - 8)
        here = c2[x, low]
        OP[x, low] = Pr[x, low] + here
        moved = final_velocity(
            [W[c, e, low] for c in range(3)], [C[c, e, low] for c in range(3)], here, c2[x + 1, low],
            c2[x, ny - 8 : ny - 7],
        )
        for c in range(3):
            OV[c, x, low] = moved[c]

    for k in range(2, final - 1):
        a, b, _, _ = groups[k]
        arrive(k)
        loop(a, b, first)
        loop(a - 1, b - 1, second)
        loop(a - 2, b - 2, finish)

    @pl.when(jnp.logical_not(has_prev))
    def _():
        rL[...] = jnp.zeros_like(rL)

    ex_dn.wait_recv()
    a = groups[final][0]
    arrive(final - 1)
    loop(a, nx - 1, first)
    loop(a - 1, nx, second)
    loop(a - 2, nx, finish_low)

    @pl.when(has_prev)
    def _():
        pieces[final].wait_recv()

    @pl.when(has_next & jnp.logical_not(pauses))
    def _():
        wait_rows(send_sem.at[1], 3 * nx * ny)

    @pl.when(has_next & pauses)
    def _():
        wait_rows(send_sem.at[1], 3 * nx * ny - outer_rows)

    if detour:

        @pl.when(ta == via)
        def _():
            wait_rows(send_sem.at[1], 24 * parts)

    wait_rows(send_sem.at[0], 13 * ny + 16 + 16 * nx)


def settle(
    last, moved, pressed, rL, W, C, c1, c2, c2e, SC, S, Pr, up_r, Ch, step_v, step_p, nV, nP, nW, n1, n2, sem
):
    out_v, out_p = step_v.at[:, 0], step_p.at[0]
    _, nx, ny, nz = moved.shape
    a, b = last
    ready, u = a - 2, ny - 8
    done, rest = pl.ds(0, ready), pl.ds(ready, nx - ready)
    low, top = pl.ds(0, u), pl.ds(u, 8)

    for c in range(3):
        pltpu.make_async_copy(moved.at[c, done], out_v.at[c, done], sem.at[0]).start()
        pltpu.make_async_copy(moved.at[c, rest, low], out_v.at[c, rest, low], sem.at[0]).start()
    pltpu.make_async_copy(pressed.at[done], out_p.at[done], sem.at[1]).start()
    pltpu.make_async_copy(pressed.at[rest, low], out_p.at[rest, low], sem.at[1]).start()

    def w(c, x):
        return nW[c, x - a] if a <= x < b else W[c, x + 1, u:ny]

    def change(x):
        return n1[x - a] if a <= x < nx - 1 else c1[x + 1, u:ny]

    def second(x):
        return n2[x - (a - 1)] if a - 1 <= x < nx else c2[x, u:ny]

    @pl.when(lax.axis_index("ta") >= 0)
    def _():
        for x in range(a, b):
            for c in range(3):
                nW[c, x - a] = W[c, x + 1, u:ny]
                nW[c, x - a, 2:6] = W[c, x + 1, u + 2 : u + 6] + C[c, x + 1, u + 2 : u + 6] * rL[x - a, 0, c]
        for x in range(a, nx - 1):
            n1[x - a] = first_change(
                SC[x, u:ny], S[x, u:ny], w(0, x), w(0, x - 1), w(1, x), W[1, x + 1, u - 1 : u], w(2, x)
            )
        for x in range(a - 1, nx):
            e = x + 1
            n2[x - (a - 1)] = second_change(
                SC[x, u:ny], change(x), change(x + 1), change(x - 1), c1[e, ny : ny + 1], c1[e, u - 1 : u],
                C[0, e, u:ny], C[0, x, u:ny], C[1, e, u:ny], C[1, e, u - 1 : u], C[2, e, u:ny],
            )
        for x in range(ready, nx):
            here = second(x)
            nP[x - ready] = Pr[x, u:ny] + here
            fresh = final_velocity(
                [w(c, x) for c in range(3)], [C[c, x + 1, u:ny] for c in range(3)], here, second(x + 1), c2e[x]
            )
            for c in range(3):
                nV[c, x - ready] = fresh[c]
        for c in range(3):
            pltpu.make_async_copy(nV.at[c], out_v.at[c, rest, top], sem.at[0]).start()
        pltpu.make_async_copy(nP, out_p.at[rest, top], sem.at[1]).start()

    pltpu.make_async_copy(moved, out_v, sem.at[0]).wait()
    pltpu.make_async_copy(pressed, out_p, sem.at[1]).wait()


def body(counts, velocity, pressure, forcing, source, viscosity):
    _, steps, nx, ny, nz = velocity.shape
    assert steps == 1 and nx >= 12 and ny >= 16 and ny % 8 == 0
    parts = (ny - 4) // 4
    last = (nx - 4, nx - 2)
    whole = [(0, 2), (nx - 2, nx), (2, 4)] + groups_of(4, nx - 4, 4)
    groups = [(a, b, 0, parts) for a, b in whole] + [(*last, 0, parts - 1), (*last, parts - 1, parts)]
    detour = (1, 3, 2, 2) if counts[0] == 4 else None
    vmem = lambda *shape: pltpu.VMEM(shape, jnp.float32)
    rows = lambda *lead: vmem(*lead, nx, 1, nz)
    any_space = pl.BlockSpec(memory_space=pl.ANY)
    on_chip = pl.BlockSpec(memory_space=pltpu.VMEM)
    kept = (
        vmem(3, nx, ny, nz), vmem(nx, ny, nz), vmem(2, 1, 3, 4, nz),
        vmem(3, nx + 1, ny, nz), vmem(3, nx + 1, ny, nz), vmem(nx + 2, ny + 8, nz), vmem(nx + 1, ny, nz), rows(),
        vmem(nx, ny, nz), vmem(nx, ny, nz), vmem(nx + 1, ny, nz), rows(2), rows(),
    )
    inputs = (velocity[:, 0], pressure[0], forcing[:, 0], source[0], viscosity)
    held = pl.pallas_call(
        functools.partial(kernel, *counts, groups, detour),
        out_shape=kept,
        in_specs=[any_space] * 5,
        out_specs=(on_chip,) * len(kept),
        scratch_shapes=[
            vmem(3, nx + 2, ny, nz), vmem(3, nx, ny, nz), vmem(3, nx + 1, ny, nz),
            vmem(3, nx, 4, nz), vmem(3, nx, 4, nz),
            vmem(nx, parts, 3, 4, nz), vmem(nx, parts, 3, 4, nz), vmem(2, parts, 3, 4, nz),
            rows(4), rows(4), rows(4), rows(4), rows(4), rows(4),
            vmem(ny, nz), vmem(ny, nz), rows(2), rows(2), rows(2), rows(), vmem(4 * nx * ny, nz),
            pltpu.SemaphoreType.DMA((3,)),
            pltpu.SemaphoreType.DMA((2,)),
            pltpu.SemaphoreType.DMA((7 + len(groups),)),
        ],
        compiler_params=pltpu.CompilerParams(
            collective_id=0, has_side_effects=True, vmem_limit_bytes=40 << 20
        ),
        name="smoother",
    )(*(pltpu.with_memory_space_constraint(a, pltpu.HBM) for a in inputs))
    return pl.pallas_call(
        functools.partial(settle, last),
        out_shape=(
            jax.ShapeDtypeStruct((3, 1, nx, ny, nz), jnp.float32),
            jax.ShapeDtypeStruct((1, nx, ny, nz), jnp.float32),
        ),
        in_specs=[on_chip] * len(kept),
        out_specs=(any_space, any_space),
        scratch_shapes=[
            vmem(3, 6, 8, nz), vmem(6, 8, nz), vmem(3, 2, 8, nz), vmem(3, 8, nz), vmem(5, 8, nz),
            pltpu.SemaphoreType.DMA((2,)),
        ],
        compiler_params=pltpu.CompilerParams(vmem_limit_bytes=2 << 20),
        name="settle",
    )(*held)


def solution(mesh):
    placed = (
        P(None, "ta", "gx", "gy", None),
        P("ta", "gx", "gy", None),
        P(None, "ta", "gx", "gy", None),
        P("ta", "gx", "gy", None),
        P(None, "gx", "gy", None),
    )
    counts = tuple(mesh.shape[axis] for axis in ("ta", "gx", "gy"))
    return jax.shard_map(
        functools.partial(body, counts),
        mesh=mesh,
        in_specs=placed,
        out_specs=(P(None, "ta", "gx", "gy", None), P("ta", "gx", "gy", None)),
        check_vma=False,
    )
```

```python
import functools

import jax
import jax.numpy as jnp
from jax import lax
from jax.experimental import pallas as pl
from jax.experimental.pallas import tpu as pltpu
from jax.sharding import PartitionSpec as P

relax_factor = 1.5
damping = 0.8
MESH = pl.DeviceIdType.MESH


def loop(lo, hi, body):
    def step(i, carry):
        body(i)
        return carry

    if hi > lo:
        lax.fori_loop(lo, hi, step, 0, unroll=hi - lo)


def row_index(f):
    return lax.broadcasted_iota(jnp.int32, f.shape, 0)


def y_next(f, row):
    n = f.shape[0]
    return jnp.where(row_index(f) == n - 1, row, pltpu.roll(f, n - 1, 0))


def y_last(f, row):
    return jnp.where(row_index(f) == 0, row, pltpu.roll(f, 1, 0))


def z_next(f):
    return pltpu.roll(f, f.shape[1] - 1, 1)


def z_last(f):
    return pltpu.roll(f, 1, 1)


def coeff_of(nu):
    return 1.0 / (relax_factor * (1.0 + 6.0 * nu))


def groups_of(lo, hi, size):
    return [(a, min(a + size, hi)) for a in range(lo, hi, size)]


def first_change(scale, source, w0, w0_last, w1, row, w2):
    div = (w0 - w0_last) + (w1 - y_last(w1, row)) + (w2 - z_last(w2))
    return scale * (source - div)


def second_change(scale, here, x_above, x_below, above, row, c0, c0_last, c1, c1_row, c2):
    g0, g0_last = c0 * (x_above - here), c0_last * (here - x_below)
    g1 = c1 * (y_next(here, above) - here)
    g2 = c2 * (z_next(here) - here)
    div = (g0 - g0_last) + (g1 - y_last(g1, c1_row * (here[0:1] - row))) + (g2 - z_last(g2))
    return 2.0 * here + scale * div


def final_velocity(w, c, here, x_above, above):
    return (
        w[0] - c[0] * (x_above - here),
        w[1] - c[1] * (y_next(here, above) - here),
        w[2] - c[2] * (z_next(here) - here),
    )


def kernel(
    slabs, nx_parts, ny_parts, groups, detour,
    vel, prs, frc, src, vis,
    OV, OP, rL, W, C, c1, c2, c2e, SC, S, Pr, up_r, Ch,
    V, F, Nu, sE, rE, sI, rI, rR, yu_s, yd_s, yu_r, yd_r, Ce, m_s, fe_s, fe_r, up_s, dn_s, dn_r, Se, tally,
    load_sem, send_sem, recv_sem,
):
    _, nx, ny, nz = vel.shape
    parts = (ny - 4) // 4
    final = len(groups) - 1
    ta, gx, gy = lax.axis_index("ta"), lax.axis_index("gx"), lax.axis_index("gy")
    t_next, t_prev = lax.rem(ta + 1, slabs), lax.rem(ta + slabs - 1, slabs)
    has_next, has_prev = ta < slabs - 1, ta > 0
    xu, xd = lax.rem(gx + 1, nx_parts), lax.rem(gx + nx_parts - 1, nx_parts)
    yu, yd = lax.rem(gy + 1, ny_parts), lax.rem(gy + ny_parts - 1, ny_parts)
    first_row = gy == 0

    barrier = pltpu.get_barrier_semaphore()

    def greet(axis, index):
        pl.semaphore_signal(barrier, inc=1, device_id={axis: index}, device_id_type=MESH)

    @pl.when(has_prev)
    def _():
        greet("ta", t_prev)

    expected = 2 + has_next.astype(jnp.int32) + jnp.where(first_row, 0, 2)
    if detour:
        giver, via, taker, lane = detour

        @pl.when(ta == via)
        def _():
            greet("ta", giver)

        @pl.when(ta == taker)
        def _():
            greet("ta", via)

        expected = expected + ((ta == giver) | (ta == via)).astype(jnp.int32)

    def fetch(source, target, k):
        pltpu.make_async_copy(source, target, load_sem.at[k]).start()

    def wait_rows(sem, count):
        size = pl.ds(0, count)
        pltpu.make_async_copy(tally.at[size], tally.at[size], sem).wait()

    half = nx // 2
    for a, n in ((0, half), (half, nx - half)):
        for c in range(3):
            fetch(vel.at[c, pl.ds(a, n)], V.at[c, pl.ds(1 + a, n)], 0)
    greet("gx", xu)
    greet("gx", xd)
    for beside in (yu, yd):

        @pl.when(jnp.logical_not(first_row) & (beside != 0))
        def _():
            greet("gy", beside)

    def remote(send, recv, source, target, axis, index):
        return pltpu.make_async_remote_copy(
            src_ref=source, dst_ref=target, send_sem=send_sem.at[send], recv_sem=recv_sem.at[recv],
            device_id={axis: index}, device_id_type=MESH,
        )

    vx_up = remote(0, 0, V.at[:, nx], V.at[:, 0], "gx", xu)
    vx_dn = remote(0, 0, V.at[:, 1], V.at[:, nx + 1], "gx", xd)
    px_dn = remote(0, 0, Pr.at[0], Pr.at[nx], "gx", xd)
    nx_up = remote(0, 0, Nu.at[0, nx], Nu.at[0, 0], "gx", xu)
    three, fourth = pl.ds(0, 3), pl.ds(3, 1)
    ry_up = remote(0, 6, yu_s.at[three], yu_r.at[three], "gy", yu)
    ry_dn = remote(0, 6, yd_s.at[three], yd_r.at[three], "gy", yd)
    rz_up = remote(0, 6, yu_s.at[fourth], yu_r.at[fourth], "gy", yu)
    rz_dn = remote(0, 6, yd_s.at[fourth], yd_r.at[fourth], "gy", yd)
    fe_up = remote(0, 1, fe_s, fe_r, "gx", xu)
    fx_up = remote(0, 2, W.at[0, nx], W.at[0, 0], "gx", xu)
    cx_dn = remote(0, 3, c1.at[1], c1.at[nx + 1], "gx", xd)
    cx_up = remote(0, 3, c1.at[nx], c1.at[0], "gx", xu)
    m_dn = remote(0, 2, m_s, Ce, "gy", yd)
    y_up = remote(0, 2, up_s, up_r, "gy", yu)
    y_dn = remote(0, 2, dn_s, dn_r, "gy", yd)
    ex_dn = remote(0, 4, c2.at[0], c2.at[nx], "gx", xd)
    edge = remote(1, 5, sE, rE, "ta", t_next)
    landing = [rI.at[pl.ds(a, b - a), pl.ds(p, q - p)] for a, b, p, q in groups[:final]] + [rL]
    leaving = [sI.at[pl.ds(a, b - a), pl.ds(p, q - p)] for a, b, p, q in groups]
    pieces = [remote(1, 7 + max(k, 1), leaving[k], landing[k], "ta", t_next) for k in range(final + 1)]
    if detour:
        to_via = remote(1, 7, leaving[lane], rR, "ta", via)
        from_via = remote(1, 7 + lane, rR, landing[lane], "ta", taker)

    def pack_edges(x):
        for c in range(3):
            sE[c, x, 0:2] = V[c, x + 1, 0:2]
            sE[c, x, 2:4] = V[c, x + 1, ny - 2 : ny]

    def pack_rows(x):
        for c in range(3):
            yu_s[c, x] = V[c, x + 1, ny - 1 : ny]
            yd_s[c, x] = V[c, x + 1, 0:1]

    def pack_more(x):
        yu_s[3, x] = Nu[1, x + 1, ny - 1 : ny]
        yd_s[3, x] = Pr[x, 0:1]

    def pack_inner(x):
        for c in range(3):
            for p in range(parts):
                sI[x, p, c] = V[c, x + 1, 2 + 4 * p : 6 + 4 * p]

    wait_rows(load_sem.at[0], 3 * nx * ny)
    for c in range(3):
        fetch(vis.at[c], Nu.at[c, pl.ds(1, nx)], 1)
    fetch(prs, Pr.at[pl.ds(0, nx)], 1)
    for c in range(3):
        fetch(frc.at[c], F.at[c], 1)
    fetch(src, S, 1)
    loop(0, nx, pack_edges)
    pl.semaphore_wait(barrier, expected)

    @pl.when(has_next)
    def _():
        edge.start()

    for beside in (yu, yd):

        @pl.when(first_row | (beside == 0))
        def _():
            greet("gy", beside)

    loop(0, nx, pack_rows)
    for copy in (vx_up, vx_dn):
        copy.start()

    @pl.when(jnp.logical_not(first_row))
    def _():
        ry_up.start()
        ry_dn.start()

    wait_rows(load_sem.at[1], 8 * nx * ny)
    loop(0, nx, pack_more)
    for copy in (px_dn, nx_up):
        copy.start()

    @pl.when(jnp.logical_not(first_row))
    def _():
        rz_up.start()
        rz_dn.start()

    loop(0, nx, pack_inner)

    pauses = first_row & (ta == 0) & (lax.rem(gx, 2) == 1)
    outer_rows = 12 * nx + 48 * parts

    def send_inner():
        for k in range(2, final + 1):
            if detour and k == lane:

                @pl.when(ta == giver)
                def _():
                    to_via.start()

                @pl.when(ta != giver)
                def _():
                    pieces[k].start()

            else:
                pieces[k].start()

    @pl.when(has_next)
    def _():
        pieces[0].start()
        pieces[1].start()

    @pl.when(has_next & jnp.logical_not(pauses))
    def _():
        send_inner()

    @pl.when(first_row)
    def _():
        pl.semaphore_wait(barrier, 2)
        for copy in (ry_up, ry_dn, rz_up, rz_dn):
            copy.start()

    wait_rows(recv_sem.at[0], 8 * ny)
    C[0, 0] = coeff_of(Nu[0, 0])

    def prepare(x):
        e = x + 1
        none = jnp.zeros((1, nz), jnp.float32)
        coeff = [coeff_of(Nu[c, e]) for c in range(3)]
        for c in range(3):
            C[c, e] = coeff[c]
            m_s[c, x] = coeff[c][0:1]
        total = coeff[0] + C[0, x] + coeff[1] + y_last(coeff[1], none) + coeff[2] + z_last(coeff[2])
        SC[x] = damping / total
        m_s[3, x] = total[0:1]
        press = Pr[x]
        grads = (Pr[x + 1] - press, y_next(press, none) - press, z_next(press) - press)
        for c in range(3):
            v = V[c, e]
            near = V[c, e - 1] + V[c, e + 1] + y_last(v, none) + y_next(v, none)
            near = near + z_last(v) + z_next(v)
            momentum = F[c, x] - (v + Nu[c, e] * (6.0 * v - near)) - grads[c]
            W[c, e] = v + coeff[c] * momentum

    def complete(x):
        e, t = x + 1, ny - 1
        below = coeff_of(yu_r[3, x])
        Ch[x] = below
        SC[x, 0:1] = damping / (m_s[3, x] + below)
        for c in range(3):
            W[c, e, 0:1] = W[c, e, 0:1] + C[c, e, 0:1] * (Nu[c, e, 0:1] * yu_r[c, x])
            more = Nu[c, e, t:ny] * yd_r[c, x]
            if c == 1:
                more = more - yd_r[3, x]
            W[c, e, t:ny] = W[c, e, t:ny] + C[c, e, t:ny] * more

    loop(0, nx, prepare)
    m_dn.start()
    wait_rows(recv_sem.at[6], 8 * nx)
    loop(0, nx, complete)
    if detour:

        @pl.when(ta == via)
        def _():
            to_via.wait_recv()
            from_via.start()

    def add_edges(x):
        for c in range(3):
            for s, t in ((0, 0), (2, ny - 2)):
                W[c, x + 1, t : t + 2] = (
                    W[c, x + 1, t : t + 2] + C[c, x + 1, t : t + 2] * rE[c, x, s : s + 2]
                )

    def add_inner(x, first_part, parts_end):
        for c in range(3):
            for p in range(first_part, parts_end):
                t = 2 + 4 * p
                W[c, x + 1, t : t + 4] = W[c, x + 1, t : t + 4] + C[c, x + 1, t : t + 4] * rI[x, p, c]

    @pl.when(has_prev)
    def _():
        edge.wait_recv()
        loop(0, nx, add_edges)

    def arrive(k):
        @pl.when(has_prev)
        def _():
            pieces[k].wait_recv()
            a, b, p, q = groups[k]
            loop(a, b, lambda x: add_inner(x, p, q))

    fe_s[...] = W[0, nx]
    fe_up.start()
    fe_up.wait_recv()

    def edge_rows(x, w0_last):
        e = x + 1
        zero = jnp.zeros((1, nz), jnp.float32)
        change = first_change(SC[x], S[x], W[0, e], w0_last, W[1, e], zero, W[2, e])
        up_s[0, x] = W[1, e, ny - 1 : ny]
        up_s[1, x] = change[ny - 1 : ny]
        dn_s[0, x] = change[0:1]
        dn_s[1, x] = change[1:2]

    edge_rows(0, fe_r[...])
    loop(1, nx, lambda x: edge_rows(x, W[0, x]))
    y_up.start()
    y_dn.start()

    @pl.when(has_next & pauses)
    def _():
        wait_rows(send_sem.at[1], outer_rows)
        send_inner()

    @pl.when(has_prev)
    def _():
        wait_rows(recv_sem.at[8], 48 * parts)
        for a in (0, nx - 2):
            loop(a, a + 2, lambda x: add_inner(x, 0, parts))

    fx_up.start()
    wait_rows(recv_sem.at[2], ny + 8 * nx)

    def first(x):
        e = x + 1
        c1[e, 0:ny] = first_change(SC[x], S[x], W[0, e], W[0, x], W[1, e], up_r[0, x], W[2, e])

    def first_above(x):
        e = x + 1
        scale = damping / (Ce[3, x] + C[1, e, ny - 1 : ny])
        Se[x] = scale
        c1[e, ny : ny + 1] = dn_r[0, x] + scale * W[1, e, ny - 1 : ny]

    for x in (0, nx - 1):
        first(x)
        first_above(x)
    c1[nx, ny + 1 : ny + 2] = Ce[0, nx - 1]
    for copy in (cx_dn, cx_up):
        copy.start()
    loop(1, nx - 1, first)
    loop(1, nx - 1, first_above)
    wait_rows(recv_sem.at[3], 2 * (ny + 8))

    def second(x):
        e = x + 1
        c2[x] = second_change(
            SC[x], c1[e, 0:ny], c1[e + 1, 0:ny], c1[e - 1, 0:ny], c1[e, ny : ny + 1], up_r[1, x],
            C[0, e], C[0, x], C[1, e], Ch[x], C[2, e],
        )

    def second_above(x, c0_last):
        e = x + 1
        wide = lambda row: jnp.broadcast_to(row, (8, nz))
        here = wide(c1[e, ny : ny + 1])
        g0 = wide(Ce[0, x]) * (wide(c1[e + 1, ny : ny + 1]) - here)
        g0_last = wide(c0_last) * (here - wide(c1[e - 1, ny : ny + 1]))
        g1 = wide(Ce[1, x]) * (wide(dn_r[1, x]) - here)
        g1_last = wide(C[1, e, ny - 1 : ny]) * (here - wide(c1[e, ny - 1 : ny]))
        g2 = wide(Ce[2, x]) * (z_next(here) - here)
        div = (g0 - g0_last) + (g1 - g1_last) + (g2 - z_last(g2))
        c2e[x] = (2.0 * here + wide(Se[x]) * div)[0:1]

    second(0)
    ex_dn.start()
    second_above(0, c1[0, ny + 1 : ny + 2])
    loop(1, nx, lambda x: second_above(x, Ce[0, x - 1]))

    def finish(x):
        e = x + 1
        here = c2[x]
        OP[x] = Pr[x] + here
        moved = final_velocity(
            [W[c, e] for c in range(3)], [C[c, e] for c in range(3)], here, c2[x + 1], c2e[x]
        )
        for c in range(3):
            OV[c, x] = moved[c]

    top = slice(8, ny)

    def second_top(x):
        e = x + 1
        c2[x, top] = second_change(
            SC[x, top], c1[e, top], c1[e + 1, top], c1[e - 1, top], c1[e, ny : ny + 1], c1[e, 7:8],
            C[0, e, top], C[0, x, top], C[1, e, top], C[1, e, 7:8], C[2, e, top],
        )

    def finish_top(x):
        e = x + 1
        here = c2[x, top]
        OP[x, top] = Pr[x, top] + here
        moved = final_velocity(
            [W[c, e, top] for c in range(3)], [C[c, e, top] for c in range(3)], here, c2[x + 1, top], c2e[x]
        )
        for c in range(3):
            OV[c, x, top] = moved[c]

    for k in range(2, final - 1):
        a, b, _, _ = groups[k]
        arrive(k)
        loop(a, b, first)
        loop(a - 1, b - 1, second)
        loop(a - 2, b - 2, finish)

    @pl.when(jnp.logical_not(has_prev))
    def _():
        rL[...] = jnp.zeros_like(rL)

    ex_dn.wait_recv()
    a = groups[final][0]
    arrive(final - 1)
    loop(a, nx - 1, first)
    loop(a - 1, nx, second_top)
    loop(a - 2, nx, finish_top)

    @pl.when(has_prev)
    def _():
        pieces[final].wait_recv()

    @pl.when(has_next & jnp.logical_not(pauses))
    def _():
        wait_rows(send_sem.at[1], 3 * nx * ny)

    @pl.when(has_next & pauses)
    def _():
        wait_rows(send_sem.at[1], 3 * nx * ny - outer_rows)

    if detour:

        @pl.when(ta == via)
        def _():
            wait_rows(send_sem.at[1], 24 * parts)

    wait_rows(send_sem.at[0], 13 * ny + 16 + 16 * nx)


def settle(
    last, moved, pressed, rL, W, C, c1, c2, c2e, SC, S, Pr, up_r, Ch, step_v, step_p, nV, nP, nW, n1, n2, sem
):
    out_v, out_p = step_v.at[:, 0], step_p.at[0]
    _, nx, ny, nz = moved.shape
    a, b = last
    ready, low = a - 2, slice(0, 8)
    done, rest = pl.ds(0, ready), pl.ds(ready, nx - ready)
    bottom, top = pl.ds(0, 8), pl.ds(8, ny - 8)

    for c in range(3):
        pltpu.make_async_copy(moved.at[c, done], out_v.at[c, done], sem.at[0]).start()
        pltpu.make_async_copy(moved.at[c, rest, top], out_v.at[c, rest, top], sem.at[0]).start()
    pltpu.make_async_copy(pressed.at[done], out_p.at[done], sem.at[1]).start()
    pltpu.make_async_copy(pressed.at[rest, top], out_p.at[rest, top], sem.at[1]).start()

    def w(c, x):
        return nW[c, x - a] if a <= x < b else W[c, x + 1, low]

    def change(x):
        return n1[x - a] if a <= x < nx - 1 else c1[x + 1, low]

    def second(x):
        return n2[x - (a - 1)] if a - 1 <= x < nx else c2[x, low]

    @pl.when(lax.axis_index("ta") >= 0)
    def _():
        for x in range(a, b):
            for c in range(3):
                nW[c, x - a] = W[c, x + 1, low]
                nW[c, x - a, 2:6] = W[c, x + 1, 2:6] + C[c, x + 1, 2:6] * rL[x - a, 0, c]
        for x in range(a, nx - 1):
            n1[x - a] = first_change(SC[x, low], S[x, low], w(0, x), w(0, x - 1), w(1, x), up_r[0, x], w(2, x))
        for x in range(a - 1, nx):
            e = x + 1
            n2[x - (a - 1)] = second_change(
                SC[x, low], change(x), change(x + 1), change(x - 1), c1[e, 8:9], up_r[1, x],
                C[0, e, low], C[0, x, low], C[1, e, low], Ch[x], C[2, e, low],
            )
        for x in range(ready, nx):
            here = second(x)
            nP[x - ready] = Pr[x, low] + here
            fresh = final_velocity(
                [w(c, x) for c in range(3)], [C[c, x + 1, low] for c in range(3)], here, second(x + 1), c2[x, 8:9]
            )
            for c in range(3):
                nV[c, x - ready] = fresh[c]
        for c in range(3):
            pltpu.make_async_copy(nV.at[c], out_v.at[c, rest, bottom], sem.at[0]).start()
        pltpu.make_async_copy(nP, out_p.at[rest, bottom], sem.at[1]).start()

    pltpu.make_async_copy(moved, out_v, sem.at[0]).wait()
    pltpu.make_async_copy(pressed, out_p, sem.at[1]).wait()


def body(counts, velocity, pressure, forcing, source, viscosity):
    _, steps, nx, ny, nz = velocity.shape
    assert steps == 1 and nx >= 12 and ny >= 16 and ny % 8 == 0
    parts = (ny - 4) // 4
    last = (nx - 4, nx - 2)
    whole = [(0, 2), (nx - 2, nx), (2, 4)] + groups_of(4, nx - 4, 4)
    groups = [(a, b, 0, parts) for a, b in whole] + [(*last, 1, parts), (*last, 0, 1)]
    detour = (1, 3, 2, 2) if counts[0] == 4 else None
    vmem = lambda *shape: pltpu.VMEM(shape, jnp.float32)
    rows = lambda *lead: vmem(*lead, nx, 1, nz)
    any_space = pl.BlockSpec(memory_space=pl.ANY)
    on_chip = pl.BlockSpec(memory_space=pltpu.VMEM)
    kept = (
        vmem(3, nx, ny, nz), vmem(nx, ny, nz), vmem(2, 1, 3, 4, nz),
        vmem(3, nx + 1, ny, nz), vmem(3, nx + 1, ny, nz), vmem(nx + 2, ny + 8, nz), vmem(nx + 1, ny, nz), rows(),
        vmem(nx, ny, nz), vmem(nx, ny, nz), vmem(nx + 1, ny, nz), rows(2), rows(),
    )
    inputs = (velocity[:, 0], pressure[0], forcing[:, 0], source[0], viscosity)
    held = pl.pallas_call(
        functools.partial(kernel, *counts, groups, detour),
        out_shape=kept,
        in_specs=[any_space] * 5,
        out_specs=(on_chip,) * len(kept),
        scratch_shapes=[
            vmem(3, nx + 2, ny, nz), vmem(3, nx, ny, nz), vmem(3, nx + 1, ny, nz),
            vmem(3, nx, 4, nz), vmem(3, nx, 4, nz),
            vmem(nx, parts, 3, 4, nz), vmem(nx, parts, 3, 4, nz), vmem(2, parts, 3, 4, nz),
            rows(4), rows(4), rows(4), rows(4), rows(4), rows(4),
            vmem(ny, nz), vmem(ny, nz), rows(2), rows(2), rows(2), rows(), vmem(8 * nx * ny, nz),
            pltpu.SemaphoreType.DMA((2,)),
            pltpu.SemaphoreType.DMA((2,)),
            pltpu.SemaphoreType.DMA((7 + len(groups),)),
        ],
        compiler_params=pltpu.CompilerParams(
            collective_id=0, has_side_effects=True, vmem_limit_bytes=40 << 20
        ),
        name="smoother",
    )(*(pltpu.with_memory_space_constraint(a, pltpu.HBM) for a in inputs))
    return pl.pallas_call(
        functools.partial(settle, last),
        out_shape=(
            jax.ShapeDtypeStruct((3, 1, nx, ny, nz), jnp.float32),
            jax.ShapeDtypeStruct((1, nx, ny, nz), jnp.float32),
        ),
        in_specs=[on_chip] * len(kept),
        out_specs=(any_space, any_space),
        scratch_shapes=[
            vmem(3, 6, 8, nz), vmem(6, 8, nz), vmem(3, 2, 8, nz), vmem(3, 8, nz), vmem(5, 8, nz),
            pltpu.SemaphoreType.DMA((2,)),
        ],
        compiler_params=pltpu.CompilerParams(vmem_limit_bytes=2 << 20),
        name="settle",
    )(*held)


def solution(mesh):
    placed = (
        P(None, "ta", "gx", "gy", None),
        P("ta", "gx", "gy", None),
        P(None, "ta", "gx", "gy", None),
        P("ta", "gx", "gy", None),
        P(None, "gx", "gy", None),
    )
    counts = tuple(mesh.shape[axis] for axis in ("ta", "gx", "gy"))
    return jax.shard_map(
        functools.partial(body, counts),
        mesh=mesh,
        in_specs=placed,
        out_specs=(P(None, "ta", "gx", "gy", None), P("ta", "gx", "gy", None)),
        check_vma=False,
    )
```

```python
import functools

import jax
import jax.numpy as jnp
from jax import lax
from jax.experimental import pallas as pl
from jax.experimental.pallas import tpu as pltpu
from jax.sharding import PartitionSpec as P

relax_factor = 1.5
damping = 0.8
MESH = pl.DeviceIdType.MESH


def loop(lo, hi, body):
    def step(i, carry):
        body(i)
        return carry

    if hi > lo:
        lax.fori_loop(lo, hi, step, 0, unroll=hi - lo)


def row_index(f):
    return lax.broadcasted_iota(jnp.int32, f.shape, 0)


def y_next(f, row):
    n = f.shape[0]
    return jnp.where(row_index(f) == n - 1, row, pltpu.roll(f, n - 1, 0))


def y_last(f, row):
    return jnp.where(row_index(f) == 0, row, pltpu.roll(f, 1, 0))


def z_next(f):
    return pltpu.roll(f, f.shape[1] - 1, 1)


def z_last(f):
    return pltpu.roll(f, 1, 1)


def coeff_of(nu):
    return 1.0 / (relax_factor * (1.0 + 6.0 * nu))


def groups_of(lo, hi, size):
    return [(a, min(a + size, hi)) for a in range(lo, hi, size)]


def first_change(scale, source, w0, w0_last, w1, row, w2):
    div = (w0 - w0_last) + (w1 - y_last(w1, row)) + (w2 - z_last(w2))
    return scale * (source - div)


def second_change(scale, here, x_above, x_below, above, row, c0, c0_last, c1, c1_row, c2):
    g0, g0_last = c0 * (x_above - here), c0_last * (here - x_below)
    g1 = c1 * (y_next(here, above) - here)
    g2 = c2 * (z_next(here) - here)
    div = (g0 - g0_last) + (g1 - y_last(g1, c1_row * (here[0:1] - row))) + (g2 - z_last(g2))
    return 2.0 * here + scale * div


def final_velocity(w, c, here, x_above, above):
    return (
        w[0] - c[0] * (x_above - here),
        w[1] - c[1] * (y_next(here, above) - here),
        w[2] - c[2] * (z_next(here) - here),
    )


def kernel(
    slabs, nx_parts, ny_parts, groups, detour,
    vel, prs, frc, src, vis,
    OV, OP, rL, W, C, c1, c2, c2e, SC, S, Pr, up_r, Ch,
    V, F, Nu, sE, rE, sI, rI, rR, yu_s, yd_s, yu_r, yd_r, Ce, m_s, fe_s, fe_r, up_s, dn_s, dn_r, Se, tally,
    load_sem, send_sem, recv_sem,
):
    _, nx, ny, nz = vel.shape
    parts = (ny - 4) // 4
    final = len(groups) - 1
    ta, gx, gy = lax.axis_index("ta"), lax.axis_index("gx"), lax.axis_index("gy")
    t_next, t_prev = lax.rem(ta + 1, slabs), lax.rem(ta + slabs - 1, slabs)
    has_next, has_prev = ta < slabs - 1, ta > 0
    xu, xd = lax.rem(gx + 1, nx_parts), lax.rem(gx + nx_parts - 1, nx_parts)
    yu, yd = lax.rem(gy + 1, ny_parts), lax.rem(gy + ny_parts - 1, ny_parts)
    first_row = gy == 0

    barrier = pltpu.get_barrier_semaphore()

    def greet(axis, index):
        pl.semaphore_signal(barrier, inc=1, device_id={axis: index}, device_id_type=MESH)

    @pl.when(has_prev)
    def _():
        greet("ta", t_prev)

    expected = 2 + has_next.astype(jnp.int32) + jnp.where(first_row, 0, 2)
    if detour:
        giver, via, taker, lane = detour

        @pl.when(ta == via)
        def _():
            greet("ta", giver)

        @pl.when(ta == taker)
        def _():
            greet("ta", via)

        expected = expected + ((ta == giver) | (ta == via)).astype(jnp.int32)

    def fetch(source, target, k):
        pltpu.make_async_copy(source, target, load_sem.at[k]).start()

    def wait_rows(sem, count):
        size = pl.ds(0, count)
        pltpu.make_async_copy(tally.at[size], tally.at[size], sem).wait()

    half = nx // 2
    for a, n in ((0, half), (half, nx - half)):
        for c in range(3):
            fetch(vel.at[c, pl.ds(a, n)], V.at[c, pl.ds(1 + a, n)], 0)
    greet("gx", xu)
    greet("gx", xd)
    for beside in (yu, yd):

        @pl.when(jnp.logical_not(first_row) & (beside != 0))
        def _():
            greet("gy", beside)

    def remote(send, recv, source, target, axis, index):
        return pltpu.make_async_remote_copy(
            src_ref=source, dst_ref=target, send_sem=send_sem.at[send], recv_sem=recv_sem.at[recv],
            device_id={axis: index}, device_id_type=MESH,
        )

    vx_up = remote(0, 0, V.at[:, nx], V.at[:, 0], "gx", xu)
    vx_dn = remote(0, 0, V.at[:, 1], V.at[:, nx + 1], "gx", xd)
    px_dn = remote(0, 0, Pr.at[0], Pr.at[nx], "gx", xd)
    nx_up = remote(0, 0, Nu.at[0, nx], Nu.at[0, 0], "gx", xu)
    three, fourth = pl.ds(0, 3), pl.ds(3, 1)
    ry_up = remote(0, 6, yu_s.at[three], yu_r.at[three], "gy", yu)
    ry_dn = remote(0, 6, yd_s.at[three], yd_r.at[three], "gy", yd)
    rz_up = remote(0, 6, yu_s.at[fourth], yu_r.at[fourth], "gy", yu)
    rz_dn = remote(0, 6, yd_s.at[fourth], yd_r.at[fourth], "gy", yd)
    fe_up = remote(0, 1, fe_s, fe_r, "gx", xu)
    fx_up = remote(0, 2, W.at[0, nx], W.at[0, 0], "gx", xu)
    cx_dn = remote(0, 3, c1.at[1], c1.at[nx + 1], "gx", xd)
    cx_up = remote(0, 3, c1.at[nx], c1.at[0], "gx", xu)
    m_dn = remote(0, 2, m_s, Ce, "gy", yd)
    y_up = remote(0, 2, up_s, up_r, "gy", yu)
    y_dn = remote(0, 2, dn_s, dn_r, "gy", yd)
    ex_dn = remote(0, 4, c2.at[0], c2.at[nx], "gx", xd)
    edge = remote(1, 5, sE, rE, "ta", t_next)
    landing = [rI.at[pl.ds(a, b - a), pl.ds(p, q - p)] for a, b, p, q in groups[:final]] + [rL]
    leaving = [sI.at[pl.ds(a, b - a), pl.ds(p, q - p)] for a, b, p, q in groups]
    pieces = [remote(1, 7 + max(k, 1), leaving[k], landing[k], "ta", t_next) for k in range(final + 1)]
    if detour:
        to_via = remote(1, 7, leaving[lane], rR, "ta", via)
        from_via = remote(1, 7 + lane, rR, landing[lane], "ta", taker)

    def pack_edges(x):
        for c in range(3):
            sE[c, x, 0:2] = V[c, x + 1, 0:2]
            sE[c, x, 2:4] = V[c, x + 1, ny - 2 : ny]

    def pack_rows(x):
        for c in range(3):
            yu_s[c, x] = V[c, x + 1, ny - 1 : ny]
            yd_s[c, x] = V[c, x + 1, 0:1]

    def pack_more(x):
        yu_s[3, x] = Nu[1, x + 1, ny - 1 : ny]
        yd_s[3, x] = Pr[x, 0:1]

    def pack_inner(x):
        for c in range(3):
            for p in range(parts):
                sI[x, p, c] = V[c, x + 1, 2 + 4 * p : 6 + 4 * p]

    wait_rows(load_sem.at[0], 3 * nx * ny)
    for c in range(3):
        fetch(vis.at[c], Nu.at[c, pl.ds(1, nx)], 1)
    fetch(prs, Pr.at[pl.ds(0, nx)], 1)
    for c in range(3):
        fetch(frc.at[c], F.at[c], 2)
    fetch(src, S, 2)
    loop(0, nx, pack_edges)
    pl.semaphore_wait(barrier, expected)

    @pl.when(has_next)
    def _():
        edge.start()

    for beside in (yu, yd):

        @pl.when(first_row | (beside == 0))
        def _():
            greet("gy", beside)

    loop(0, nx, pack_rows)
    for copy in (vx_up, vx_dn):
        copy.start()

    @pl.when(jnp.logical_not(first_row))
    def _():
        ry_up.start()
        ry_dn.start()

    wait_rows(load_sem.at[1], 4 * nx * ny)
    loop(0, nx, pack_more)
    for copy in (px_dn, nx_up):
        copy.start()

    @pl.when(jnp.logical_not(first_row))
    def _():
        rz_up.start()
        rz_dn.start()

    loop(0, nx, pack_inner)

    pauses = first_row & (ta == 0) & (lax.rem(gx, 2) == 1)
    outer_rows = 12 * nx + 48 * parts

    def send_inner():
        for k in range(2, final + 1):
            if detour and k == lane:

                @pl.when(ta == giver)
                def _():
                    to_via.start()

                @pl.when(ta != giver)
                def _():
                    pieces[k].start()

            else:
                pieces[k].start()

    @pl.when(has_next)
    def _():
        pieces[0].start()
        pieces[1].start()

    @pl.when(has_next & jnp.logical_not(pauses))
    def _():
        send_inner()

    @pl.when(first_row)
    def _():
        pl.semaphore_wait(barrier, 2)
        for copy in (ry_up, ry_dn, rz_up, rz_dn):
            copy.start()

    wait_rows(load_sem.at[2], 4 * nx * ny)
    wait_rows(recv_sem.at[0], 8 * ny)
    C[0, 0] = coeff_of(Nu[0, 0])

    def prepare(x):
        e = x + 1
        none = jnp.zeros((1, nz), jnp.float32)
        coeff = [coeff_of(Nu[c, e]) for c in range(3)]
        for c in range(3):
            C[c, e] = coeff[c]
            m_s[c, x] = coeff[c][0:1]
        total = coeff[0] + C[0, x] + coeff[1] + y_last(coeff[1], none) + coeff[2] + z_last(coeff[2])
        SC[x] = damping / total
        m_s[3, x] = total[0:1]
        press = Pr[x]
        grads = (Pr[x + 1] - press, y_next(press, none) - press, z_next(press) - press)
        for c in range(3):
            v = V[c, e]
            near = V[c, e - 1] + V[c, e + 1] + y_last(v, none) + y_next(v, none)
            near = near + z_last(v) + z_next(v)
            momentum = F[c, x] - (v + Nu[c, e] * (6.0 * v - near)) - grads[c]
            W[c, e] = v + coeff[c] * momentum

    def complete(x):
        e, t = x + 1, ny - 1
        below = coeff_of(yu_r[3, x])
        Ch[x] = below
        SC[x, 0:1] = damping / (m_s[3, x] + below)
        for c in range(3):
            W[c, e, 0:1] = W[c, e, 0:1] + C[c, e, 0:1] * (Nu[c, e, 0:1] * yu_r[c, x])
            more = Nu[c, e, t:ny] * yd_r[c, x]
            if c == 1:
                more = more - yd_r[3, x]
            W[c, e, t:ny] = W[c, e, t:ny] + C[c, e, t:ny] * more

    loop(0, nx, prepare)
    m_dn.start()
    wait_rows(recv_sem.at[6], 8 * nx)
    loop(0, nx, complete)
    if detour:

        @pl.when(ta == via)
        def _():
            to_via.wait_recv()
            from_via.start()

    def add_edges(x):
        for c in range(3):
            for s, t in ((0, 0), (2, ny - 2)):
                W[c, x + 1, t : t + 2] = (
                    W[c, x + 1, t : t + 2] + C[c, x + 1, t : t + 2] * rE[c, x, s : s + 2]
                )

    def add_inner(x, first_part, parts_end):
        for c in range(3):
            for p in range(first_part, parts_end):
                t = 2 + 4 * p
                W[c, x + 1, t : t + 4] = W[c, x + 1, t : t + 4] + C[c, x + 1, t : t + 4] * rI[x, p, c]

    @pl.when(has_prev)
    def _():
        edge.wait_recv()
        loop(0, nx, add_edges)

    def arrive(k):
        @pl.when(has_prev)
        def _():
            pieces[k].wait_recv()
            a, b, p, q = groups[k]
            loop(a, b, lambda x: add_inner(x, p, q))

    fe_s[...] = W[0, nx]
    fe_up.start()
    fe_up.wait_recv()

    def edge_rows(x, w0_last):
        e = x + 1
        zero = jnp.zeros((1, nz), jnp.float32)
        change = first_change(SC[x], S[x], W[0, e], w0_last, W[1, e], zero, W[2, e])
        up_s[0, x] = W[1, e, ny - 1 : ny]
        up_s[1, x] = change[ny - 1 : ny]
        dn_s[0, x] = change[0:1]
        dn_s[1, x] = change[1:2]

    edge_rows(0, fe_r[...])
    loop(1, nx, lambda x: edge_rows(x, W[0, x]))
    y_up.start()
    y_dn.start()

    @pl.when(has_next & pauses)
    def _():
        wait_rows(send_sem.at[1], outer_rows)
        send_inner()

    @pl.when(has_prev)
    def _():
        wait_rows(recv_sem.at[8], 48 * parts)
        for a in (0, nx - 2):
            loop(a, a + 2, lambda x: add_inner(x, 0, parts))

    fx_up.start()
    wait_rows(recv_sem.at[2], ny + 8 * nx)

    def first(x):
        e = x + 1
        c1[e, 0:ny] = first_change(SC[x], S[x], W[0, e], W[0, x], W[1, e], up_r[0, x], W[2, e])

    def first_above(x):
        e = x + 1
        scale = damping / (Ce[3, x] + C[1, e, ny - 1 : ny])
        Se[x] = scale
        c1[e, ny : ny + 1] = dn_r[0, x] + scale * W[1, e, ny - 1 : ny]

    for x in (0, nx - 1):
        first(x)
        first_above(x)
    c1[nx, ny + 1 : ny + 2] = Ce[0, nx - 1]
    for copy in (cx_dn, cx_up):
        copy.start()
    loop(1, nx - 1, first)
    loop(1, nx - 1, first_above)
    wait_rows(recv_sem.at[3], 2 * (ny + 8))

    def second(x):
        e = x + 1
        c2[x] = second_change(
            SC[x], c1[e, 0:ny], c1[e + 1, 0:ny], c1[e - 1, 0:ny], c1[e, ny : ny + 1], up_r[1, x],
            C[0, e], C[0, x], C[1, e], Ch[x], C[2, e],
        )

    def second_above(x, c0_last):
        e = x + 1
        wide = lambda row: jnp.broadcast_to(row, (8, nz))
        here = wide(c1[e, ny : ny + 1])
        g0 = wide(Ce[0, x]) * (wide(c1[e + 1, ny : ny + 1]) - here)
        g0_last = wide(c0_last) * (here - wide(c1[e - 1, ny : ny + 1]))
        g1 = wide(Ce[1, x]) * (wide(dn_r[1, x]) - here)
        g1_last = wide(C[1, e, ny - 1 : ny]) * (here - wide(c1[e, ny - 1 : ny]))
        g2 = wide(Ce[2, x]) * (z_next(here) - here)
        div = (g0 - g0_last) + (g1 - g1_last) + (g2 - z_last(g2))
        c2e[x] = (2.0 * here + wide(Se[x]) * div)[0:1]

    second(0)
    ex_dn.start()
    second_above(0, c1[0, ny + 1 : ny + 2])
    loop(1, nx, lambda x: second_above(x, Ce[0, x - 1]))

    def finish(x):
        e = x + 1
        here = c2[x]
        OP[x] = Pr[x] + here
        moved = final_velocity(
            [W[c, e] for c in range(3)], [C[c, e] for c in range(3)], here, c2[x + 1], c2e[x]
        )
        for c in range(3):
            OV[c, x] = moved[c]

    top = slice(8, ny)

    def second_top(x):
        e = x + 1
        c2[x, top] = second_change(
            SC[x, top], c1[e, top], c1[e + 1, top], c1[e - 1, top], c1[e, ny : ny + 1], c1[e, 7:8],
            C[0, e, top], C[0, x, top], C[1, e, top], C[1, e, 7:8], C[2, e, top],
        )

    def finish_top(x):
        e = x + 1
        here = c2[x, top]
        OP[x, top] = Pr[x, top] + here
        moved = final_velocity(
            [W[c, e, top] for c in range(3)], [C[c, e, top] for c in range(3)], here, c2[x + 1, top], c2e[x]
        )
        for c in range(3):
            OV[c, x, top] = moved[c]

    for k in range(2, final - 1):
        a, b, _, _ = groups[k]
        arrive(k)
        loop(a, b, first)
        loop(a - 1, b - 1, second)
        loop(a - 2, b - 2, finish)

    @pl.when(jnp.logical_not(has_prev))
    def _():
        rL[...] = jnp.zeros_like(rL)

    ex_dn.wait_recv()
    a = groups[final][0]
    arrive(final - 1)
    loop(a, nx - 1, first)
    loop(a - 1, nx, second_top)
    loop(a - 2, nx, finish_top)

    @pl.when(has_prev)
    def _():
        pieces[final].wait_recv()

    @pl.when(has_next & jnp.logical_not(pauses))
    def _():
        wait_rows(send_sem.at[1], 3 * nx * ny)

    @pl.when(has_next & pauses)
    def _():
        wait_rows(send_sem.at[1], 3 * nx * ny - outer_rows)

    if detour:

        @pl.when(ta == via)
        def _():
            wait_rows(send_sem.at[1], 24 * parts)

    wait_rows(send_sem.at[0], 13 * ny + 16 + 16 * nx)


def settle(
    last, moved, pressed, rL, W, C, c1, c2, c2e, SC, S, Pr, up_r, Ch, step_v, step_p, nV, nP, nW, n1, n2, sem
):
    out_v, out_p = step_v.at[:, 0], step_p.at[0]
    _, nx, ny, nz = moved.shape
    a, b = last
    ready, low = a - 2, slice(0, 8)
    done, rest = pl.ds(0, ready), pl.ds(ready, nx - ready)
    bottom, top = pl.ds(0, 8), pl.ds(8, ny - 8)

    for c in range(3):
        pltpu.make_async_copy(moved.at[c, done], out_v.at[c, done], sem.at[0]).start()
        pltpu.make_async_copy(moved.at[c, rest, top], out_v.at[c, rest, top], sem.at[0]).start()
    pltpu.make_async_copy(pressed.at[done], out_p.at[done], sem.at[1]).start()
    pltpu.make_async_copy(pressed.at[rest, top], out_p.at[rest, top], sem.at[1]).start()

    def w(c, x):
        return nW[c, x - a] if a <= x < b else W[c, x + 1, low]

    def change(x):
        return n1[x - a] if a <= x < nx - 1 else c1[x + 1, low]

    def second(x):
        return n2[x - (a - 1)] if a - 1 <= x < nx else c2[x, low]

    @pl.when(lax.axis_index("ta") >= 0)
    def _():
        for x in range(a, b):
            for c in range(3):
                nW[c, x - a] = W[c, x + 1, low]
                nW[c, x - a, 2:6] = W[c, x + 1, 2:6] + C[c, x + 1, 2:6] * rL[x - a, 0, c]
        for x in range(a, nx - 1):
            n1[x - a] = first_change(SC[x, low], S[x, low], w(0, x), w(0, x - 1), w(1, x), up_r[0, x], w(2, x))
        for x in range(a - 1, nx):
            e = x + 1
            n2[x - (a - 1)] = second_change(
                SC[x, low], change(x), change(x + 1), change(x - 1), c1[e, 8:9], up_r[1, x],
                C[0, e, low], C[0, x, low], C[1, e, low], Ch[x], C[2, e, low],
            )
        for x in range(ready, nx):
            here = second(x)
            nP[x - ready] = Pr[x, low] + here
            fresh = final_velocity(
                [w(c, x) for c in range(3)], [C[c, x + 1, low] for c in range(3)], here, second(x + 1), c2[x, 8:9]
            )
            for c in range(3):
                nV[c, x - ready] = fresh[c]
        for c in range(3):
            pltpu.make_async_copy(nV.at[c], out_v.at[c, rest, bottom], sem.at[0]).start()
        pltpu.make_async_copy(nP, out_p.at[rest, bottom], sem.at[1]).start()

    pltpu.make_async_copy(moved, out_v, sem.at[0]).wait()
    pltpu.make_async_copy(pressed, out_p, sem.at[1]).wait()


def body(counts, velocity, pressure, forcing, source, viscosity):
    _, steps, nx, ny, nz = velocity.shape
    assert steps == 1 and nx >= 12 and ny >= 16 and ny % 8 == 0
    parts = (ny - 4) // 4
    last = (nx - 4, nx - 2)
    whole = [(0, 2), (nx - 2, nx), (2, 4)] + groups_of(4, nx - 4, 4)
    groups = [(a, b, 0, parts) for a, b in whole] + [(*last, 1, parts), (*last, 0, 1)]
    detour = (1, 3, 2, 2) if counts[0] == 4 else None
    vmem = lambda *shape: pltpu.VMEM(shape, jnp.float32)
    rows = lambda *lead: vmem(*lead, nx, 1, nz)
    any_space = pl.BlockSpec(memory_space=pl.ANY)
    on_chip = pl.BlockSpec(memory_space=pltpu.VMEM)
    kept = (
        vmem(3, nx, ny, nz), vmem(nx, ny, nz), vmem(2, 1, 3, 4, nz),
        vmem(3, nx + 1, ny, nz), vmem(3, nx + 1, ny, nz), vmem(nx + 2, ny + 8, nz), vmem(nx + 1, ny, nz), rows(),
        vmem(nx, ny, nz), vmem(nx, ny, nz), vmem(nx + 1, ny, nz), rows(2), rows(),
    )
    inputs = (velocity[:, 0], pressure[0], forcing[:, 0], source[0], viscosity)
    held = pl.pallas_call(
        functools.partial(kernel, *counts, groups, detour),
        out_shape=kept,
        in_specs=[any_space] * 5,
        out_specs=(on_chip,) * len(kept),
        scratch_shapes=[
            vmem(3, nx + 2, ny, nz), vmem(3, nx, ny, nz), vmem(3, nx + 1, ny, nz),
            vmem(3, nx, 4, nz), vmem(3, nx, 4, nz),
            vmem(nx, parts, 3, 4, nz), vmem(nx, parts, 3, 4, nz), vmem(2, parts, 3, 4, nz),
            rows(4), rows(4), rows(4), rows(4), rows(4), rows(4),
            vmem(ny, nz), vmem(ny, nz), rows(2), rows(2), rows(2), rows(), vmem(4 * nx * ny, nz),
            pltpu.SemaphoreType.DMA((3,)),
            pltpu.SemaphoreType.DMA((2,)),
            pltpu.SemaphoreType.DMA((7 + len(groups),)),
        ],
        compiler_params=pltpu.CompilerParams(
            collective_id=0, has_side_effects=True, vmem_limit_bytes=40 << 20
        ),
        name="smoother",
    )(*(pltpu.with_memory_space_constraint(a, pltpu.HBM) for a in inputs))
    return pl.pallas_call(
        functools.partial(settle, last),
        out_shape=(
            jax.ShapeDtypeStruct((3, 1, nx, ny, nz), jnp.float32),
            jax.ShapeDtypeStruct((1, nx, ny, nz), jnp.float32),
        ),
        in_specs=[on_chip] * len(kept),
        out_specs=(any_space, any_space),
        scratch_shapes=[
            vmem(3, 6, 8, nz), vmem(6, 8, nz), vmem(3, 2, 8, nz), vmem(3, 8, nz), vmem(5, 8, nz),
            pltpu.SemaphoreType.DMA((2,)),
        ],
        compiler_params=pltpu.CompilerParams(vmem_limit_bytes=2 << 20),
        name="settle",
    )(*held)


def solution(mesh):
    placed = (
        P(None, "ta", "gx", "gy", None),
        P("ta", "gx", "gy", None),
        P(None, "ta", "gx", "gy", None),
        P("ta", "gx", "gy", None),
        P(None, "gx", "gy", None),
    )
    counts = tuple(mesh.shape[axis] for axis in ("ta", "gx", "gy"))
    return jax.shard_map(
        functools.partial(body, counts),
        mesh=mesh,
        in_specs=placed,
        out_specs=(P(None, "ta", "gx", "gy", None), P("ta", "gx", "gy", None)),
        check_vma=False,
    )
```

```python
import functools

import jax
import jax.numpy as jnp
from jax import lax
from jax.experimental import pallas as pl
from jax.experimental.pallas import tpu as pltpu
from jax.sharding import PartitionSpec as P

relax_factor = 1.5
damping = 0.8
MESH = pl.DeviceIdType.MESH


def loop(lo, hi, body):
    def step(i, carry):
        body(i)
        return carry

    if hi > lo:
        lax.fori_loop(lo, hi, step, 0, unroll=hi - lo)


def row_index(f):
    return lax.broadcasted_iota(jnp.int32, f.shape, 0)


def y_next(f, row):
    n = f.shape[0]
    return jnp.where(row_index(f) == n - 1, row, pltpu.roll(f, n - 1, 0))


def y_last(f, row):
    return jnp.where(row_index(f) == 0, row, pltpu.roll(f, 1, 0))


def z_next(f):
    return pltpu.roll(f, f.shape[1] - 1, 1)


def z_last(f):
    return pltpu.roll(f, 1, 1)


def coeff_of(nu):
    return 1.0 / (relax_factor * (1.0 + 6.0 * nu))


def groups_of(lo, hi, size):
    return [(a, min(a + size, hi)) for a in range(lo, hi, size)]


def first_change(scale, source, w0, w0_last, w1, row, w2):
    div = (w0 - w0_last) + (w1 - y_last(w1, row)) + (w2 - z_last(w2))
    return scale * (source - div)


def second_change(scale, here, x_above, x_below, above, row, c0, c0_last, c1, c1_row, c2):
    g0, g0_last = c0 * (x_above - here), c0_last * (here - x_below)
    g1 = c1 * (y_next(here, above) - here)
    g2 = c2 * (z_next(here) - here)
    div = (g0 - g0_last) + (g1 - y_last(g1, c1_row * (here[0:1] - row))) + (g2 - z_last(g2))
    return 2.0 * here + scale * div


def final_velocity(w, c, here, x_above, above):
    return (
        w[0] - c[0] * (x_above - here),
        w[1] - c[1] * (y_next(here, above) - here),
        w[2] - c[2] * (z_next(here) - here),
    )


def kernel(
    slabs, nx_parts, ny_parts, groups, detour,
    vel, prs, frc, src, vis,
    OV, OP, rL, W, C, c1, c2, c2e, SC, S, Pr, up_r, Ch,
    V, F, Nu, sE, rE, sI, rI, rR, yu_s, yd_s, yu_r, yd_r, Ce, m_s, fe_s, fe_r, up_s, dn_s, dn_r, Se, tally,
    load_sem, send_sem, recv_sem,
):
    _, nx, ny, nz = vel.shape
    parts = (ny - 4) // 4
    final = len(groups) - 1
    ta, gx, gy = lax.axis_index("ta"), lax.axis_index("gx"), lax.axis_index("gy")
    t_next, t_prev = lax.rem(ta + 1, slabs), lax.rem(ta + slabs - 1, slabs)
    has_next, has_prev = ta < slabs - 1, ta > 0
    xu, xd = lax.rem(gx + 1, nx_parts), lax.rem(gx + nx_parts - 1, nx_parts)
    yu, yd = lax.rem(gy + 1, ny_parts), lax.rem(gy + ny_parts - 1, ny_parts)
    first_row = gy == 0

    barrier = pltpu.get_barrier_semaphore()

    def greet(axis, index):
        pl.semaphore_signal(barrier, inc=1, device_id={axis: index}, device_id_type=MESH)

    @pl.when(has_prev)
    def _():
        greet("ta", t_prev)

    expected = 2 + has_next.astype(jnp.int32) + jnp.where(first_row, 0, 2)
    if detour:
        giver, via, taker, lane = detour

        @pl.when(ta == via)
        def _():
            greet("ta", giver)

        @pl.when(ta == taker)
        def _():
            greet("ta", via)

        expected = expected + ((ta == giver) | (ta == via)).astype(jnp.int32)

    def fetch(source, target, k):
        pltpu.make_async_copy(source, target, load_sem.at[k]).start()

    def wait_rows(sem, count):
        size = pl.ds(0, count)
        pltpu.make_async_copy(tally.at[size], tally.at[size], sem).wait()

    half = nx // 2
    for a, n in ((0, half), (half, nx - half)):
        for c in range(3):
            fetch(vel.at[c, pl.ds(a, n)], V.at[c, pl.ds(1 + a, n)], 0)
    greet("gx", xu)
    greet("gx", xd)
    for beside in (yu, yd):

        @pl.when(jnp.logical_not(first_row) & (beside != 0))
        def _():
            greet("gy", beside)

    def remote(send, recv, source, target, axis, index):
        return pltpu.make_async_remote_copy(
            src_ref=source, dst_ref=target, send_sem=send_sem.at[send], recv_sem=recv_sem.at[recv],
            device_id={axis: index}, device_id_type=MESH,
        )

    vx_up = remote(0, 0, V.at[:, nx], V.at[:, 0], "gx", xu)
    vx_dn = remote(0, 0, V.at[:, 1], V.at[:, nx + 1], "gx", xd)
    px_dn = remote(0, 0, Pr.at[0], Pr.at[nx], "gx", xd)
    nx_up = remote(0, 0, Nu.at[0, nx], Nu.at[0, 0], "gx", xu)
    three, fourth = pl.ds(0, 3), pl.ds(3, 1)
    ry_up = remote(0, 6, yu_s.at[three], yu_r.at[three], "gy", yu)
    ry_dn = remote(0, 6, yd_s.at[three], yd_r.at[three], "gy", yd)
    rz_up = remote(0, 6, yu_s.at[fourth], yu_r.at[fourth], "gy", yu)
    rz_dn = remote(0, 6, yd_s.at[fourth], yd_r.at[fourth], "gy", yd)
    fe_up = remote(0, 1, fe_s, fe_r, "gx", xu)
    fx_up = remote(0, 2, W.at[0, nx], W.at[0, 0], "gx", xu)
    cx_dn = remote(0, 3, c1.at[1], c1.at[nx + 1], "gx", xd)
    cx_up = remote(0, 3, c1.at[nx], c1.at[0], "gx", xu)
    m_dn = remote(0, 2, m_s, Ce, "gy", yd)
    y_up = remote(0, 2, up_s, up_r, "gy", yu)
    y_dn = remote(0, 2, dn_s, dn_r, "gy", yd)
    ex_dn = remote(0, 4, c2.at[0], c2.at[nx], "gx", xd)
    edge = remote(1, 5, sE, rE, "ta", t_next)
    landing = [rI.at[pl.ds(a, b - a), pl.ds(p, q - p)] for a, b, p, q in groups[:final]] + [rL]
    leaving = [sI.at[pl.ds(a, b - a), pl.ds(p, q - p)] for a, b, p, q in groups]
    pieces = [remote(1, 7 + max(k, 1), leaving[k], landing[k], "ta", t_next) for k in range(final + 1)]
    if detour:
        to_via = remote(1, 7, leaving[lane], rR, "ta", via)
        from_via = remote(1, 7 + lane, rR, landing[lane], "ta", taker)

    def pack_edges(x):
        for c in range(3):
            sE[c, x, 0:2] = V[c, x + 1, 0:2]
            sE[c, x, 2:4] = V[c, x + 1, ny - 2 : ny]

    def pack_rows(x):
        for c in range(3):
            yu_s[c, x] = V[c, x + 1, ny - 1 : ny]
            yd_s[c, x] = V[c, x + 1, 0:1]

    def pack_more(x):
        yu_s[3, x] = Nu[1, x + 1, ny - 1 : ny]
        yd_s[3, x] = Pr[x, 0:1]

    def pack_inner(x):
        for c in range(3):
            for p in range(parts):
                sI[x, p, c] = V[c, x + 1, 2 + 4 * p : 6 + 4 * p]

    wait_rows(load_sem.at[0], 3 * nx * ny)
    for c in range(3):
        fetch(vis.at[c], Nu.at[c, pl.ds(1, nx)], 1)
    fetch(prs, Pr.at[pl.ds(0, nx)], 1)
    for c in range(3):
        fetch(frc.at[c], F.at[c], 2)
    fetch(src, S, 2)
    loop(0, nx, pack_edges)
    pl.semaphore_wait(barrier, expected)

    @pl.when(has_next)
    def _():
        edge.start()

    for beside in (yu, yd):

        @pl.when(first_row | (beside == 0))
        def _():
            greet("gy", beside)

    loop(0, nx, pack_rows)
    for copy in (vx_up, vx_dn):
        copy.start()

    @pl.when(jnp.logical_not(first_row))
    def _():
        ry_up.start()
        ry_dn.start()

    wait_rows(load_sem.at[1], 4 * nx * ny)
    loop(0, nx, pack_more)
    for copy in (px_dn, nx_up):
        copy.start()

    @pl.when(jnp.logical_not(first_row))
    def _():
        rz_up.start()
        rz_dn.start()

    loop(0, nx, pack_inner)

    pauses = first_row & (ta == 0) & (lax.rem(gx, 2) == 1)
    outer_rows = 12 * nx + 48 * parts

    def send_inner():
        for k in range(2, final + 1):
            if detour and k == lane:

                @pl.when(ta == giver)
                def _():
                    to_via.start()

                @pl.when(ta != giver)
                def _():
                    pieces[k].start()

            else:
                pieces[k].start()

    @pl.when(has_next)
    def _():
        pieces[0].start()
        pieces[1].start()

    @pl.when(has_next & jnp.logical_not(pauses))
    def _():
        send_inner()

    @pl.when(first_row)
    def _():
        pl.semaphore_wait(barrier, 2)
        for copy in (ry_up, ry_dn, rz_up, rz_dn):
            copy.start()

    wait_rows(load_sem.at[2], 4 * nx * ny)
    wait_rows(recv_sem.at[0], 8 * ny)
    C[0, 0] = coeff_of(Nu[0, 0])

    def prepare(x):
        e = x + 1
        none = jnp.zeros((1, nz), jnp.float32)
        coeff = [coeff_of(Nu[c, e]) for c in range(3)]
        for c in range(3):
            C[c, e] = coeff[c]
            m_s[c, x] = coeff[c][0:1]
        total = coeff[0] + C[0, x] + coeff[1] + y_last(coeff[1], none) + coeff[2] + z_last(coeff[2])
        SC[x] = damping / total
        m_s[3, x] = total[0:1]
        press = Pr[x]
        grads = (Pr[x + 1] - press, y_next(press, none) - press, z_next(press) - press)
        for c in range(3):
            v = V[c, e]
            near = V[c, e - 1] + V[c, e + 1] + y_last(v, none) + y_next(v, none)
            near = near + z_last(v) + z_next(v)
            momentum = F[c, x] - (v + Nu[c, e] * (6.0 * v - near)) - grads[c]
            W[c, e] = v + coeff[c] * momentum

    def complete(x):
        e, t = x + 1, ny - 1
        below = coeff_of(yu_r[3, x])
        Ch[x] = below
        SC[x, 0:1] = damping / (m_s[3, x] + below)
        for c in range(3):
            W[c, e, 0:1] = W[c, e, 0:1] + C[c, e, 0:1] * (Nu[c, e, 0:1] * yu_r[c, x])
            more = Nu[c, e, t:ny] * yd_r[c, x]
            if c == 1:
                more = more - yd_r[3, x]
            W[c, e, t:ny] = W[c, e, t:ny] + C[c, e, t:ny] * more

    loop(0, nx, prepare)
    m_dn.start()
    wait_rows(recv_sem.at[6], 8 * nx)
    loop(0, nx, complete)
    if detour:

        @pl.when(ta == via)
        def _():
            to_via.wait_recv()
            from_via.start()

    def add_edges(x):
        for c in range(3):
            for s, t in ((0, 0), (2, ny - 2)):
                W[c, x + 1, t : t + 2] = (
                    W[c, x + 1, t : t + 2] + C[c, x + 1, t : t + 2] * rE[c, x, s : s + 2]
                )

    def add_inner(x, first_part, parts_end):
        for c in range(3):
            for p in range(first_part, parts_end):
                t = 2 + 4 * p
                W[c, x + 1, t : t + 4] = W[c, x + 1, t : t + 4] + C[c, x + 1, t : t + 4] * rI[x, p, c]

    @pl.when(has_prev)
    def _():
        edge.wait_recv()
        loop(0, nx, add_edges)

    def arrive(k):
        @pl.when(has_prev)
        def _():
            pieces[k].wait_recv()
            a, b, p, q = groups[k]
            loop(a, b, lambda x: add_inner(x, p, q))

    fe_s[...] = W[0, nx]
    fe_up.start()
    fe_up.wait_recv()

    def edge_rows(x, w0_last):
        e = x + 1
        zero = jnp.zeros((1, nz), jnp.float32)
        change = first_change(SC[x], S[x], W[0, e], w0_last, W[1, e], zero, W[2, e])
        up_s[0, x] = W[1, e, ny - 1 : ny]
        up_s[1, x] = change[ny - 1 : ny]
        dn_s[0, x] = change[0:1]
        dn_s[1, x] = change[1:2]

    edge_rows(0, fe_r[...])
    loop(1, nx, lambda x: edge_rows(x, W[0, x]))
    y_up.start()
    y_dn.start()

    @pl.when(has_next & pauses)
    def _():
        wait_rows(send_sem.at[1], outer_rows)
        send_inner()

    @pl.when(has_prev)
    def _():
        wait_rows(recv_sem.at[8], 48 * parts)
        for a in (0, nx - 2):
            loop(a, a + 2, lambda x: add_inner(x, 0, parts))

    fx_up.start()
    wait_rows(recv_sem.at[2], ny + 8 * nx)

    def first(x):
        e = x + 1
        c1[e, 0:ny] = first_change(SC[x], S[x], W[0, e], W[0, x], W[1, e], up_r[0, x], W[2, e])

    def first_above(x):
        e = x + 1
        scale = damping / (Ce[3, x] + C[1, e, ny - 1 : ny])
        Se[x] = scale
        c1[e, ny : ny + 1] = dn_r[0, x] + scale * W[1, e, ny - 1 : ny]

    for x in (0, nx - 1):
        first(x)
        first_above(x)
    c1[nx, ny + 1 : ny + 2] = Ce[0, nx - 1]
    for copy in (cx_dn, cx_up):
        copy.start()
    loop(1, nx - 1, first)
    loop(1, nx - 1, first_above)
    wait_rows(recv_sem.at[3], 2 * (ny + 8))

    def second(x):
        e = x + 1
        c2[x] = second_change(
            SC[x], c1[e, 0:ny], c1[e + 1, 0:ny], c1[e - 1, 0:ny], c1[e, ny : ny + 1], up_r[1, x],
            C[0, e], C[0, x], C[1, e], Ch[x], C[2, e],
        )

    def second_above(x, c0_last):
        e = x + 1
        wide = lambda row: jnp.broadcast_to(row, (8, nz))
        here = wide(c1[e, ny : ny + 1])
        g0 = wide(Ce[0, x]) * (wide(c1[e + 1, ny : ny + 1]) - here)
        g0_last = wide(c0_last) * (here - wide(c1[e - 1, ny : ny + 1]))
        g1 = wide(Ce[1, x]) * (wide(dn_r[1, x]) - here)
        g1_last = wide(C[1, e, ny - 1 : ny]) * (here - wide(c1[e, ny - 1 : ny]))
        g2 = wide(Ce[2, x]) * (z_next(here) - here)
        div = (g0 - g0_last) + (g1 - g1_last) + (g2 - z_last(g2))
        c2e[x] = (2.0 * here + wide(Se[x]) * div)[0:1]

    second(0)
    ex_dn.start()
    second_above(0, c1[0, ny + 1 : ny + 2])
    loop(1, nx, lambda x: second_above(x, Ce[0, x - 1]))

    def finish(x):
        e = x + 1
        here = c2[x]
        OP[x] = Pr[x] + here
        moved = final_velocity(
            [W[c, e] for c in range(3)], [C[c, e] for c in range(3)], here, c2[x + 1], c2e[x]
        )
        for c in range(3):
            OV[c, x] = moved[c]

    top = slice(8, ny)

    def second_top(x):
        e = x + 1
        c2[x, top] = second_change(
            SC[x, top], c1[e, top], c1[e + 1, top], c1[e - 1, top], c1[e, ny : ny + 1], c1[e, 7:8],
            C[0, e, top], C[0, x, top], C[1, e, top], C[1, e, 7:8], C[2, e, top],
        )

    def finish_top(x):
        e = x + 1
        here = c2[x, top]
        OP[x, top] = Pr[x, top] + here
        moved = final_velocity(
            [W[c, e, top] for c in range(3)], [C[c, e, top] for c in range(3)], here, c2[x + 1, top], c2e[x]
        )
        for c in range(3):
            OV[c, x, top] = moved[c]

    for k in range(2, final - 1):
        a, b, _, _ = groups[k]
        arrive(k)
        loop(a, b, first)
        loop(a - 1, b - 1, second)
        loop(a - 2, b - 2, finish)

    @pl.when(jnp.logical_not(has_prev))
    def _():
        rL[...] = jnp.zeros_like(rL)

    ex_dn.wait_recv()
    a = groups[final][0]
    arrive(final - 1)
    loop(a, nx - 1, first)
    loop(a - 1, nx, second_top)
    loop(a - 2, nx, finish_top)

    @pl.when(has_prev)
    def _():
        pieces[final].wait_recv()

    @pl.when(has_next & jnp.logical_not(pauses))
    def _():
        wait_rows(send_sem.at[1], 3 * nx * ny)

    @pl.when(has_next & pauses)
    def _():
        wait_rows(send_sem.at[1], 3 * nx * ny - outer_rows)

    if detour:

        @pl.when(ta == via)
        def _():
            wait_rows(send_sem.at[1], 24 * parts)

    wait_rows(send_sem.at[0], 13 * ny + 16 + 16 * nx)


def settle(
    last, moved, pressed, rL, W, C, c1, c2, c2e, SC, S, Pr, up_r, Ch, step_v, step_p, nV, nP, nW, n1, n2, sem
):
    out_v, out_p = step_v.at[:, 0], step_p.at[0]
    _, nx, ny, nz = moved.shape
    a, b = last
    ready, low = a - 2, slice(0, 8)
    done, rest = pl.ds(0, ready), pl.ds(ready, nx - ready)
    bottom, top = pl.ds(0, 8), pl.ds(8, ny - 8)

    for c in range(3):
        pltpu.make_async_copy(moved.at[c, done], out_v.at[c, done], sem.at[0]).start()
        pltpu.make_async_copy(moved.at[c, rest, top], out_v.at[c, rest, top], sem.at[0]).start()
    pltpu.make_async_copy(pressed.at[done], out_p.at[done], sem.at[1]).start()
    pltpu.make_async_copy(pressed.at[rest, top], out_p.at[rest, top], sem.at[1]).start()

    def w(c, x):
        return nW[c, x - a] if a <= x < b else W[c, x + 1, low]

    def change(x):
        return n1[x - a] if a <= x < nx - 1 else c1[x + 1, low]

    def second(x):
        return n2[x - (a - 1)] if a - 1 <= x < nx else c2[x, low]

    @pl.when(lax.axis_index("ta") >= 0)
    def _():
        for x in range(a, b):
            for c in range(3):
                nW[c, x - a] = W[c, x + 1, low]
                nW[c, x - a, 2:6] = W[c, x + 1, 2:6] + C[c, x + 1, 2:6] * rL[x - a, 0, c]
        for x in range(a, nx - 1):
            n1[x - a] = first_change(SC[x, low], S[x, low], w(0, x), w(0, x - 1), w(1, x), up_r[0, x], w(2, x))
        for x in range(a - 1, nx):
            e = x + 1
            n2[x - (a - 1)] = second_change(
                SC[x, low], change(x), change(x + 1), change(x - 1), c1[e, 8:9], up_r[1, x],
                C[0, e, low], C[0, x, low], C[1, e, low], Ch[x], C[2, e, low],
            )
        for x in range(ready, nx):
            here = second(x)
            nP[x - ready] = Pr[x, low] + here
            fresh = final_velocity(
                [w(c, x) for c in range(3)], [C[c, x + 1, low] for c in range(3)], here, second(x + 1), c2[x, 8:9]
            )
            for c in range(3):
                nV[c, x - ready] = fresh[c]
        for c in range(3):
            pltpu.make_async_copy(nV.at[c], out_v.at[c, rest, bottom], sem.at[0]).start()
        pltpu.make_async_copy(nP, out_p.at[rest, bottom], sem.at[1]).start()

    pltpu.make_async_copy(moved, out_v, sem.at[0]).wait()
    pltpu.make_async_copy(pressed, out_p, sem.at[1]).wait()


def body(counts, velocity, pressure, forcing, source, viscosity):
    _, steps, nx, ny, nz = velocity.shape
    assert steps == 1 and nx >= 12 and ny >= 16 and ny % 8 == 0
    parts = (ny - 4) // 4
    last = (nx - 4, nx - 2)
    whole = [(0, 2), (nx - 2, nx), (2, 4)] + groups_of(4, nx - 6, 4) + [(nx - 6, nx - 4)]
    groups = [(a, b, 0, parts) for a, b in whole] + [(*last, 1, parts), (*last, 0, 1)]
    detour = (1, 3, 2, 2) if counts[0] == 4 else None
    vmem = lambda *shape: pltpu.VMEM(shape, jnp.float32)
    rows = lambda *lead: vmem(*lead, nx, 1, nz)
    any_space = pl.BlockSpec(memory_space=pl.ANY)
    on_chip = pl.BlockSpec(memory_space=pltpu.VMEM)
    kept = (
        vmem(3, nx, ny, nz), vmem(nx, ny, nz), vmem(2, 1, 3, 4, nz),
        vmem(3, nx + 1, ny, nz), vmem(3, nx + 1, ny, nz), vmem(nx + 2, ny + 8, nz), vmem(nx + 1, ny, nz), rows(),
        vmem(nx, ny, nz), vmem(nx, ny, nz), vmem(nx + 1, ny, nz), rows(2), rows(),
    )
    inputs = (velocity[:, 0], pressure[0], forcing[:, 0], source[0], viscosity)
    held = pl.pallas_call(
        functools.partial(kernel, *counts, groups, detour),
        out_shape=kept,
        in_specs=[any_space] * 5,
        out_specs=(on_chip,) * len(kept),
        scratch_shapes=[
            vmem(3, nx + 2, ny, nz), vmem(3, nx, ny, nz), vmem(3, nx + 1, ny, nz),
            vmem(3, nx, 4, nz), vmem(3, nx, 4, nz),
            vmem(nx, parts, 3, 4, nz), vmem(nx, parts, 3, 4, nz), vmem(2, parts, 3, 4, nz),
            rows(4), rows(4), rows(4), rows(4), rows(4), rows(4),
            vmem(ny, nz), vmem(ny, nz), rows(2), rows(2), rows(2), rows(), vmem(4 * nx * ny, nz),
            pltpu.SemaphoreType.DMA((3,)),
            pltpu.SemaphoreType.DMA((2,)),
            pltpu.SemaphoreType.DMA((7 + len(groups),)),
        ],
        compiler_params=pltpu.CompilerParams(
            collective_id=0, has_side_effects=True, vmem_limit_bytes=40 << 20
        ),
        name="smoother",
    )(*(pltpu.with_memory_space_constraint(a, pltpu.HBM) for a in inputs))
    return pl.pallas_call(
        functools.partial(settle, last),
        out_shape=(
            jax.ShapeDtypeStruct((3, 1, nx, ny, nz), jnp.float32),
            jax.ShapeDtypeStruct((1, nx, ny, nz), jnp.float32),
        ),
        in_specs=[on_chip] * len(kept),
        out_specs=(any_space, any_space),
        scratch_shapes=[
            vmem(3, 6, 8, nz), vmem(6, 8, nz), vmem(3, 2, 8, nz), vmem(3, 8, nz), vmem(5, 8, nz),
            pltpu.SemaphoreType.DMA((2,)),
        ],
        compiler_params=pltpu.CompilerParams(vmem_limit_bytes=2 << 20),
        name="settle",
    )(*held)


def solution(mesh):
    placed = (
        P(None, "ta", "gx", "gy", None),
        P("ta", "gx", "gy", None),
        P(None, "ta", "gx", "gy", None),
        P("ta", "gx", "gy", None),
        P(None, "gx", "gy", None),
    )
    counts = tuple(mesh.shape[axis] for axis in ("ta", "gx", "gy"))
    return jax.shard_map(
        functools.partial(body, counts),
        mesh=mesh,
        in_specs=placed,
        out_specs=(P(None, "ta", "gx", "gy", None), P("ta", "gx", "gy", None)),
        check_vma=False,
    )
```

```python
import functools

import jax
import jax.numpy as jnp
from jax import lax
from jax.experimental import pallas as pl
from jax.experimental.pallas import tpu as pltpu
from jax.sharding import PartitionSpec as P

relax_factor = 1.5
damping = 0.8
MESH = pl.DeviceIdType.MESH


def loop(lo, hi, body):
    def step(i, carry):
        body(i)
        return carry

    if hi > lo:
        lax.fori_loop(lo, hi, step, 0, unroll=hi - lo)


def row_index(f):
    return lax.broadcasted_iota(jnp.int32, f.shape, 0)


def y_next(f, row):
    n = f.shape[0]
    return jnp.where(row_index(f) == n - 1, row, pltpu.roll(f, n - 1, 0))


def y_last(f, row):
    return jnp.where(row_index(f) == 0, row, pltpu.roll(f, 1, 0))


def z_next(f):
    return pltpu.roll(f, f.shape[1] - 1, 1)


def z_last(f):
    return pltpu.roll(f, 1, 1)


def coeff_of(nu):
    return 1.0 / (relax_factor * (1.0 + 6.0 * nu))


def groups_of(lo, hi, size):
    return [(a, min(a + size, hi)) for a in range(lo, hi, size)]


def first_change(scale, source, w0, w0_last, w1, row, w2):
    div = (w0 - w0_last) + (w1 - y_last(w1, row)) + (w2 - z_last(w2))
    return scale * (source - div)


def second_change(scale, here, x_above, x_below, above, row, c0, c0_last, c1, c1_row, c2):
    g0, g0_last = c0 * (x_above - here), c0_last * (here - x_below)
    g1 = c1 * (y_next(here, above) - here)
    g2 = c2 * (z_next(here) - here)
    div = (g0 - g0_last) + (g1 - y_last(g1, c1_row * (here[0:1] - row))) + (g2 - z_last(g2))
    return 2.0 * here + scale * div


def final_velocity(w, c, here, x_above, above):
    return (
        w[0] - c[0] * (x_above - here),
        w[1] - c[1] * (y_next(here, above) - here),
        w[2] - c[2] * (z_next(here) - here),
    )


def kernel(
    slabs, nx_parts, ny_parts, groups, detour,
    vel, prs, frc, src, vis,
    OV, OP, rL, W, C, c1, c2, c2e, SC, S, Pr, up_r, Ch,
    V, F, Nu, sE, rE, sI, rI, rR, yu_s, yd_s, yu_r, yd_r, Ce, m_s, fe_s, fe_r, up_s, dn_s, dn_r, Se, tally,
    load_sem, send_sem, recv_sem,
):
    _, nx, ny, nz = vel.shape
    parts = (ny - 4) // 4
    final = len(groups) - 1
    ta, gx, gy = lax.axis_index("ta"), lax.axis_index("gx"), lax.axis_index("gy")
    t_next = jnp.minimum(ta + 1, slabs - 1)
    has_next, has_prev = ta < slabs - 1, ta > 0
    xu, xd = lax.rem(gx + 1, nx_parts), lax.rem(gx + nx_parts - 1, nx_parts)
    yu, yd = lax.rem(gy + 1, ny_parts), lax.rem(gy + ny_parts - 1, ny_parts)
    first_row = gy == 0

    barrier = pltpu.get_barrier_semaphore()

    def greet(axis, index):
        pl.semaphore_signal(barrier, inc=1, device_id={axis: index}, device_id_type=MESH)

    @pl.when(has_prev)
    def _():
        greet("ta", ta - 1)

    expected = 2 + has_next.astype(jnp.int32) + jnp.where(first_row, 0, 2)
    if detour:
        giver, via, taker, lane = detour

        @pl.when(ta == via)
        def _():
            greet("ta", giver)

        @pl.when(ta == taker)
        def _():
            greet("ta", via)

        expected = expected + ((ta == giver) | (ta == via)).astype(jnp.int32)

    def fetch(source, target, k):
        pltpu.make_async_copy(source, target, load_sem.at[k]).start()

    def wait_rows(sem, count):
        size = pl.ds(0, count)
        pltpu.make_async_copy(tally.at[size], tally.at[size], sem).wait()

    half = nx // 2
    for a, n in ((0, half), (half, nx - half)):
        for c in range(3):
            fetch(vel.at[c, pl.ds(a, n)], V.at[c, pl.ds(1 + a, n)], 0)
    greet("gx", xu)
    greet("gx", xd)
    for beside in (yu, yd):

        @pl.when(jnp.logical_not(first_row) & (beside != 0))
        def _():
            greet("gy", beside)

    def remote(send, recv, source, target, axis, index):
        return pltpu.make_async_remote_copy(
            src_ref=source, dst_ref=target, send_sem=send_sem.at[send], recv_sem=recv_sem.at[recv],
            device_id={axis: index}, device_id_type=MESH,
        )

    vx_up = remote(0, 0, V.at[:, nx], V.at[:, 0], "gx", xu)
    vx_dn = remote(0, 0, V.at[:, 1], V.at[:, nx + 1], "gx", xd)
    px_dn = remote(0, 0, Pr.at[0], Pr.at[nx], "gx", xd)
    nx_up = remote(0, 0, Nu.at[0, nx], Nu.at[0, 0], "gx", xu)
    three, fourth = pl.ds(0, 3), pl.ds(3, 1)
    ry_up = remote(0, 6, yu_s.at[three], yu_r.at[three], "gy", yu)
    ry_dn = remote(0, 6, yd_s.at[three], yd_r.at[three], "gy", yd)
    rz_up = remote(0, 6, yu_s.at[fourth], yu_r.at[fourth], "gy", yu)
    rz_dn = remote(0, 6, yd_s.at[fourth], yd_r.at[fourth], "gy", yd)
    fe_up = remote(0, 1, fe_s, fe_r, "gx", xu)
    fx_up = remote(0, 2, W.at[0, nx], W.at[0, 0], "gx", xu)
    cx_dn = remote(0, 3, c1.at[1], c1.at[nx + 1], "gx", xd)
    cx_up = remote(0, 3, c1.at[nx], c1.at[0], "gx", xu)
    m_dn = remote(0, 2, m_s, Ce, "gy", yd)
    y_up = remote(0, 2, up_s, up_r, "gy", yu)
    y_dn = remote(0, 2, dn_s, dn_r, "gy", yd)
    ex_dn = remote(0, 4, c2.at[0], c2.at[nx], "gx", xd)
    edge = remote(1, 5, sE, rE, "ta", t_next)
    landing = [rI.at[pl.ds(a, b - a), pl.ds(p, q - p)] for a, b, p, q in groups[:final]] + [rL]
    leaving = [sI.at[pl.ds(a, b - a), pl.ds(p, q - p)] for a, b, p, q in groups]
    pieces = [remote(1, 7 + max(k, 1), leaving[k], landing[k], "ta", t_next) for k in range(final + 1)]
    if detour:
        to_via = remote(1, 7, leaving[lane], rR, "ta", via)
        from_via = remote(1, 7 + lane, rR, landing[lane], "ta", taker)

    def pack_edges(x):
        for c in range(3):
            sE[c, x, 0:2] = V[c, x + 1, 0:2]
            sE[c, x, 2:4] = V[c, x + 1, ny - 2 : ny]

    def pack_rows(x):
        for c in range(3):
            yu_s[c, x] = V[c, x + 1, ny - 1 : ny]
            yd_s[c, x] = V[c, x + 1, 0:1]

    def pack_more(x):
        yu_s[3, x] = Nu[1, x + 1, ny - 1 : ny]
        yd_s[3, x] = Pr[x, 0:1]

    def pack_inner(x):
        for c in range(3):
            for p in range(parts):
                sI[x, p, c] = V[c, x + 1, 2 + 4 * p : 6 + 4 * p]

    wait_rows(load_sem.at[0], 3 * nx * ny)
    for c in range(3):
        fetch(vis.at[c], Nu.at[c, pl.ds(1, nx)], 1)
    fetch(prs, Pr.at[pl.ds(0, nx)], 1)
    for c in range(3):
        fetch(frc.at[c], F.at[c], 2)
    fetch(src, S, 2)
    loop(0, nx, pack_edges)
    pl.semaphore_wait(barrier, expected)

    @pl.when(has_next)
    def _():
        edge.start()

    for beside in (yu, yd):

        @pl.when(first_row | (beside == 0))
        def _():
            greet("gy", beside)

    loop(0, nx, pack_rows)
    for copy in (vx_up, vx_dn):
        copy.start()

    @pl.when(jnp.logical_not(first_row))
    def _():
        ry_up.start()
        ry_dn.start()

    wait_rows(load_sem.at[1], 4 * nx * ny)
    loop(0, nx, pack_more)
    for copy in (px_dn, nx_up):
        copy.start()

    @pl.when(jnp.logical_not(first_row))
    def _():
        rz_up.start()
        rz_dn.start()

    loop(0, nx, pack_inner)

    pauses = first_row & (ta == 0) & (lax.rem(gx, 2) == 1)
    outer_rows = 12 * nx + 48 * parts

    def send_inner():
        for k in range(2, final + 1):
            if detour and k == lane:

                @pl.when(ta == giver)
                def _():
                    to_via.start()

                @pl.when(ta != giver)
                def _():
                    pieces[k].start()

            else:
                pieces[k].start()

    @pl.when(has_next)
    def _():
        pieces[0].start()
        pieces[1].start()

    @pl.when(has_next & jnp.logical_not(pauses))
    def _():
        send_inner()

    @pl.when(first_row)
    def _():
        pl.semaphore_wait(barrier, 2)
        for copy in (ry_up, ry_dn, rz_up, rz_dn):
            copy.start()

    wait_rows(load_sem.at[2], 4 * nx * ny)
    wait_rows(recv_sem.at[0], 8 * ny)
    C[0, 0] = coeff_of(Nu[0, 0])

    def prepare(x):
        e = x + 1
        none = jnp.zeros((1, nz), jnp.float32)
        coeff = [coeff_of(Nu[c, e]) for c in range(3)]
        for c in range(3):
            C[c, e] = coeff[c]
            m_s[c, x] = coeff[c][0:1]
        total = coeff[0] + C[0, x] + coeff[1] + y_last(coeff[1], none) + coeff[2] + z_last(coeff[2])
        SC[x] = damping / total
        m_s[3, x] = total[0:1]
        press = Pr[x]
        grads = (Pr[x + 1] - press, y_next(press, none) - press, z_next(press) - press)
        for c in range(3):
            v = V[c, e]
            near = V[c, e - 1] + V[c, e + 1] + y_last(v, none) + y_next(v, none)
            near = near + z_last(v) + z_next(v)
            momentum = F[c, x] - (v + Nu[c, e] * (6.0 * v - near)) - grads[c]
            W[c, e] = v + coeff[c] * momentum

    def complete(x):
        e, t = x + 1, ny - 1
        below = coeff_of(yu_r[3, x])
        Ch[x] = below
        SC[x, 0:1] = damping / (m_s[3, x] + below)
        for c in range(3):
            W[c, e, 0:1] = W[c, e, 0:1] + C[c, e, 0:1] * (Nu[c, e, 0:1] * yu_r[c, x])
            more = Nu[c, e, t:ny] * yd_r[c, x]
            if c == 1:
                more = more - yd_r[3, x]
            W[c, e, t:ny] = W[c, e, t:ny] + C[c, e, t:ny] * more

    loop(0, nx, prepare)
    m_dn.start()
    wait_rows(recv_sem.at[6], 8 * nx)
    loop(0, nx, complete)
    if detour:

        @pl.when(ta == via)
        def _():
            to_via.wait_recv()
            from_via.start()

    def add_edges(x):
        for c in range(3):
            for s, t in ((0, 0), (2, ny - 2)):
                W[c, x + 1, t : t + 2] = (
                    W[c, x + 1, t : t + 2] + C[c, x + 1, t : t + 2] * rE[c, x, s : s + 2]
                )

    def add_inner(x, first_part, parts_end):
        for c in range(3):
            for p in range(first_part, parts_end):
                t = 2 + 4 * p
                W[c, x + 1, t : t + 4] = W[c, x + 1, t : t + 4] + C[c, x + 1, t : t + 4] * rI[x, p, c]

    @pl.when(has_prev)
    def _():
        edge.wait_recv()
        loop(0, nx, add_edges)

    def arrive(k):
        @pl.when(has_prev)
        def _():
            pieces[k].wait_recv()
            a, b, p, q = groups[k]
            loop(a, b, lambda x: add_inner(x, p, q))

    fe_s[...] = W[0, nx]
    fe_up.start()
    fe_up.wait_recv()

    def edge_rows(x, w0_last):
        e = x + 1
        zero = jnp.zeros((1, nz), jnp.float32)
        change = first_change(SC[x], S[x], W[0, e], w0_last, W[1, e], zero, W[2, e])
        up_s[0, x] = W[1, e, ny - 1 : ny]
        up_s[1, x] = change[ny - 1 : ny]
        dn_s[0, x] = change[0:1]
        dn_s[1, x] = change[1:2]

    edge_rows(0, fe_r[...])
    loop(1, nx, lambda x: edge_rows(x, W[0, x]))
    y_up.start()
    y_dn.start()

    @pl.when(has_next & pauses)
    def _():
        wait_rows(send_sem.at[1], outer_rows)
        send_inner()

    @pl.when(has_prev)
    def _():
        wait_rows(recv_sem.at[8], 48 * parts)
        for a in (0, nx - 2):
            loop(a, a + 2, lambda x: add_inner(x, 0, parts))

    fx_up.start()
    wait_rows(recv_sem.at[2], ny + 8 * nx)

    def first(x):
        e = x + 1
        c1[e, 0:ny] = first_change(SC[x], S[x], W[0, e], W[0, x], W[1, e], up_r[0, x], W[2, e])

    def first_above(x):
        e = x + 1
        scale = damping / (Ce[3, x] + C[1, e, ny - 1 : ny])
        Se[x] = scale
        c1[e, ny : ny + 1] = dn_r[0, x] + scale * W[1, e, ny - 1 : ny]

    for x in (0, nx - 1):
        first(x)
        first_above(x)
    c1[nx, ny + 1 : ny + 2] = Ce[0, nx - 1]
    for copy in (cx_dn, cx_up):
        copy.start()
    loop(1, nx - 1, first)
    loop(1, nx - 1, first_above)
    wait_rows(recv_sem.at[3], 2 * (ny + 8))

    def second(x):
        e = x + 1
        c2[x] = second_change(
            SC[x], c1[e, 0:ny], c1[e + 1, 0:ny], c1[e - 1, 0:ny], c1[e, ny : ny + 1], up_r[1, x],
            C[0, e], C[0, x], C[1, e], Ch[x], C[2, e],
        )

    def second_above(x, c0_last):
        e = x + 1
        wide = lambda row: jnp.broadcast_to(row, (8, nz))
        here = wide(c1[e, ny : ny + 1])
        g0 = wide(Ce[0, x]) * (wide(c1[e + 1, ny : ny + 1]) - here)
        g0_last = wide(c0_last) * (here - wide(c1[e - 1, ny : ny + 1]))
        g1 = wide(Ce[1, x]) * (wide(dn_r[1, x]) - here)
        g1_last = wide(C[1, e, ny - 1 : ny]) * (here - wide(c1[e, ny - 1 : ny]))
        g2 = wide(Ce[2, x]) * (z_next(here) - here)
        div = (g0 - g0_last) + (g1 - g1_last) + (g2 - z_last(g2))
        c2e[x] = (2.0 * here + wide(Se[x]) * div)[0:1]

    second(0)
    ex_dn.start()
    second_above(0, c1[0, ny + 1 : ny + 2])
    loop(1, nx, lambda x: second_above(x, Ce[0, x - 1]))

    def finish(x):
        e = x + 1
        here = c2[x]
        OP[x] = Pr[x] + here
        moved = final_velocity(
            [W[c, e] for c in range(3)], [C[c, e] for c in range(3)], here, c2[x + 1], c2e[x]
        )
        for c in range(3):
            OV[c, x] = moved[c]

    top = slice(8, ny)

    def second_top(x):
        e = x + 1
        c2[x, top] = second_change(
            SC[x, top], c1[e, top], c1[e + 1, top], c1[e - 1, top], c1[e, ny : ny + 1], c1[e, 7:8],
            C[0, e, top], C[0, x, top], C[1, e, top], C[1, e, 7:8], C[2, e, top],
        )

    def finish_top(x):
        e = x + 1
        here = c2[x, top]
        OP[x, top] = Pr[x, top] + here
        moved = final_velocity(
            [W[c, e, top] for c in range(3)], [C[c, e, top] for c in range(3)], here, c2[x + 1, top], c2e[x]
        )
        for c in range(3):
            OV[c, x, top] = moved[c]

    for k in range(2, final - 1):
        a, b, _, _ = groups[k]
        arrive(k)
        loop(a, b, first)
        loop(a - 1, b - 1, second)
        loop(a - 2, b - 2, finish)

    @pl.when(jnp.logical_not(has_prev))
    def _():
        rL[...] = jnp.zeros_like(rL)

    ex_dn.wait_recv()
    a = groups[final][0]
    arrive(final - 1)
    loop(a, nx - 1, first)
    loop(a - 1, nx, second_top)
    loop(a - 2, nx, finish_top)

    @pl.when(has_prev)
    def _():
        pieces[final].wait_recv()

    @pl.when(has_next & jnp.logical_not(pauses))
    def _():
        wait_rows(send_sem.at[1], 3 * nx * ny)

    @pl.when(has_next & pauses)
    def _():
        wait_rows(send_sem.at[1], 3 * nx * ny - outer_rows)

    if detour:

        @pl.when(ta == via)
        def _():
            wait_rows(send_sem.at[1], 24 * parts)

    wait_rows(send_sem.at[0], 13 * ny + 16 + 16 * nx)


def settle(
    last, moved, pressed, rL, W, C, c1, c2, c2e, SC, S, Pr, up_r, Ch, step_v, step_p, nV, nP, nW, n1, n2, sem
):
    out_v, out_p = step_v.at[:, 0], step_p.at[0]
    _, nx, ny, nz = moved.shape
    a, b = last
    ready, low = a - 2, slice(0, 8)
    done, rest = pl.ds(0, ready), pl.ds(ready, nx - ready)
    bottom, top = pl.ds(0, 8), pl.ds(8, ny - 8)

    for c in range(3):
        pltpu.make_async_copy(moved.at[c, done], out_v.at[c, done], sem.at[0]).start()
        pltpu.make_async_copy(moved.at[c, rest, top], out_v.at[c, rest, top], sem.at[0]).start()
    pltpu.make_async_copy(pressed.at[done], out_p.at[done], sem.at[1]).start()
    pltpu.make_async_copy(pressed.at[rest, top], out_p.at[rest, top], sem.at[1]).start()

    def w(c, x):
        return nW[c, x - a] if a <= x < b else W[c, x + 1, low]

    def change(x):
        return n1[x - a] if a <= x < nx - 1 else c1[x + 1, low]

    def second(x):
        return n2[x - (a - 1)] if a - 1 <= x < nx else c2[x, low]

    @pl.when(lax.axis_index("ta") >= 0)
    def _():
        for x in range(a, b):
            for c in range(3):
                nW[c, x - a] = W[c, x + 1, low]
                nW[c, x - a, 2:6] = W[c, x + 1, 2:6] + C[c, x + 1, 2:6] * rL[x - a, 0, c]
        for x in range(a, nx - 1):
            n1[x - a] = first_change(SC[x, low], S[x, low], w(0, x), w(0, x - 1), w(1, x), up_r[0, x], w(2, x))
        for x in range(a - 1, nx):
            e = x + 1
            n2[x - (a - 1)] = second_change(
                SC[x, low], change(x), change(x + 1), change(x - 1), c1[e, 8:9], up_r[1, x],
                C[0, e, low], C[0, x, low], C[1, e, low], Ch[x], C[2, e, low],
            )
        for x in range(ready, nx):
            here = second(x)
            nP[x - ready] = Pr[x, low] + here
            fresh = final_velocity(
                [w(c, x) for c in range(3)], [C[c, x + 1, low] for c in range(3)], here, second(x + 1), c2[x, 8:9]
            )
            for c in range(3):
                nV[c, x - ready] = fresh[c]
        for c in range(3):
            pltpu.make_async_copy(nV.at[c], out_v.at[c, rest, bottom], sem.at[0]).start()
        pltpu.make_async_copy(nP, out_p.at[rest, bottom], sem.at[1]).start()

    pltpu.make_async_copy(moved, out_v, sem.at[0]).wait()
    pltpu.make_async_copy(pressed, out_p, sem.at[1]).wait()


def body(counts, velocity, pressure, forcing, source, viscosity):
    _, steps, nx, ny, nz = velocity.shape
    assert steps == 1 and nx >= 12 and ny >= 16 and ny % 8 == 0
    parts = (ny - 4) // 4
    last = (nx - 4, nx - 2)
    whole = [(0, 2), (nx - 2, nx), (2, 4)] + groups_of(4, nx - 4, 4)
    groups = [(a, b, 0, parts) for a, b in whole] + [(*last, 1, parts), (*last, 0, 1)]
    detour = (1, 3, 2, 2) if counts[0] == 4 else None
    vmem = lambda *shape: pltpu.VMEM(shape, jnp.float32)
    rows = lambda *lead: vmem(*lead, nx, 1, nz)
    any_space = pl.BlockSpec(memory_space=pl.ANY)
    on_chip = pl.BlockSpec(memory_space=pltpu.VMEM)
    kept = (
        vmem(3, nx, ny, nz), vmem(nx, ny, nz), vmem(2, 1, 3, 4, nz),
        vmem(3, nx + 1, ny, nz), vmem(3, nx + 1, ny, nz), vmem(nx + 2, ny + 8, nz), vmem(nx + 1, ny, nz), rows(),
        vmem(nx, ny, nz), vmem(nx, ny, nz), vmem(nx + 1, ny, nz), rows(2), rows(),
    )
    inputs = (velocity[:, 0], pressure[0], forcing[:, 0], source[0], viscosity)
    held = pl.pallas_call(
        functools.partial(kernel, *counts, groups, detour),
        out_shape=kept,
        in_specs=[any_space] * 5,
        out_specs=(on_chip,) * len(kept),
        scratch_shapes=[
            vmem(3, nx + 2, ny, nz), vmem(3, nx, ny, nz), vmem(3, nx + 1, ny, nz),
            vmem(3, nx, 4, nz), vmem(3, nx, 4, nz),
            vmem(nx, parts, 3, 4, nz), vmem(nx, parts, 3, 4, nz), vmem(2, parts, 3, 4, nz),
            rows(4), rows(4), rows(4), rows(4), rows(4), rows(4),
            vmem(ny, nz), vmem(ny, nz), rows(2), rows(2), rows(2), rows(), vmem(4 * nx * ny, nz),
            pltpu.SemaphoreType.DMA((3,)),
            pltpu.SemaphoreType.DMA((2,)),
            pltpu.SemaphoreType.DMA((7 + len(groups),)),
        ],
        compiler_params=pltpu.CompilerParams(
            collective_id=0, has_side_effects=True, vmem_limit_bytes=40 << 20
        ),
        name="smoother",
    )(*(pltpu.with_memory_space_constraint(a, pltpu.HBM) for a in inputs))
    return pl.pallas_call(
        functools.partial(settle, last),
        out_shape=(
            jax.ShapeDtypeStruct((3, 1, nx, ny, nz), jnp.float32),
            jax.ShapeDtypeStruct((1, nx, ny, nz), jnp.float32),
        ),
        in_specs=[on_chip] * len(kept),
        out_specs=(any_space, any_space),
        scratch_shapes=[
            vmem(3, 6, 8, nz), vmem(6, 8, nz), vmem(3, 2, 8, nz), vmem(3, 8, nz), vmem(5, 8, nz),
            pltpu.SemaphoreType.DMA((2,)),
        ],
        compiler_params=pltpu.CompilerParams(vmem_limit_bytes=2 << 20),
        name="settle",
    )(*held)


def solution(mesh):
    placed = (
        P(None, "ta", "gx", "gy", None),
        P("ta", "gx", "gy", None),
        P(None, "ta", "gx", "gy", None),
        P("ta", "gx", "gy", None),
        P(None, "gx", "gy", None),
    )
    counts = tuple(mesh.shape[axis] for axis in ("ta", "gx", "gy"))
    return jax.shard_map(
        functools.partial(body, counts),
        mesh=mesh,
        in_specs=placed,
        out_specs=(P(None, "ta", "gx", "gy", None), P("ta", "gx", "gy", None)),
        check_vma=False,
    )
```

```python
import functools

import jax
import jax.numpy as jnp
from jax import lax
from jax.experimental import pallas as pl
from jax.experimental.pallas import tpu as pltpu
from jax.sharding import PartitionSpec as P

relax_factor = 1.5
damping = 0.8
MESH = pl.DeviceIdType.MESH


def loop(lo, hi, body):
    def step(i, carry):
        body(i)
        return carry

    if hi > lo:
        lax.fori_loop(lo, hi, step, 0, unroll=hi - lo)


def row_index(f):
    return lax.broadcasted_iota(jnp.int32, f.shape, 0)


def y_next(f, row):
    n = f.shape[0]
    return jnp.where(row_index(f) == n - 1, row, pltpu.roll(f, n - 1, 0))


def y_last(f, row):
    return jnp.where(row_index(f) == 0, row, pltpu.roll(f, 1, 0))


def z_next(f):
    return pltpu.roll(f, f.shape[1] - 1, 1)


def z_last(f):
    return pltpu.roll(f, 1, 1)


def coeff_of(nu):
    return 1.0 / (relax_factor * (1.0 + 6.0 * nu))


def groups_of(lo, hi, size):
    return [(a, min(a + size, hi)) for a in range(lo, hi, size)]


def first_change(scale, source, w0, w0_last, w1, row, w2):
    div = (w0 - w0_last) + (w1 - y_last(w1, row)) + (w2 - z_last(w2))
    return scale * (source - div)


def second_change(scale, here, x_above, x_below, above, row, c0, c0_last, c1, c1_row, c2):
    g0, g0_last = c0 * (x_above - here), c0_last * (here - x_below)
    g1 = c1 * (y_next(here, above) - here)
    g2 = c2 * (z_next(here) - here)
    div = (g0 - g0_last) + (g1 - y_last(g1, c1_row * (here[0:1] - row))) + (g2 - z_last(g2))
    return 2.0 * here + scale * div


def final_velocity(w, c, here, x_above, above):
    return (
        w[0] - c[0] * (x_above - here),
        w[1] - c[1] * (y_next(here, above) - here),
        w[2] - c[2] * (z_next(here) - here),
    )


def kernel(
    slabs, nx_parts, ny_parts, groups, detour,
    vel, prs, frc, src, vis,
    OV, OP, rL, W, C, c1, c2, c2e, SC, S, Pr, up_r, Ch,
    V, F, Nu, sE, rE, sI, rI, rR, yu_s, yd_s, yu_r, yd_r, Ce, m_s, fe_s, fe_r, up_s, dn_s, dn_r, Se, tally,
    load_sem, send_sem, recv_sem,
):
    _, nx, ny, nz = vel.shape
    parts = (ny - 4) // 4
    final = len(groups) - 1
    ta, gx, gy = lax.axis_index("ta"), lax.axis_index("gx"), lax.axis_index("gy")
    t_next = jnp.minimum(ta + 1, slabs - 1)
    has_next, has_prev = ta < slabs - 1, ta > 0
    xu, xd = lax.rem(gx + 1, nx_parts), lax.rem(gx + nx_parts - 1, nx_parts)
    yu, yd = lax.rem(gy + 1, ny_parts), lax.rem(gy + ny_parts - 1, ny_parts)
    first_row = gy == 0

    barrier = pltpu.get_barrier_semaphore()

    def greet(axis, index):
        pl.semaphore_signal(barrier, inc=1, device_id={axis: index}, device_id_type=MESH)

    @pl.when(has_prev)
    def _():
        greet("ta", ta - 1)

    expected = 2 + has_next.astype(jnp.int32) + jnp.where(first_row, 0, 2)
    if detour:
        giver, via, taker, lane = detour

        @pl.when(ta == via)
        def _():
            greet("ta", giver)

        @pl.when(ta == taker)
        def _():
            greet("ta", via)

        expected = expected + ((ta == giver) | (ta == via)).astype(jnp.int32)

    def fetch(source, target, k):
        pltpu.make_async_copy(source, target, load_sem.at[k]).start()

    def wait_rows(sem, count):
        size = pl.ds(0, count)
        pltpu.make_async_copy(tally.at[size], tally.at[size], sem).wait()

    half = nx // 2
    for a, n in ((0, half), (half, nx - half)):
        for c in range(3):
            fetch(vel.at[c, pl.ds(a, n)], V.at[c, pl.ds(1 + a, n)], 0)
    greet("gx", xu)
    greet("gx", xd)
    for beside in (yu, yd):

        @pl.when(jnp.logical_not(first_row) & (beside != 0))
        def _():
            greet("gy", beside)

    def remote(send, recv, source, target, axis, index):
        return pltpu.make_async_remote_copy(
            src_ref=source, dst_ref=target, send_sem=send_sem.at[send], recv_sem=recv_sem.at[recv],
            device_id={axis: index}, device_id_type=MESH,
        )

    vx_up = remote(0, 0, V.at[:, nx], V.at[:, 0], "gx", xu)
    vx_dn = remote(0, 0, V.at[:, 1], V.at[:, nx + 1], "gx", xd)
    px_dn = remote(0, 0, Pr.at[0], Pr.at[nx], "gx", xd)
    nx_up = remote(0, 0, Nu.at[0, nx], Nu.at[0, 0], "gx", xu)
    three, fourth = pl.ds(0, 3), pl.ds(3, 1)
    ry_up = remote(0, 6, yu_s.at[three], yu_r.at[three], "gy", yu)
    ry_dn = remote(0, 6, yd_s.at[three], yd_r.at[three], "gy", yd)
    rz_up = remote(0, 6, yu_s.at[fourth], yu_r.at[fourth], "gy", yu)
    rz_dn = remote(0, 6, yd_s.at[fourth], yd_r.at[fourth], "gy", yd)
    fe_up = remote(0, 1, fe_s, fe_r, "gx", xu)
    fx_up = remote(0, 2, W.at[0, nx], W.at[0, 0], "gx", xu)
    cx_dn = remote(0, 3, c1.at[1], c1.at[nx + 1], "gx", xd)
    cx_up = remote(0, 3, c1.at[nx], c1.at[0], "gx", xu)
    m_dn = remote(0, 2, m_s, Ce, "gy", yd)
    y_up = remote(0, 2, up_s, up_r, "gy", yu)
    y_dn = remote(0, 2, dn_s, dn_r, "gy", yd)
    ex_dn = remote(0, 4, c2.at[0], c2.at[nx], "gx", xd)
    edge = remote(1, 5, sE, rE, "ta", t_next)
    landing = [rI.at[pl.ds(a, b - a), pl.ds(p, q - p)] for a, b, p, q in groups[:final]] + [rL]
    leaving = [sI.at[pl.ds(a, b - a), pl.ds(p, q - p)] for a, b, p, q in groups]
    pieces = [remote(1, 7 + max(k, 1), leaving[k], landing[k], "ta", t_next) for k in range(final + 1)]
    if detour:
        to_via = remote(1, 7, leaving[lane], rR, "ta", via)
        from_via = remote(1, 7 + lane, rR, landing[lane], "ta", taker)

    def pack_edges(x):
        for c in range(3):
            sE[c, x, 0:2] = V[c, x + 1, 0:2]
            sE[c, x, 2:4] = V[c, x + 1, ny - 2 : ny]

    def pack_rows(x):
        for c in range(3):
            yu_s[c, x] = V[c, x + 1, ny - 1 : ny]
            yd_s[c, x] = V[c, x + 1, 0:1]

    def pack_more(x):
        yu_s[3, x] = Nu[1, x + 1, ny - 1 : ny]
        yd_s[3, x] = Pr[x, 0:1]

    def pack_inner(x):
        for c in range(3):
            for p in range(parts):
                sI[x, p, c] = V[c, x + 1, 2 + 4 * p : 6 + 4 * p]

    wait_rows(load_sem.at[0], 3 * nx * ny)
    for c in range(3):
        fetch(vis.at[c], Nu.at[c, pl.ds(1, nx)], 1)
    fetch(prs, Pr.at[pl.ds(0, nx)], 1)
    for c in range(3):
        fetch(frc.at[c], F.at[c], 2)
    fetch(src, S, 2)
    loop(0, nx, pack_edges)
    pl.semaphore_wait(barrier, expected)

    @pl.when(has_next)
    def _():
        edge.start()

    for beside in (yu, yd):

        @pl.when(first_row | (beside == 0))
        def _():
            greet("gy", beside)

    loop(0, nx, pack_rows)
    for copy in (vx_up, vx_dn):
        copy.start()

    @pl.when(jnp.logical_not(first_row))
    def _():
        ry_up.start()
        ry_dn.start()

    wait_rows(load_sem.at[1], 4 * nx * ny)
    loop(0, nx, pack_more)
    for copy in (px_dn, nx_up):
        copy.start()

    @pl.when(jnp.logical_not(first_row))
    def _():
        rz_up.start()
        rz_dn.start()

    loop(0, nx, pack_inner)

    pauses = first_row & (ta == 0) & (lax.rem(gx, 2) == 1)
    outer_rows = 12 * nx + 48 * parts

    def send_inner():
        for k in range(2, final + 1):
            if detour and k == lane:

                @pl.when(ta == giver)
                def _():
                    to_via.start()

                @pl.when(ta != giver)
                def _():
                    pieces[k].start()

            else:
                pieces[k].start()

    @pl.when(has_next)
    def _():
        pieces[0].start()
        pieces[1].start()

    @pl.when(has_next & jnp.logical_not(pauses))
    def _():
        send_inner()

    @pl.when(first_row)
    def _():
        pl.semaphore_wait(barrier, 2)
        for copy in (ry_up, ry_dn, rz_up, rz_dn):
            copy.start()

    wait_rows(load_sem.at[2], 4 * nx * ny)
    wait_rows(recv_sem.at[0], 8 * ny)
    C[0, 0] = coeff_of(Nu[0, 0])

    def prepare(x):
        e = x + 1
        none = jnp.zeros((1, nz), jnp.float32)
        coeff = [coeff_of(Nu[c, e]) for c in range(3)]
        for c in range(3):
            C[c, e] = coeff[c]
            m_s[c, x] = coeff[c][0:1]
        total = coeff[0] + C[0, x] + coeff[1] + y_last(coeff[1], none) + coeff[2] + z_last(coeff[2])
        SC[x] = damping / total
        m_s[3, x] = total[0:1]
        press = Pr[x]
        grads = (Pr[x + 1] - press, y_next(press, none) - press, z_next(press) - press)
        for c in range(3):
            v = V[c, e]
            near = V[c, e - 1] + V[c, e + 1] + y_last(v, none) + y_next(v, none)
            near = near + z_last(v) + z_next(v)
            momentum = F[c, x] - (v + Nu[c, e] * (6.0 * v - near)) - grads[c]
            W[c, e] = v + coeff[c] * momentum

    def complete(x):
        e, t = x + 1, ny - 1
        below = coeff_of(yu_r[3, x])
        Ch[x] = below
        SC[x, 0:1] = damping / (m_s[3, x] + below)
        for c in range(3):
            W[c, e, 0:1] = W[c, e, 0:1] + C[c, e, 0:1] * (Nu[c, e, 0:1] * yu_r[c, x])
            more = Nu[c, e, t:ny] * yd_r[c, x]
            if c == 1:
                more = more - yd_r[3, x]
            W[c, e, t:ny] = W[c, e, t:ny] + C[c, e, t:ny] * more

    loop(0, nx, prepare)
    m_dn.start()
    wait_rows(recv_sem.at[6], 8 * nx)
    loop(0, nx, complete)
    if detour:

        @pl.when(ta == via)
        def _():
            to_via.wait_recv()
            from_via.start()

    def add_edges(x):
        for c in range(3):
            for s, t in ((0, 0), (2, ny - 2)):
                W[c, x + 1, t : t + 2] = (
                    W[c, x + 1, t : t + 2] + C[c, x + 1, t : t + 2] * rE[c, x, s : s + 2]
                )

    def add_inner(x, first_part, parts_end):
        for c in range(3):
            for p in range(first_part, parts_end):
                t = 2 + 4 * p
                W[c, x + 1, t : t + 4] = W[c, x + 1, t : t + 4] + C[c, x + 1, t : t + 4] * rI[x, p, c]

    @pl.when(has_prev)
    def _():
        edge.wait_recv()
        loop(0, nx, add_edges)

    def arrive(k):
        @pl.when(has_prev)
        def _():
            pieces[k].wait_recv()
            a, b, p, q = groups[k]
            loop(a, b, lambda x: add_inner(x, p, q))

    fe_s[...] = W[0, nx]
    fe_up.start()
    fe_up.wait_recv()

    def edge_rows(x, w0_last):
        e = x + 1
        zero = jnp.zeros((1, nz), jnp.float32)
        change = first_change(SC[x], S[x], W[0, e], w0_last, W[1, e], zero, W[2, e])
        up_s[0, x] = W[1, e, ny - 1 : ny]
        up_s[1, x] = change[ny - 1 : ny]
        dn_s[0, x] = change[0:1]
        dn_s[1, x] = change[1:2]

    edge_rows(0, fe_r[...])
    loop(1, nx, lambda x: edge_rows(x, W[0, x]))
    y_up.start()
    y_dn.start()

    @pl.when(has_next & pauses)
    def _():
        wait_rows(send_sem.at[1], outer_rows)
        send_inner()

    @pl.when(has_prev)
    def _():
        wait_rows(recv_sem.at[8], 48 * parts)
        for a in (0, nx - 2):
            loop(a, a + 2, lambda x: add_inner(x, 0, parts))

    fx_up.start()
    wait_rows(recv_sem.at[2], ny + 8 * nx)

    def first(x):
        e = x + 1
        c1[e, 0:ny] = first_change(SC[x], S[x], W[0, e], W[0, x], W[1, e], up_r[0, x], W[2, e])

    def first_above(x):
        e = x + 1
        scale = damping / (Ce[3, x] + C[1, e, ny - 1 : ny])
        Se[x] = scale
        c1[e, ny : ny + 1] = dn_r[0, x] + scale * W[1, e, ny - 1 : ny]

    for x in (0, nx - 1):
        first(x)
        first_above(x)
    c1[nx, ny + 1 : ny + 2] = Ce[0, nx - 1]
    for copy in (cx_dn, cx_up):
        copy.start()
    loop(1, nx - 1, first)
    loop(1, nx - 1, first_above)
    wait_rows(recv_sem.at[3], 2 * (ny + 8))

    def second(x):
        e = x + 1
        c2[x] = second_change(
            SC[x], c1[e, 0:ny], c1[e + 1, 0:ny], c1[e - 1, 0:ny], c1[e, ny : ny + 1], up_r[1, x],
            C[0, e], C[0, x], C[1, e], Ch[x], C[2, e],
        )

    def second_above(x, c0_last):
        e = x + 1
        wide = lambda row: jnp.broadcast_to(row, (8, nz))
        here = wide(c1[e, ny : ny + 1])
        g0 = wide(Ce[0, x]) * (wide(c1[e + 1, ny : ny + 1]) - here)
        g0_last = wide(c0_last) * (here - wide(c1[e - 1, ny : ny + 1]))
        g1 = wide(Ce[1, x]) * (wide(dn_r[1, x]) - here)
        g1_last = wide(C[1, e, ny - 1 : ny]) * (here - wide(c1[e, ny - 1 : ny]))
        g2 = wide(Ce[2, x]) * (z_next(here) - here)
        div = (g0 - g0_last) + (g1 - g1_last) + (g2 - z_last(g2))
        c2e[x] = (2.0 * here + wide(Se[x]) * div)[0:1]

    second(0)
    ex_dn.start()
    second_above(0, c1[0, ny + 1 : ny + 2])
    loop(1, nx, lambda x: second_above(x, Ce[0, x - 1]))

    def finish(x):
        e = x + 1
        here = c2[x]
        OP[x] = Pr[x] + here
        moved = final_velocity(
            [W[c, e] for c in range(3)], [C[c, e] for c in range(3)], here, c2[x + 1], c2e[x]
        )
        for c in range(3):
            OV[c, x] = moved[c]

    top = slice(8, ny)

    def second_top(x):
        e = x + 1
        c2[x, top] = second_change(
            SC[x, top], c1[e, top], c1[e + 1, top], c1[e - 1, top], c1[e, ny : ny + 1], c1[e, 7:8],
            C[0, e, top], C[0, x, top], C[1, e, top], C[1, e, 7:8], C[2, e, top],
        )

    def finish_top(x):
        e = x + 1
        here = c2[x, top]
        OP[x, top] = Pr[x, top] + here
        moved = final_velocity(
            [W[c, e, top] for c in range(3)], [C[c, e, top] for c in range(3)], here, c2[x + 1, top], c2e[x]
        )
        for c in range(3):
            OV[c, x, top] = moved[c]

    for k in range(2, final - 1):
        a, b, _, _ = groups[k]
        arrive(k)
        loop(a, b, first)
        loop(a - 1, b - 1, second)
        loop(a - 2, b - 2, finish)

    @pl.when(jnp.logical_not(has_prev))
    def _():
        rL[...] = jnp.zeros_like(rL)

    ex_dn.wait_recv()
    a = groups[final][0]
    arrive(final - 1)
    loop(a, nx - 1, first)
    loop(a - 1, nx, second_top)
    loop(a - 2, nx, finish_top)

    @pl.when(has_prev)
    def _():
        pieces[final].wait_recv()

    @pl.when(has_next & jnp.logical_not(pauses))
    def _():
        wait_rows(send_sem.at[1], 3 * nx * ny)

    @pl.when(has_next & pauses)
    def _():
        wait_rows(send_sem.at[1], 3 * nx * ny - outer_rows)

    if detour:

        @pl.when(ta == via)
        def _():
            wait_rows(send_sem.at[1], 24 * parts)

    wait_rows(send_sem.at[0], 13 * ny + 16 + 16 * nx)


def settle(
    last, moved, pressed, rL, W, C, c1, c2, c2e, SC, S, Pr, up_r, Ch, step_v, step_p, nV, nP, nW, n1, n2, sem
):
    out_v, out_p = step_v.at[:, 0], step_p.at[0]
    _, nx, ny, nz = moved.shape
    a, b = last
    ready, low = a - 2, slice(0, 8)
    done, rest = pl.ds(0, ready), pl.ds(ready, nx - ready)
    bottom, top = pl.ds(0, 8), pl.ds(8, ny - 8)

    for c in range(3):
        pltpu.make_async_copy(moved.at[c, done], out_v.at[c, done], sem.at[0]).start()
        pltpu.make_async_copy(moved.at[c, rest, top], out_v.at[c, rest, top], sem.at[0]).start()
    pltpu.make_async_copy(pressed.at[done], out_p.at[done], sem.at[1]).start()
    pltpu.make_async_copy(pressed.at[rest, top], out_p.at[rest, top], sem.at[1]).start()

    def w(c, x):
        return nW[c, x - a] if a <= x < b else W[c, x + 1, low]

    def change(x):
        return n1[x - a] if a <= x < nx - 1 else c1[x + 1, low]

    def second(x):
        return n2[x - (a - 1)] if a - 1 <= x < nx else c2[x, low]

    @pl.when(lax.axis_index("ta") >= 0)
    def _():
        for x in range(a, b):
            for c in range(3):
                nW[c, x - a] = W[c, x + 1, low]
                nW[c, x - a, 2:6] = W[c, x + 1, 2:6] + C[c, x + 1, 2:6] * rL[x - a, 0, c]
        for x in range(a, nx - 1):
            n1[x - a] = first_change(SC[x, low], S[x, low], w(0, x), w(0, x - 1), w(1, x), up_r[0, x], w(2, x))
        for x in range(a - 1, nx):
            e = x + 1
            n2[x - (a - 1)] = second_change(
                SC[x, low], change(x), change(x + 1), change(x - 1), c1[e, 8:9], up_r[1, x],
                C[0, e, low], C[0, x, low], C[1, e, low], Ch[x], C[2, e, low],
            )
        for x in range(ready, nx):
            here = second(x)
            nP[x - ready] = Pr[x, low] + here
            fresh = final_velocity(
                [w(c, x) for c in range(3)], [C[c, x + 1, low] for c in range(3)], here, second(x + 1), c2[x, 8:9]
            )
            for c in range(3):
                nV[c, x - ready] = fresh[c]
        for c in range(3):
            pltpu.make_async_copy(nV.at[c], out_v.at[c, rest, bottom], sem.at[0]).start(priority=1)
        pltpu.make_async_copy(nP, out_p.at[rest, bottom], sem.at[1]).start(priority=1)

    pltpu.make_async_copy(moved, out_v, sem.at[0]).wait()
    pltpu.make_async_copy(pressed, out_p, sem.at[1]).wait()


def body(counts, velocity, pressure, forcing, source, viscosity):
    _, steps, nx, ny, nz = velocity.shape
    assert steps == 1 and nx >= 12 and ny >= 16 and ny % 8 == 0
    parts = (ny - 4) // 4
    last = (nx - 4, nx - 2)
    whole = [(0, 2), (nx - 2, nx), (2, 4)] + groups_of(4, nx - 4, 4)
    groups = [(a, b, 0, parts) for a, b in whole] + [(*last, 1, parts), (*last, 0, 1)]
    detour = (1, 3, 2, 2) if counts[0] == 4 else None
    vmem = lambda *shape: pltpu.VMEM(shape, jnp.float32)
    rows = lambda *lead: vmem(*lead, nx, 1, nz)
    any_space = pl.BlockSpec(memory_space=pl.ANY)
    on_chip = pl.BlockSpec(memory_space=pltpu.VMEM)
    kept = (
        vmem(3, nx, ny, nz), vmem(nx, ny, nz), vmem(2, 1, 3, 4, nz),
        vmem(3, nx + 1, ny, nz), vmem(3, nx + 1, ny, nz), vmem(nx + 2, ny + 8, nz), vmem(nx + 1, ny, nz), rows(),
        vmem(nx, ny, nz), vmem(nx, ny, nz), vmem(nx + 1, ny, nz), rows(2), rows(),
    )
    inputs = (velocity[:, 0], pressure[0], forcing[:, 0], source[0], viscosity)
    held = pl.pallas_call(
        functools.partial(kernel, *counts, groups, detour),
        out_shape=kept,
        in_specs=[any_space] * 5,
        out_specs=(on_chip,) * len(kept),
        scratch_shapes=[
            vmem(3, nx + 2, ny, nz), vmem(3, nx, ny, nz), vmem(3, nx + 1, ny, nz),
            vmem(3, nx, 4, nz), vmem(3, nx, 4, nz),
            vmem(nx, parts, 3, 4, nz), vmem(nx, parts, 3, 4, nz), vmem(2, parts, 3, 4, nz),
            rows(4), rows(4), rows(4), rows(4), rows(4), rows(4),
            vmem(ny, nz), vmem(ny, nz), rows(2), rows(2), rows(2), rows(), vmem(4 * nx * ny, nz),
            pltpu.SemaphoreType.DMA((3,)),
            pltpu.SemaphoreType.DMA((2,)),
            pltpu.SemaphoreType.DMA((7 + len(groups),)),
        ],
        compiler_params=pltpu.CompilerParams(
            collective_id=0, has_side_effects=True, vmem_limit_bytes=40 << 20
        ),
        name="smoother",
    )(*(pltpu.with_memory_space_constraint(a, pltpu.HBM) for a in inputs))
    return pl.pallas_call(
        functools.partial(settle, last),
        out_shape=(
            jax.ShapeDtypeStruct((3, 1, nx, ny, nz), jnp.float32),
            jax.ShapeDtypeStruct((1, nx, ny, nz), jnp.float32),
        ),
        in_specs=[on_chip] * len(kept),
        out_specs=(any_space, any_space),
        scratch_shapes=[
            vmem(3, 6, 8, nz), vmem(6, 8, nz), vmem(3, 2, 8, nz), vmem(3, 8, nz), vmem(5, 8, nz),
            pltpu.SemaphoreType.DMA((2,)),
        ],
        compiler_params=pltpu.CompilerParams(vmem_limit_bytes=2 << 20),
        name="settle",
    )(*held)


def solution(mesh):
    placed = (
        P(None, "ta", "gx", "gy", None),
        P("ta", "gx", "gy", None),
        P(None, "ta", "gx", "gy", None),
        P("ta", "gx", "gy", None),
        P(None, "gx", "gy", None),
    )
    counts = tuple(mesh.shape[axis] for axis in ("ta", "gx", "gy"))
    return jax.shard_map(
        functools.partial(body, counts),
        mesh=mesh,
        in_specs=placed,
        out_specs=(P(None, "ta", "gx", "gy", None), P("ta", "gx", "gy", None)),
        check_vma=False,
    )
```
